32 devices in a mesh: dom: 16 (over z, y, x), sub: 2 (over core).
Axes of the slice: x: 2, y: 2, z: 4, core: 2. Of those that a mesh axis runs over, the one named last changes fastest.
Arguments:
- positions: float32 [3, 262144], P(None, ('dom', 'sub')), may hold values from -6 to 6
- masses: float32 [262144], P(('dom', 'sub')), may hold values from 0.0005 to 0.005
- old_accel: float32 [3, 262144], P(None, ('dom', 'sub')), may hold values from -6 to 6
- active: int32 [1024], P('dom'), may hold values from 0 to 1, as said below
- parent_of: int32 [1024], P(('dom', 'sub')), may hold values from 0 to 255
- parent_centers: float32 [3, 256], replicated, may hold values from -4 to 4
- local_list: int32 [1024, 8], P('dom'), may hold values from 0 to 63
- near_list: int32 [1024, 8], P('dom'), may hold values from 0 to 127, as said below
- far_list: int32 [1024, 16], P('dom'), may hold values from 0 to 255, as said below
- send_ids: int32 [32, 16, 4], P(('dom', 'sub')), may hold values from -1 to 31, as said below
- cell_send_ids: int32 [32, 16, 8], P(('dom', 'sub')), may hold values from -1 to 31, as said below
Outputs:
- accel: float32 [3, 262144], P(None, ('dom', 'sub'))
- parent_moments: float32 [35, 256], P(None, 'dom')
The draws below stay inside these ranges and needn't reach their ends.
Inputs may be any that keep to these rules, and one draw needn't show every extreme that they name: On each device between 1 and 16 of its 32 groups are active, and on some device exactly 16. For device g and chip c, slots 0 to n - 1 of send_ids[g, c] name groups of device g and the others hold -1, with 1 <= n <= 4; n = 4 and n = 1 occur in every draw. For device g and chip c, slots 0 to n - 1 of cell_send_ids[g, c] name groups of device g and the others hold -1, with 1 <= n <= 8; n = 8 and n = 1 occur in every draw. `near_list`: an entry g * 4 + k names slot k of send_ids[g, c], c the chip of the row's group; that slot is never -1. `far_list`: an entry g * 8 + k names slot k of cell_send_ids[g, c], c the chip of the row's group; that slot is never -1.
All inputs are finite; a program needn't handle non-finite values.
Results may differ from the reference program's by a relative error of at most 0.0003.
Values sent between devices are 32-bit elements; how exact they have to be, the bound alone decides.
A program may use at most 64 MiB of HBM per device.

```python
import math
import jax
import jax.numpy as jnp
import numpy as np
from jax import lax

BUCKET = 256
NB = 32
LOCAL_N = 8
NEAR = 8
FAR = 16
RQ = 4
RQC = 8
ACT_MAX = 16
CHIPS = 16
CORES = 32
BUCKETS = 1024
PARTICLES = 262144
NPAR = 256


def slot_counts(key, capacity, salt):
    count_key, spot_key = jax.random.split(jax.random.fold_in(key, salt))
    counts = jax.random.randint(count_key, (CORES, CHIPS), 1, capacity + 1)
    places = jnp.arange(CORES * CHIPS, dtype=jnp.int32).reshape(CORES, CHIPS)
    full_spot = jax.random.randint(spot_key, (), 0, CORES * CHIPS)
    thin_spot = (full_spot + CHIPS) % (CORES * CHIPS)
    counts = jnp.where(places == thin_spot, 1, counts)
    return jnp.where(places == full_spot, capacity, counts)


def send_table(key, capacity, count_salt, pick_salt):
    counts = slot_counts(key, capacity, count_salt)
    chosen = jax.random.randint(jax.random.fold_in(key, pick_salt), (CORES, CHIPS, capacity), 0, NB)
    slot_places = jnp.arange(capacity, dtype=jnp.int32)
    return jnp.where(slot_places[None, None, :] < counts[:, :, None], chosen, -1).astype(jnp.int32)


def list_table(key, capacity, count_salt, list_salt, width):
    counts = slot_counts(key, capacity, count_salt)
    source_key, slot_key = jax.random.split(jax.random.fold_in(key, list_salt))
    senders = jax.random.randint(source_key, (BUCKETS, width), 0, CORES)
    raw_slots = jax.random.randint(slot_key, (BUCKETS, width), 0, 1 << 20)
    chips = jnp.arange(BUCKETS, dtype=jnp.int32) // (BUCKETS // CHIPS)
    limits = counts[senders, chips[:, None]]
    return (senders * capacity + raw_slots % limits).astype(jnp.int32)


def draw_send_ids(key, part):
    return send_table(key, RQ, 11, 12)


def draw_near_list(key, part):
    return list_table(key, RQ, 11, 13, NEAR)


def draw_cell_send_ids(key, part):
    return send_table(key, RQC, 21, 22)


def draw_far_list(key, part):
    return list_table(key, RQC, 21, 23, FAR)


def draw_active(key, part):
    active_key = jax.random.fold_in(key, 31)
    count_key, spot_key, order_key = jax.random.split(active_key, 3)
    drawn = jax.random.randint(count_key, (CORES,), 0, ACT_MAX)
    counts = 1 + drawn * drawn // ACT_MAX
    busiest = jax.random.randint(spot_key, (), 0, CORES)
    counts = jnp.where(jnp.arange(CORES, dtype=jnp.int32) == busiest, ACT_MAX, counts)
    orders = jax.vmap(lambda order_seed: jax.random.permutation(order_seed, NB))(jax.random.split(order_key, CORES))
    return (orders < counts[:, None]).astype(jnp.int32).reshape(BUCKETS)


def draw_positions(key, part):
    center_key, offset_key = jax.random.split(jax.random.fold_in(key, 41))
    centers = jnp.clip(0.7 * jax.random.normal(center_key, (3, BUCKETS), jnp.float32), -4.0, 4.0)
    offsets = jnp.clip(0.5 * jax.random.normal(offset_key, (3, BUCKETS, BUCKET), jnp.float32), -2.0, 2.0)
    return (centers[:, :, None] + offsets).reshape(3, PARTICLES)


def plant(result, key, low, high):
    longest = result.shape.index(max(result.shape))
    spots = []
    for shift in (0, 1):
        where = [jax.random.randint(jax.random.fold_in(key, axis), (), 0, length) for axis, length in enumerate(result.shape)]
        where[longest] = (where[longest] + shift) % result.shape[longest]
        spots.append(tuple(where))
    return result.at[spots[0]].set(low).at[spots[1]].set(high)


def steps_of(key, shape, shards, least, high):
    factor_of, own = 1.0, jax.random.fold_in(key, 6)
    for dim, blocks in shards:
        steps = jnp.exp(jax.random.uniform(jax.random.fold_in(own, dim), (blocks,), jnp.float32, least / len(shards), high / len(shards)))
        factor_of = factor_of * jnp.repeat(steps, shape[dim] // blocks).reshape([-1 if axis == dim else 1 for axis in range(len(shape))])
    return factor_of


def noise(own_key, extent, spread, limit, cuts=(), kind=jnp.bfloat16):
    array = jax.random.normal(own_key, extent, jnp.float32) * spread
    if len(cuts) > 0:
        array = steps_of(own_key, extent, cuts, -0.22, 0.18) * array
    return jnp.clip(array, min=-limit, max=limit).astype(kind)


def setup_inputs(seed: int = 0) -> dict:
    arg_keys = jax.random.split(jax.random.key(seed), 12)
    return {
        "positions": draw_positions(jax.random.fold_in(arg_keys[11], 71), 0),
        "masses": jnp.clip(jnp.exp(math.log(0.005) - 2.30258502 * jax.random.uniform(arg_keys[1], (PARTICLES,), jnp.float32) ** steps_of(arg_keys[1], (PARTICLES,), ((0, 32),), -0.2, 0.2)), 0.0005, 0.005),
        "old_accel": noise(arg_keys[2], (3, PARTICLES), 1.0, 6.0, ((1, 32),), jnp.float32),
        "active": draw_active(jax.random.fold_in(arg_keys[11], 71), 0),
        "parent_of": plant(jax.random.randint(arg_keys[4], (BUCKETS,), 0, NPAR), jax.random.fold_in(arg_keys[4], 1), 0, NPAR - 1).astype(jnp.int32),
        "parent_centers": noise(arg_keys[5], (3, NPAR), 0.7, 4.0, (), jnp.float32),
        "local_list": plant(jax.random.randint(arg_keys[6], (BUCKETS, LOCAL_N), 0, 2 * NB), jax.random.fold_in(arg_keys[6], 1), 0, (2 * NB) - 1).astype(jnp.int32),
        "near_list": draw_near_list(jax.random.fold_in(arg_keys[11], 71), 0),
        "far_list": draw_far_list(jax.random.fold_in(arg_keys[11], 71), 0),
        "send_ids": draw_send_ids(jax.random.fold_in(arg_keys[11], 71), 0),
        "cell_send_ids": draw_cell_send_ids(jax.random.fold_in(arg_keys[11], 71), 0),
    }


soft_sq = 0.0025
far_sq = 0.25

def exponent_rows():
    listing = []
    for degree in range(5):
        for power_x in range(degree, -1, -1):
            for power_y in range(degree - power_x, -1, -1):
                listing.append((power_x, power_y, degree - power_x - power_y))
    return listing

def multinomial(triple):
    return math.factorial(sum(triple)) / (math.factorial(triple[0]) * math.factorial(triple[1]) * math.factorial(triple[2]))

def weight_layout():
    triples = exponent_rows()
    position = {triple: number for number, triple in enumerate(triples)}
    weight_table = np.zeros((46, 35))
    s_scale = [1.0, 1.0, 1.5, 2.5, 4.375]
    t_scale = [-0.5, -1.5, -3.75]
    mono_index = []
    radial_index = []
    for number, triple in enumerate(triples):
        weight_table[number, number] = multinomial(triple) * s_scale[sum(triple)]
        mono_index.append(number)
        radial_index.append(sum(triple))
    for number in range(10):
        triple = triples[number]
        for axis_at in range(3):
            raised = list(triple)
            raised[axis_at] += 2
            weight_table[35 + number, position[tuple(raised)]] += multinomial(triple) * t_scale[sum(triple)]
        mono_index.append(number)
        radial_index.append(sum(triple) + 1)
    for axis_one in range(3):
        for axis_two in range(3):
            raised = [0, 0, 0]
            raised[axis_one] += 2
            raised[axis_two] += 2
            weight_table[45, position[tuple(raised)]] += 0.375
    mono_index.append(0)
    radial_index.append(2)
    return (weight_table, mono_index, radial_index)

def monomial_list(comp_x, comp_y, comp_z):
    powers = []
    for component in (comp_x, comp_y, comp_z):
        series = [jnp.ones_like(component)]
        for degree in range(4):
            series.append(series[-1] * component)
        powers.append(series)
    return [powers[0][power_x] * powers[1][power_y] * powers[2][power_z] for power_x, power_y, power_z in exponent_rows()]

def moments_about(rows, centers):
    monomials = monomial_list(rows[:, 0] - centers[0][:, None], rows[:, 1] - centers[1][:, None], rows[:, 2] - centers[2][:, None])
    return jnp.stack([lax.optimization_barrier(jnp.sum(rows[:, 3] * monomial, axis=1)) for monomial in monomials])

def bucket_cells(rows):
    centers = lax.optimization_barrier(jnp.mean(rows[:, :3], axis=2)).T
    moments = moments_about(rows, centers)
    return jnp.concatenate([moments.T, centers.T], axis=1)

def near_field(targets, sources):

    def add_source(number, running):
        source = lax.dynamic_index_in_dim(sources, number, 0, keepdims=False)
        offset = source[:3, :, None] - targets[:, None, :]
        dist_sq = lax.optimization_barrier(jnp.sum(offset * offset, axis=0)) + soft_sq
        weight = source[3][:, None] / (dist_sq * jnp.sqrt(dist_sq))
        return running + lax.optimization_barrier(jnp.sum(offset * weight[None], axis=1))
    return lax.fori_loop(0, sources.shape[0], add_source, jnp.zeros(targets.shape, jnp.float32))

def far_field(targets, cells):
    weight_table, mono_index, radial_index = weight_layout()
    centers = cells[:, 35:38].T
    weights = jnp.dot(cells[:, :35], jnp.asarray(weight_table.T, dtype=jnp.float32), precision=lax.Precision.HIGHEST)

    def potential(points):
        offset = points[:, None, :] - centers[:, :, None]
        rho_sq = lax.optimization_barrier(jnp.sum(offset * offset, axis=0)) + far_sq
        inv_rho = 1.0 / jnp.sqrt(rho_sq)
        inv_sq = 1.0 / rho_sq
        radial = [inv_rho]
        for degree in range(4):
            radial.append(radial[-1] * inv_sq)
        monomials = monomial_list(offset[0], offset[1], offset[2])
        running = jnp.zeros(rho_sq.shape, jnp.float32)
        for number in range(46):
            running = running + monomials[mono_index[number]] * weights[:, number][:, None] * radial[radial_index[number]]
        return jnp.sum(running)
    return jax.grad(potential)(targets)

def reference(positions, masses, old_accel, active, parent_of, parent_centers, local_list, near_list, far_list, send_ids, cell_send_ids):
    rows = jnp.concatenate([positions, masses[None]], axis=0).reshape(4, BUCKETS, BUCKET).transpose(1, 0, 2)
    cells = bucket_cells(rows)
    parent_terms = moments_about(rows, parent_centers[:, parent_of])
    parent_moments = jax.ops.segment_sum(parent_terms.T, parent_of, num_segments=NPAR).T
    per_chip = BUCKETS // CHIPS
    bucket_ids = jnp.arange(BUCKETS, dtype=jnp.int32)
    chip_of = bucket_ids // per_chip
    local_global = (chip_of * per_chip)[:, None] + local_list
    near_device = near_list // RQ
    near_global = near_device * NB + send_ids[near_device, chip_of[:, None], near_list % RQ]
    far_device = far_list // RQC
    far_global = far_device * NB + cell_send_ids[far_device, chip_of[:, None], far_list % RQC]
    source_ids = jnp.concatenate([local_global, near_global], axis=1)

    def one_bucket(bucket_at):

        def compute(bucket_row):
            targets = rows[bucket_row, :3]
            return near_field(targets, rows[source_ids[bucket_row]]) + far_field(targets, cells[far_global[bucket_row]])

        def skipped(bucket_row):
            return jnp.zeros((3, BUCKET), jnp.float32)
        return lax.cond(active[bucket_at] > 0, compute, skipped, bucket_at)
    computed = lax.map(one_bucket, bucket_ids)
    new_accel = computed.transpose(1, 0, 2).reshape(3, PARTICLES)
    active_cols = jnp.repeat(active > 0, BUCKET)
    return (jnp.where(active_cols[None, :], new_accel, old_accel), parent_moments)
```

```python
import functools
import math

import jax
import jax.numpy as jnp
import numpy as np
from jax import lax
from jax.experimental import pallas as pl
from jax.experimental.pallas import tpu as pltpu
from jax.sharding import PartitionSpec as P

BUCKET = 256
NB = 32
RQ = 4
RQC = 8


soft_sq = 0.0025
far_sq = 0.25


def exponent_rows():
    listing = []
    for degree in range(5):
        for power_x in range(degree, -1, -1):
            for power_y in range(degree - power_x, -1, -1):
                listing.append((power_x, power_y, degree - power_x - power_y))
    return listing


def multinomial(triple):
    return math.factorial(sum(triple)) / (
        math.factorial(triple[0]) * math.factorial(triple[1]) * math.factorial(triple[2])
    )


def weight_layout():
    triples = exponent_rows()
    position = {triple: number for number, triple in enumerate(triples)}
    weight_table = np.zeros((46, 35))
    s_scale = [1.0, 1.0, 1.5, 2.5, 4.375]
    t_scale = [-0.5, -1.5, -3.75]
    mono_index = []
    radial_index = []
    for number, triple in enumerate(triples):
        weight_table[number, number] = multinomial(triple) * s_scale[sum(triple)]
        mono_index.append(number)
        radial_index.append(sum(triple))
    for number in range(10):
        triple = triples[number]
        for axis_at in range(3):
            raised = list(triple)
            raised[axis_at] += 2
            weight_table[35 + number, position[tuple(raised)]] += (
                multinomial(triple) * t_scale[sum(triple)]
            )
        mono_index.append(number)
        radial_index.append(sum(triple) + 1)
    for axis_one in range(3):
        for axis_two in range(3):
            raised = [0, 0, 0]
            raised[axis_one] += 2
            raised[axis_two] += 2
            weight_table[45, position[tuple(raised)]] += 0.375
    mono_index.append(0)
    radial_index.append(2)
    return (weight_table, mono_index, radial_index)


def monomial_list(comp_x, comp_y, comp_z):
    powers = []
    for component in (comp_x, comp_y, comp_z):
        series = [jnp.ones_like(component)]
        for degree in range(4):
            series.append(series[-1] * component)
        powers.append(series)
    return [
        powers[0][power_x] * powers[1][power_y] * powers[2][power_z]
        for power_x, power_y, power_z in exponent_rows()
    ]


def gradient_table():
    weight_table, _, _ = weight_layout()
    triples = exponent_rows()
    position = {triple: number for number, triple in enumerate(triples)}
    table = np.zeros((128, 38))

    def lowered(numbers, first, base, start, count):
        for offset, number in enumerate(numbers):
            triple = triples[first + offset]
            for axis_at in range(3):
                if triple[axis_at] > 0:
                    less = list(triple)
                    less[axis_at] -= 1
                    column = base + axis_at * count + position[tuple(less)] - start
                    table[column, :35] += triple[axis_at] * weight_table[number]

    lowered(range(20, 35), 20, 0, 10, 10)
    lowered(range(10, 20), 10, 30, 4, 6)
    lowered(range(39, 45), 4, 48, 1, 3)
    lowered(range(4, 10), 4, 57, 1, 3)
    lowered(range(36, 39), 1, 66, 0, 1)
    lowered(range(1, 4), 1, 69, 0, 1)
    table[72, :35] = weight_table[0]
    table[73, :35] = weight_table[35]
    table[74, :35] = weight_table[45]
    for axis_at in range(3):
        table[75 + axis_at, 35 + axis_at] = 1.0
    return table


def split_three(value):
    first = value.astype(jnp.bfloat16).astype(jnp.float32)
    rest = value - first
    second = rest.astype(jnp.bfloat16).astype(jnp.float32)
    return first, second, rest - second


def weighted(columns, base, monomials):
    total = columns[base] * monomials[0]
    for number in range(1, len(monomials)):
        total = total + columns[base + number] * monomials[number]
    return total


def far_group(cells, points):
    columns = [cells[:, number : number + 1] for number in range(78)]
    r = [points[axis_at : axis_at + 1, :] - columns[75 + axis_at] for axis_at in range(3)]
    x, y, z = r
    xx, xy, xz, yy, yz, zz = x * x, x * y, x * z, y * y, y * z, z * z
    rho_sq = xx + yy + zz + far_sq
    inv_rho = lax.rsqrt(rho_sq)
    inv_sq = inv_rho * inv_rho
    radial = [inv_rho]
    for degree in range(5):
        radial.append(radial[-1] * inv_sq)
    quad = [xx, xy, xz, yy, yz, zz]
    cubic = [
        xx * x, xx * y, xx * z, x * yy, x * yz, x * zz, yy * y, yy * z, y * zz, zz * z,
    ]

    def dot(grad):
        return x * grad[0] + y * grad[1] + z * grad[2]

    grad_four = [weighted(columns, 10 * axis_at, cubic) for axis_at in range(3)]
    scalar = (2.25 * radial[5]) * dot(grad_four)
    total = [radial[4] * grad for grad in grad_four]
    grad_three = [weighted(columns, 30 + 6 * axis_at, quad) for axis_at in range(3)]
    grad_two_t = [weighted(columns, 48 + 3 * axis_at, r) for axis_at in range(3)]
    value_three = dot(grad_three) * (1.0 / 3.0) + dot(grad_two_t) * 0.5
    scalar = scalar + (7.0 * radial[4]) * value_three
    total = [
        t + radial[3] * (a + b) for t, a, b in zip(total, grad_three, grad_two_t)
    ]
    grad_two = [weighted(columns, 57 + 3 * axis_at, r) for axis_at in range(3)]
    value_two = dot(grad_two) * 0.5 + dot(columns[66:69]) + columns[74]
    scalar = scalar + (5.0 * radial[3]) * value_two
    total = [
        t + radial[2] * (a + b) for t, a, b in zip(total, grad_two, columns[66:69])
    ]
    value_one = dot(columns[69:72]) + columns[73]
    scalar = scalar + (3.0 * radial[2]) * value_one + radial[1] * columns[72]
    return [t + radial[1] * a - c * scalar for t, a, c in zip(total, columns[69:72], r)]


def split_two(value):
    high = value.astype(jnp.bfloat16).astype(jnp.float32)
    return high, value - high


def near_sum(target, source_of, count):
    row_at = lax.broadcasted_iota(jnp.int32, (8, BUCKET), 0)
    twice = jnp.concatenate([target, target], axis=0)
    middle = jnp.where(row_at % 4 == 3, 0.0, jnp.mean(twice, axis=1, keepdims=True))
    at = twice - middle
    norm = jnp.sum(jnp.where(row_at < 3, at * at, 0.0), axis=0, keepdims=True) + soft_sq
    feature = jnp.where(
        row_at < 3, -2.0 * at, jnp.where(row_at == 3, norm, jnp.where(row_at < 7, 1.0, 0.0))
    )
    one, two, three = split_three(feature)
    lhs = jnp.concatenate([one, two, three, one, two, one], axis=0).astype(jnp.bfloat16)
    running = jnp.zeros((8, BUCKET), jnp.float32)
    for number in range(count):
        source = source_of(number)
        offset = jnp.concatenate([source, source], axis=0) - middle
        feature = jnp.where(row_at < 3, offset, jnp.where(row_at == 3, 1.0, offset * offset))
        one, two, three = split_three(feature)
        rhs = jnp.concatenate([one, one, one, two, two, three], axis=0).astype(jnp.bfloat16)
        carried = jnp.where(row_at % 4 == 3, 1.0, offset) * source[3:4, :]
        high, low = split_two(carried)
        values = jnp.where(row_at < 4, high, low).astype(jnp.bfloat16)
        dist_sq = lax.dot_general(
            rhs, lhs, (((0,), (0,)), ((), ())), preferred_element_type=jnp.float32
        )
        inv = lax.rsqrt(dist_sq)
        weight = inv * inv * inv
        coarse = weight.astype(jnp.bfloat16)
        fine = (weight - coarse.astype(jnp.float32)).astype(jnp.bfloat16)
        for part in (coarse, fine):
            running = running + jnp.dot(values, part, preferred_element_type=jnp.float32)
    summed = running[0:4] + running[4:8]
    return summed[0:3] - at[0:3] * summed[3:4]


def far_sum(target, table_ref, index_of, count, cells):
    for number in range(count):
        cells[pl.ds(number, 1), :] = table_ref[pl.ds(index_of(number), 1), :]
    parts = None
    for group in range(count // 8):
        piece = far_group(cells[8 * group : 8 * group + 8, :], target)
        parts = piece if parts is None else [a + b for a, b in zip(parts, piece)]
    return jnp.concatenate([jnp.sum(part, axis=0, keepdims=True) for part in parts], axis=0)


def field_kernel(
    counts, active_ref, names_ref, chip_ref, pool_ref, table_ref, old_ref, out_ref, cells
):
    local_count, near_count, far_count = counts
    my_sub = lax.axis_index("sub")
    out_ref[...] = old_ref[...]
    buckets = out_ref.shape[1] // BUCKET

    def visit(bucket, carry):
        row = my_sub * buckets + bucket

        @pl.when(active_ref[row] > 0)
        def _():
            target = chip_ref[row]

            def source_of(number):
                name = names_ref[number, row]
                return chip_ref[name] if number < local_count else pool_ref[name]

            near = near_sum(target, source_of, local_count + near_count)
            far = far_sum(
                target,
                table_ref,
                lambda number: names_ref[local_count + near_count + number, row],
                far_count,
                cells,
            )
            out_ref[:, pl.ds(pl.multiple_of(bucket * BUCKET, BUCKET), BUCKET)] = near + far

        return carry

    lax.fori_loop(0, buckets, visit, 0)


def fields(counts, active, names, chip_rows, pool_rows, table, old_accel):
    smem = pl.BlockSpec(memory_space=pltpu.SMEM)
    vmem = pl.BlockSpec(memory_space=pltpu.VMEM)
    return pl.pallas_call(
        functools.partial(field_kernel, counts),
        out_shape=jax.ShapeDtypeStruct(old_accel.shape, jnp.float32),
        in_specs=[smem] * 2 + [vmem] * 4,
        out_specs=vmem,
        scratch_shapes=[pltpu.VMEM((counts[2], 128), jnp.float32)],
    )(active, names, chip_rows, pool_rows, table, old_accel)


PACK = 3
WIDTH = 40


def packed_columns(columns, rows):
    lane_at = lax.broadcasted_iota(jnp.int32, (rows, 128), 1)
    result = jnp.zeros((rows, 128), jnp.float32)
    for number, column in enumerate(columns):
        result = jnp.where(lane_at == number, column, result)
    return result


def moment_columns(comp, centers):
    monomials = monomial_list(
        comp[0] - centers[0], comp[1] - centers[1], comp[2] - centers[2]
    )
    return [jnp.sum(comp[3] * monomial, axis=1, keepdims=True) for monomial in monomials]


def exchange_kernel(
    positions_ref, masses_ref, parent_of_ref, send_ref, cell_send_ref, parent_centers_ref, expand_ref,
    chip_ref, pool_ref, table_ref, parent_ref,
    rows, blocks, comp, spread, one_hot, pick, cell_out, term_out, term_in, cell_in, halves,
    send_sem, recv_sem, near_sem, far_sem,
):
    subs = lax.axis_size("sub")
    my_dom = lax.axis_index("dom")
    my_sub = lax.axis_index("sub")
    chips = lax.axis_size("dom")
    count = rows.shape[0]
    parents = parent_ref.shape[1]
    deep = -(-parents // PACK)
    barrier = pltpu.get_barrier_semaphore()
    mesh_ids = pl.DeviceIdType.MESH
    sibling = (my_dom, lax.rem(my_sub + 1, subs))

    def chip_at(step):
        return lax.rem(my_dom + step, chips)

    def greet(step, carry):
        pl.semaphore_signal(
            barrier, inc=1, device_id=(chip_at(step), my_sub), device_id_type=mesh_ids
        )
        return carry

    pl.semaphore_signal(barrier, inc=1, device_id=sibling, device_id_type=mesh_ids)
    lax.fori_loop(1, chips, greet, 0)

    for bucket in range(count):
        lanes = pl.ds(bucket * BUCKET, BUCKET)
        tile = jnp.concatenate([positions_ref[:, lanes], masses_ref[:, lanes]], axis=0)
        rows[bucket] = tile
        for axis_at in range(4):
            comp[axis_at, pl.ds(bucket, 1), :] = tile[axis_at : axis_at + 1, :]

    def gather(chip, carry):
        for slot in range(RQ):
            blocks[chip, slot] = rows[jnp.maximum(send_ref[slot, chip], 0)]
        return carry

    lax.fori_loop(0, chips, gather, 0)

    values = [comp[axis_at] for axis_at in range(4)]
    centers = [jnp.mean(values[axis_at], axis=1, keepdims=True) for axis_at in range(3)]
    cells = packed_columns(moment_columns(values, centers) + centers, count)
    for lap in range(PACK):
        spread[lap] = cells if lap == 0 else pltpu.roll(cells, WIDTH * lap, 1)

    def gather_cells(chip, carry):
        for row in range(cell_out.shape[1]):
            total = None
            for lap in range(PACK):
                slot = PACK * row + lap
                if slot < RQC:
                    piece = spread[lap, pl.ds(jnp.maximum(cell_send_ref[slot, chip], 0), 1), :]
                    total = piece if total is None else total + piece
            if total is None:
                total = jnp.zeros((1, 128), jnp.float32)
            cell_out[chip, pl.ds(row, 1), :] = total
        return carry

    lax.fori_loop(0, chips, gather_cells, 0)

    wide = lax.broadcasted_iota(jnp.int32, (1, one_hot.shape[1]), 1)
    lane = lax.broadcasted_iota(jnp.int32, (1, pick.shape[2]), 1)
    chip_of, deep_of = lane // 8, lane % 8
    for bucket in range(count):
        owner = parent_of_ref[bucket]
        one_hot[pl.ds(bucket, 1), :] = jnp.where(wide == owner, 1.0, 0.0)
        for lap in range(PACK):
            within = deep_of + deep * lap
            named = (deep_of < deep) & (within < parents) & (chip_of * parents + within == owner)
            pick[lap, pl.ds(bucket, 1), :] = jnp.where(named, 1.0, 0.0)
    centers_of = lax.dot_general(
        one_hot[...], parent_centers_ref[...], (((1,), (1,)), ((), ())),
        precision=lax.Precision.HIGHEST, preferred_element_type=jnp.float32,
    )
    terms = packed_columns(
        moment_columns(values, [centers_of[:, axis_at : axis_at + 1] for axis_at in range(3)]), count
    )
    sums = None
    for lap in range(PACK):
        piece = lax.dot_general(
            pick[lap], terms if lap == 0 else pltpu.roll(terms, WIDTH * lap, 1),
            (((0,), (0,)), ((), ())),
            precision=lax.Precision.HIGHEST, preferred_element_type=jnp.float32,
        )
        sums = piece if sums is None else sums + piece
    term_out[...] = sums.reshape(term_out.shape)

    pl.semaphore_wait(barrier, chips + subs - 2)
    own_rows = chip_ref.at[pl.ds(my_sub * count, count)]
    twin = pltpu.make_async_remote_copy(
        src_ref=rows, dst_ref=own_rows, send_sem=near_sem.at[0], recv_sem=near_sem.at[1],
        device_id=sibling, device_id_type=mesh_ids,
    )
    twin.start()
    outgoing = ((term_out, term_in), (cell_out, cell_in.at[my_sub]), (blocks, pool_ref.at[my_sub]))

    def copy_to(number, step):
        source, sink = outgoing[number]
        to_dom = chip_at(step)
        return pltpu.make_async_remote_copy(
            src_ref=source.at[to_dom], dst_ref=sink.at[my_dom],
            send_sem=send_sem.at[number], recv_sem=recv_sem.at[number, step],
            device_id=(to_dom, my_sub), device_id_type=mesh_ids,
        )

    def arrived(number, step):
        sink = outgoing[number][1].at[lax.rem(my_dom + chips - step, chips)]
        pltpu.make_async_copy(sink, sink, recv_sem.at[number, step]).wait()

    def turn(place):
        return lax.rem(place + chips // 2 - 1, chips - 1) + 1

    for number in range(2):

        def send(place, carry):
            copy_to(number, turn(place)).start()
            return carry

        lax.fori_loop(0, chips - 1, send, 0)

    def send_block(place, carry):
        copy_to(2, turn(place)).start()
        return carry

    lax.fori_loop(0, chips - 1, send_block, 0)
    for number, (source, sink) in enumerate(outgoing):
        pltpu.make_async_copy(
            source.at[my_dom], sink.at[my_dom], recv_sem.at[number, 0]
        ).start()
    mine = pltpu.make_async_copy(rows, own_rows, near_sem.at[2])
    mine.start()

    def forward(number, step):
        piece = outgoing[number][1].at[lax.rem(my_dom + chips - step, chips)]
        return pltpu.make_async_remote_copy(
            src_ref=piece, dst_ref=piece, send_sem=far_sem.at[2 * number], recv_sem=far_sem.at[2 * number + 1],
            device_id=sibling, device_id_type=mesh_ids,
        )

    def wait_terms(step, carry):
        arrived(0, step)
        return carry

    lax.fori_loop(0, chips, wait_terms, 0)
    halves[my_sub] = jnp.sum(term_in[...], axis=0)
    swap = pltpu.make_async_remote_copy(
        src_ref=halves.at[my_sub], dst_ref=halves.at[my_sub], send_sem=far_sem.at[0], recv_sem=far_sem.at[1],
        device_id=sibling, device_id_type=mesh_ids,
    )

    def relay(number):
        def one(place, carry):
            step = turn(place)
            arrived(number, step)
            forward(number, step).start()
            return carry

        arrived(number, 0)
        forward(number, 0).start()
        lax.fori_loop(0, chips - 1, one, 0)

    relay(1)
    swap.start()
    relay(2)

    def settle(ref, sem):
        pltpu.make_async_copy(ref, ref, sem).wait()

    twin.wait()
    mine.wait()
    settle(halves.at[0], far_sem.at[0])
    settle(halves.at[0], far_sem.at[1])
    total = halves[0]
    for sub in range(1, halves.shape[0]):
        total = total + halves[sub]
    for lap in range(PACK):
        size = min(deep, parents - lap * deep)
        turned = (total if lap == 0 else pltpu.roll(total, 128 - WIDTH * lap, 1)).T
        parent_ref[:, lap * deep : lap * deep + size] = turned[: parent_ref.shape[0], :size]
    settle(cell_in.at[0], far_sem.at[2])
    settle(cell_in.at[0], far_sem.at[3])
    packed = cell_in[...].reshape(-1, 128)
    for lap in range(PACK):
        table_ref[lap] = jnp.dot(
            packed, expand_ref[lap], precision=lax.Precision.HIGHEST, preferred_element_type=jnp.float32
        )
    settle(pool_ref.at[0], far_sem.at[4])
    settle(pool_ref.at[0], far_sem.at[5])
    for number, (source, sink) in enumerate(outgoing):
        sent = source.at[pl.ds(0, chips - 1)]
        settle(sent, send_sem.at[number])


def exchange(positions, masses, parent_of, send_ids, cell_send_ids, parent_centers, moment_count):
    subs = lax.axis_size("sub")
    chips = lax.axis_size("dom")
    parent_total = parent_centers.shape[1]
    parents = parent_total // chips
    cell_rows = 4
    vmem = pl.BlockSpec(memory_space=pltpu.VMEM)
    smem = pl.BlockSpec(memory_space=pltpu.SMEM)
    table = gradient_table()
    expand = np.zeros((PACK, 128, 128))
    for lap in range(PACK):
        expand[lap, WIDTH * lap : WIDTH * lap + 38] = table[:, :38].T
    shapes = (
        (subs * NB, 4, BUCKET),
        (subs, chips, RQ, 4, BUCKET),
        (PACK, subs * chips * cell_rows, 128),
        (moment_count, parents),
    )
    f32 = jnp.float32
    return pl.pallas_call(
        exchange_kernel,
        out_shape=[jax.ShapeDtypeStruct(shape, f32) for shape in shapes],
        in_specs=[vmem] * 2 + [smem] * 3 + [vmem] * 2,
        out_specs=[vmem] * 4,
        scratch_shapes=[
            pltpu.VMEM((NB, 4, BUCKET), f32),
            pltpu.VMEM((chips, RQ, 4, BUCKET), f32),
            pltpu.VMEM((4, NB, BUCKET), f32),
            pltpu.VMEM((PACK, NB, 128), f32),
            pltpu.VMEM((NB, parent_total), f32),
            pltpu.VMEM((PACK, NB, chips * 8), f32),
            pltpu.VMEM((chips, cell_rows, 128), f32),
            pltpu.VMEM((chips, 8, 128), f32),
            pltpu.VMEM((chips, 8, 128), f32),
            pltpu.VMEM((subs, chips, cell_rows, 128), f32),
            pltpu.VMEM((subs, 8, 128), f32),
            pltpu.SemaphoreType.DMA((3,)),
            pltpu.SemaphoreType.DMA((3, chips)),
            pltpu.SemaphoreType.DMA((3,)),
            pltpu.SemaphoreType.DMA((6,)),
        ],
        compiler_params=pltpu.CompilerParams(collective_id=0, has_side_effects=True),
    )(positions, masses, parent_of, send_ids, cell_send_ids, parent_centers, jnp.asarray(expand, f32))


def local(
    positions,
    masses,
    old_accel,
    active,
    parent_of,
    parent_centers,
    local_list,
    near_list,
    far_list,
    send_ids,
    cell_send_ids,
):
    subs, chips = lax.axis_size("sub"), lax.axis_size("dom")

    def place(entry, slots):
        device = entry // slots
        return (device % subs) * chips + device // subs

    near_slots = place(near_list, RQ) * RQ + near_list % RQ
    slot = far_list % RQC
    far_slots = (slot % PACK) * (subs * chips * 4) + place(far_list, RQC) * 4 + slot // PACK
    names = jnp.concatenate([local_list, near_slots, far_slots], axis=1).T
    moment_count = len(exponent_rows())
    chip_rows, pool, table, parent_moments = exchange(
        positions, masses[None], parent_of, send_ids[0].T, cell_send_ids[0].T, parent_centers, moment_count
    )
    counts = (local_list.shape[1], near_list.shape[1], far_list.shape[1])
    accel = fields(
        counts, active, names, chip_rows, pool.reshape(-1, 4, BUCKET), table.reshape(-1, 128), old_accel
    )
    return (accel, parent_moments)


def solution(mesh):
    return jax.shard_map(
        local,
        mesh=mesh,
        in_specs=(
            P(None, ("dom", "sub")),
            P(("dom", "sub")),
            P(None, ("dom", "sub")),
            P("dom"),
            P(("dom", "sub")),
            P(),
            P("dom", None),
            P("dom", None),
            P("dom", None),
            P(("dom", "sub"), None, None),
            P(("dom", "sub"), None, None),
        ),
        out_specs=(P(None, ("dom", "sub")), P(None, "dom")),
        check_vma=False,
    )
```

```python
import functools
import math

import jax
import jax.numpy as jnp
import numpy as np
from jax import lax
from jax.experimental import pallas as pl
from jax.experimental.pallas import tpu as pltpu
from jax.sharding import PartitionSpec as P

BUCKET = 256
NB = 32
RQ = 4
RQC = 8


soft_sq = 0.0025
far_sq = 0.25


def exponent_rows():
    listing = []
    for degree in range(5):
        for power_x in range(degree, -1, -1):
            for power_y in range(degree - power_x, -1, -1):
                listing.append((power_x, power_y, degree - power_x - power_y))
    return listing


def multinomial(triple):
    return math.factorial(sum(triple)) / (
        math.factorial(triple[0]) * math.factorial(triple[1]) * math.factorial(triple[2])
    )


def weight_layout():
    triples = exponent_rows()
    position = {triple: number for number, triple in enumerate(triples)}
    weight_table = np.zeros((46, 35))
    s_scale = [1.0, 1.0, 1.5, 2.5, 4.375]
    t_scale = [-0.5, -1.5, -3.75]
    mono_index = []
    radial_index = []
    for number, triple in enumerate(triples):
        weight_table[number, number] = multinomial(triple) * s_scale[sum(triple)]
        mono_index.append(number)
        radial_index.append(sum(triple))
    for number in range(10):
        triple = triples[number]
        for axis_at in range(3):
            raised = list(triple)
            raised[axis_at] += 2
            weight_table[35 + number, position[tuple(raised)]] += (
                multinomial(triple) * t_scale[sum(triple)]
            )
        mono_index.append(number)
        radial_index.append(sum(triple) + 1)
    for axis_one in range(3):
        for axis_two in range(3):
            raised = [0, 0, 0]
            raised[axis_one] += 2
            raised[axis_two] += 2
            weight_table[45, position[tuple(raised)]] += 0.375
    mono_index.append(0)
    radial_index.append(2)
    return (weight_table, mono_index, radial_index)


def monomial_list(comp_x, comp_y, comp_z):
    powers = []
    for component in (comp_x, comp_y, comp_z):
        series = [jnp.ones_like(component)]
        for degree in range(4):
            series.append(series[-1] * component)
        powers.append(series)
    return [
        powers[0][power_x] * powers[1][power_y] * powers[2][power_z]
        for power_x, power_y, power_z in exponent_rows()
    ]


def gradient_table():
    weight_table, _, _ = weight_layout()
    triples = exponent_rows()
    position = {triple: number for number, triple in enumerate(triples)}
    table = np.zeros((128, 38))

    def lowered(numbers, first, base, start, count):
        for offset, number in enumerate(numbers):
            triple = triples[first + offset]
            for axis_at in range(3):
                if triple[axis_at] > 0:
                    less = list(triple)
                    less[axis_at] -= 1
                    column = base + axis_at * count + position[tuple(less)] - start
                    table[column, :35] += triple[axis_at] * weight_table[number]

    lowered(range(20, 35), 20, 0, 10, 10)
    lowered(range(10, 20), 10, 30, 4, 6)
    lowered(range(39, 45), 4, 48, 1, 3)
    lowered(range(4, 10), 4, 57, 1, 3)
    lowered(range(36, 39), 1, 66, 0, 1)
    lowered(range(1, 4), 1, 69, 0, 1)
    table[72, :35] = weight_table[0]
    table[73, :35] = weight_table[35]
    table[74, :35] = weight_table[45]
    for axis_at in range(3):
        table[75 + axis_at, 35 + axis_at] = 1.0
    return table


def split_three(value):
    first = value.astype(jnp.bfloat16).astype(jnp.float32)
    rest = value - first
    second = rest.astype(jnp.bfloat16).astype(jnp.float32)
    return first, second, rest - second


def weighted(columns, base, monomials):
    total = columns[base] * monomials[0]
    for number in range(1, len(monomials)):
        total = total + columns[base + number] * monomials[number]
    return total


def far_group(cells, points):
    columns = [cells[:, number : number + 1] for number in range(78)]
    r = [points[axis_at : axis_at + 1, :] - columns[75 + axis_at] for axis_at in range(3)]
    x, y, z = r
    xx, xy, xz, yy, yz, zz = x * x, x * y, x * z, y * y, y * z, z * z
    rho_sq = xx + yy + zz + far_sq
    inv_rho = lax.rsqrt(rho_sq)
    inv_sq = inv_rho * inv_rho
    radial = [inv_rho]
    for degree in range(5):
        radial.append(radial[-1] * inv_sq)
    quad = [xx, xy, xz, yy, yz, zz]
    cubic = [
        xx * x, xx * y, xx * z, x * yy, x * yz, x * zz, yy * y, yy * z, y * zz, zz * z,
    ]

    def dot(grad):
        return x * grad[0] + y * grad[1] + z * grad[2]

    grad_four = [weighted(columns, 10 * axis_at, cubic) for axis_at in range(3)]
    scalar = (2.25 * radial[5]) * dot(grad_four)
    total = [radial[4] * grad for grad in grad_four]
    grad_three = [weighted(columns, 30 + 6 * axis_at, quad) for axis_at in range(3)]
    grad_two_t = [weighted(columns, 48 + 3 * axis_at, r) for axis_at in range(3)]
    value_three = dot(grad_three) * (1.0 / 3.0) + dot(grad_two_t) * 0.5
    scalar = scalar + (7.0 * radial[4]) * value_three
    total = [
        t + radial[3] * (a + b) for t, a, b in zip(total, grad_three, grad_two_t)
    ]
    grad_two = [weighted(columns, 57 + 3 * axis_at, r) for axis_at in range(3)]
    value_two = dot(grad_two) * 0.5 + dot(columns[66:69]) + columns[74]
    scalar = scalar + (5.0 * radial[3]) * value_two
    total = [
        t + radial[2] * (a + b) for t, a, b in zip(total, grad_two, columns[66:69])
    ]
    value_one = dot(columns[69:72]) + columns[73]
    scalar = scalar + (3.0 * radial[2]) * value_one + radial[1] * columns[72]
    return [t + radial[1] * a - c * scalar for t, a, c in zip(total, columns[69:72], r)]


def split_two(value):
    high = value.astype(jnp.bfloat16).astype(jnp.float32)
    return high, value - high


def near_sum(target, source_of, count):
    row_at = lax.broadcasted_iota(jnp.int32, (8, BUCKET), 0)
    twice = jnp.concatenate([target, target], axis=0)
    middle = jnp.where(row_at % 4 == 3, 0.0, jnp.mean(twice, axis=1, keepdims=True))
    at = twice - middle
    norm = jnp.sum(jnp.where(row_at < 3, at * at, 0.0), axis=0, keepdims=True) + soft_sq
    feature = jnp.where(
        row_at < 3, -2.0 * at, jnp.where(row_at == 3, norm, jnp.where(row_at < 7, 1.0, 0.0))
    )
    one, two, three = split_three(feature)
    lhs = jnp.concatenate([one, two, three, one, two, one], axis=0).astype(jnp.bfloat16)
    running = jnp.zeros((8, BUCKET), jnp.float32)
    for number in range(count):
        source = source_of(number)
        offset = jnp.concatenate([source, source], axis=0) - middle
        feature = jnp.where(row_at < 3, offset, jnp.where(row_at == 3, 1.0, offset * offset))
        one, two, three = split_three(feature)
        rhs = jnp.concatenate([one, one, one, two, two, three], axis=0).astype(jnp.bfloat16)
        carried = jnp.where(row_at % 4 == 3, 1.0, offset) * source[3:4, :]
        high, low = split_two(carried)
        values = jnp.where(row_at < 4, high, low).astype(jnp.bfloat16)
        dist_sq = lax.dot_general(
            rhs, lhs, (((0,), (0,)), ((), ())), preferred_element_type=jnp.float32
        )
        inv = lax.rsqrt(dist_sq)
        weight = inv * inv * inv
        coarse = weight.astype(jnp.bfloat16)
        fine = (weight - coarse.astype(jnp.float32)).astype(jnp.bfloat16)
        for part in (coarse, fine):
            running = running + jnp.dot(values, part, preferred_element_type=jnp.float32)
    summed = running[0:4] + running[4:8]
    return summed[0:3] - at[0:3] * summed[3:4]


def far_sum(target, table_ref, index_of, count, cells):
    for number in range(count):
        cells[pl.ds(number, 1), :] = table_ref[pl.ds(index_of(number), 1), :]
    parts = None
    for group in range(count // 8):
        piece = far_group(cells[8 * group : 8 * group + 8, :], target)
        parts = piece if parts is None else [a + b for a, b in zip(parts, piece)]
    return jnp.concatenate([jnp.sum(part, axis=0, keepdims=True) for part in parts], axis=0)


def field_kernel(
    active_ref, local_ref, near_ref, far_ref, chip_ref, pool_ref, table_ref, parent_ref, old_ref,
    out_ref, parent_out_ref, cells,
):
    my_sub = lax.axis_index("sub")
    subs, chips = lax.axis_size("sub"), lax.axis_size("dom")
    local_count, near_count = local_ref.shape[0], near_ref.shape[0]
    lap_rows = table_ref.shape[0] // PACK
    out_ref[...] = old_ref[...]
    parent_out_ref[...] = parent_ref[...]
    buckets = out_ref.shape[1] // BUCKET

    def place(entry, slots):
        device = lax.div(entry, slots)
        return lax.rem(device, subs) * chips + lax.div(device, subs), lax.rem(entry, slots)

    def pool_at(entry):
        where, slot = place(entry, RQ)
        return where * RQ + slot

    def table_at(entry):
        where, slot = place(entry, RQC)
        row = lax.div(slot, PACK)
        return (slot - PACK * row) * lap_rows + where * CELL_ROWS + row

    def visit(bucket, carry):
        row = my_sub * buckets + bucket

        @pl.when(active_ref[row] > 0)
        def _():
            target = chip_ref[row]

            def source_of(number):
                if number < local_count:
                    return chip_ref[local_ref[number, row]]
                return pool_ref[pool_at(near_ref[number - local_count, row])]

            near = near_sum(target, source_of, local_count + near_count)
            far = far_sum(
                target,
                table_ref,
                lambda number: table_at(far_ref[number, row]),
                far_ref.shape[0],
                cells,
            )
            out_ref[:, pl.ds(pl.multiple_of(bucket * BUCKET, BUCKET), BUCKET)] = near + far

        return carry

    lax.fori_loop(0, buckets, visit, 0)


def fields(active, local_list, near_list, far_list, chip_rows, pool_rows, table, parents, old_accel):
    smem = pl.BlockSpec(memory_space=pltpu.SMEM)
    vmem = pl.BlockSpec(memory_space=pltpu.VMEM)
    return pl.pallas_call(
        field_kernel,
        out_shape=[jax.ShapeDtypeStruct(array.shape, jnp.float32) for array in (old_accel, parents)],
        in_specs=[smem] * 4 + [vmem] * 5,
        out_specs=[vmem] * 2,
        scratch_shapes=[pltpu.VMEM((far_list.shape[1], 128), jnp.float32)],
        compiler_params=pltpu.CompilerParams(vmem_limit_bytes=VMEM_BYTES),
    )(
        active, local_list.T, near_list.T, far_list.T, chip_rows, pool_rows, table, parents, old_accel
    )


PACK = 3
WIDTH = 40
CELL_ROWS = 4
VMEM_BYTES = 24 << 20


def packed_columns(columns, rows):
    lane_at = lax.broadcasted_iota(jnp.int32, (rows, 128), 1)
    result = jnp.zeros((rows, 128), jnp.float32)
    for number, column in enumerate(columns):
        result = jnp.where(lane_at == number, column, result)
    return result


def moment_columns(comp, centers):
    monomials = monomial_list(
        comp[0] - centers[0], comp[1] - centers[1], comp[2] - centers[2]
    )
    return [jnp.sum(comp[3] * monomial, axis=1, keepdims=True) for monomial in monomials]


def exchange_kernel(
    positions_ref, masses_ref, parent_of_ref, send_ref, cell_send_ref, parent_centers_ref, expand_ref,
    chip_ref, pool_ref, table_ref, parent_ref,
    rows, blocks, comp, spread, one_hot, pick, cell_out, term_out, term_in, cell_in, halves,
    send_sem, recv_sem, near_sem, far_sem,
):
    subs = lax.axis_size("sub")
    my_dom = lax.axis_index("dom")
    my_sub = lax.axis_index("sub")
    chips = lax.axis_size("dom")
    count = rows.shape[0]
    parents = parent_ref.shape[0]
    deep = -(-parents // PACK)
    barrier = pltpu.get_barrier_semaphore()
    mesh_ids = pl.DeviceIdType.MESH
    sibling = (my_dom, lax.rem(my_sub + 1, subs))

    def chip_at(step):
        return lax.rem(my_dom + step, chips)

    def greet(step, carry):
        pl.semaphore_signal(
            barrier, inc=1, device_id=(chip_at(step), my_sub), device_id_type=mesh_ids
        )
        return carry

    pl.semaphore_signal(barrier, inc=1, device_id=sibling, device_id_type=mesh_ids)
    lax.fori_loop(1, chips, greet, 0)

    for bucket in range(count):
        lanes = pl.ds(bucket * BUCKET, BUCKET)
        tile = jnp.concatenate([positions_ref[:, lanes], masses_ref[:, lanes]], axis=0)
        rows[bucket] = tile
        for axis_at in range(4):
            comp[axis_at, pl.ds(bucket, 1), :] = tile[axis_at : axis_at + 1, :]

    def gather(chip, carry):
        for slot in range(RQ):
            blocks[chip, slot] = rows[jnp.maximum(send_ref[slot, chip], 0)]
        return carry

    lax.fori_loop(0, chips, gather, 0)

    values = [comp[axis_at] for axis_at in range(4)]
    centers = [jnp.mean(values[axis_at], axis=1, keepdims=True) for axis_at in range(3)]
    cells = packed_columns(moment_columns(values, centers) + centers, count)
    for lap in range(PACK):
        spread[lap] = cells if lap == 0 else pltpu.roll(cells, WIDTH * lap, 1)

    def gather_cells(chip, carry):
        for row in range(cell_out.shape[1]):
            total = None
            for lap in range(PACK):
                slot = PACK * row + lap
                if slot < RQC:
                    piece = spread[lap, pl.ds(jnp.maximum(cell_send_ref[slot, chip], 0), 1), :]
                    total = piece if total is None else total + piece
            if total is None:
                total = jnp.zeros((1, 128), jnp.float32)
            cell_out[chip, pl.ds(row, 1), :] = total
        return carry

    lax.fori_loop(0, chips, gather_cells, 0)

    wide = lax.broadcasted_iota(jnp.int32, (1, one_hot.shape[1]), 1)
    lane = lax.broadcasted_iota(jnp.int32, (1, pick.shape[2]), 1)
    chip_of, deep_of = lane // 8, lane % 8
    for bucket in range(count):
        owner = parent_of_ref[bucket]
        one_hot[pl.ds(bucket, 1), :] = jnp.where(wide == owner, 1.0, 0.0)
        for lap in range(PACK):
            within = deep_of + deep * lap
            named = (deep_of < deep) & (within < parents) & (chip_of * parents + within == owner)
            pick[lap, pl.ds(bucket, 1), :] = jnp.where(named, 1.0, 0.0)
    centers_of = lax.dot_general(
        one_hot[...], parent_centers_ref[...], (((1,), (1,)), ((), ())),
        precision=lax.Precision.HIGHEST, preferred_element_type=jnp.float32,
    )
    terms = packed_columns(
        moment_columns(values, [centers_of[:, axis_at : axis_at + 1] for axis_at in range(3)]), count
    )
    sums = None
    for lap in range(PACK):
        piece = lax.dot_general(
            pick[lap], terms if lap == 0 else pltpu.roll(terms, WIDTH * lap, 1),
            (((0,), (0,)), ((), ())),
            precision=lax.Precision.HIGHEST, preferred_element_type=jnp.float32,
        )
        sums = piece if sums is None else sums + piece
    term_out[...] = sums.reshape(term_out.shape)

    pl.semaphore_wait(barrier, chips + subs - 2)
    own_rows = chip_ref.at[pl.ds(my_sub * count, count)]
    twin = pltpu.make_async_remote_copy(
        src_ref=rows, dst_ref=own_rows, send_sem=near_sem.at[0], recv_sem=near_sem.at[1],
        device_id=sibling, device_id_type=mesh_ids,
    )
    twin.start()
    outgoing = ((term_out, term_in), (cell_out, cell_in.at[my_sub]), (blocks, pool_ref.at[my_sub]))

    def copy_to(number, step):
        source, sink = outgoing[number]
        to_dom = chip_at(step)
        return pltpu.make_async_remote_copy(
            src_ref=source.at[to_dom], dst_ref=sink.at[my_dom],
            send_sem=send_sem.at[number], recv_sem=recv_sem.at[number, step],
            device_id=(to_dom, my_sub), device_id_type=mesh_ids,
        )

    def arrived(number, step):
        sink = outgoing[number][1].at[lax.rem(my_dom + chips - step, chips)]
        pltpu.make_async_copy(sink, sink, recv_sem.at[number, step]).wait()

    def turn(place):
        return lax.rem(place + chips // 2 - 1, chips - 1) + 1

    for number in range(2):

        def send(place, carry):
            copy_to(number, turn(place)).start()
            return carry

        lax.fori_loop(0, chips - 1, send, 0)

    def send_block(place, carry):
        copy_to(2, turn(place)).start()
        return carry

    lax.fori_loop(0, chips - 1, send_block, 0)
    for number, (source, sink) in enumerate(outgoing):
        pltpu.make_async_copy(
            source.at[my_dom], sink.at[my_dom], recv_sem.at[number, 0]
        ).start()
    mine = pltpu.make_async_copy(rows, own_rows, near_sem.at[2])
    mine.start()

    def forward(number, step):
        piece = outgoing[number][1].at[lax.rem(my_dom + chips - step, chips)]
        return pltpu.make_async_remote_copy(
            src_ref=piece, dst_ref=piece, send_sem=far_sem.at[2 * number], recv_sem=far_sem.at[2 * number + 1],
            device_id=sibling, device_id_type=mesh_ids,
        )

    def wait_terms(step, carry):
        arrived(0, step)
        return carry

    lax.fori_loop(0, chips, wait_terms, 0)
    halves[my_sub] = jnp.sum(term_in[...], axis=0)
    swap = pltpu.make_async_remote_copy(
        src_ref=halves.at[my_sub], dst_ref=halves.at[my_sub], send_sem=far_sem.at[0], recv_sem=far_sem.at[1],
        device_id=sibling, device_id_type=mesh_ids,
    )

    def relay(number):
        def one(place, carry):
            step = turn(place)
            arrived(number, step)
            forward(number, step).start()
            return carry

        arrived(number, 0)
        forward(number, 0).start()
        lax.fori_loop(0, chips - 1, one, 0)

    relay(1)
    swap.start()
    relay(2)

    def settle(ref, sem):
        pltpu.make_async_copy(ref, ref, sem).wait()

    twin.wait()
    mine.wait()
    settle(halves.at[0], far_sem.at[0])
    settle(halves.at[0], far_sem.at[1])
    total = halves[0]
    for sub in range(1, halves.shape[0]):
        total = total + halves[sub]
    for lap in range(PACK):
        size = min(deep, parents - lap * deep)
        turned = total if lap == 0 else pltpu.roll(total, 128 - WIDTH * lap, 1)
        parent_ref[lap * deep : lap * deep + size, :] = turned[:size, : parent_ref.shape[1]]
    settle(cell_in.at[0], far_sem.at[2])
    settle(cell_in.at[0], far_sem.at[3])
    packed = cell_in[...].reshape(-1, 128)
    for lap in range(PACK):
        table_ref[lap] = jnp.dot(
            packed, expand_ref[lap], precision=lax.Precision.HIGHEST, preferred_element_type=jnp.float32
        )
    settle(pool_ref.at[0], far_sem.at[4])
    settle(pool_ref.at[0], far_sem.at[5])
    for number, (source, sink) in enumerate(outgoing):
        sent = source.at[pl.ds(0, chips - 1)]
        settle(sent, send_sem.at[number])


def exchange(positions, masses, parent_of, send_ids, cell_send_ids, parent_centers, moment_count):
    subs = lax.axis_size("sub")
    chips = lax.axis_size("dom")
    parent_total = parent_centers.shape[1]
    parents = parent_total // chips
    cell_rows = CELL_ROWS
    vmem = pl.BlockSpec(memory_space=pltpu.VMEM)
    smem = pl.BlockSpec(memory_space=pltpu.SMEM)
    table = gradient_table()
    expand = np.zeros((PACK, 128, 128))
    for lap in range(PACK):
        expand[lap, WIDTH * lap : WIDTH * lap + 38] = table[:, :38].T
    shapes = (
        (subs * NB, 4, BUCKET),
        (subs, chips, RQ, 4, BUCKET),
        (PACK, subs * chips * cell_rows, 128),
        (parents, moment_count),
    )
    f32 = jnp.float32
    return pl.pallas_call(
        exchange_kernel,
        out_shape=[jax.ShapeDtypeStruct(shape, f32) for shape in shapes],
        in_specs=[vmem] * 2 + [smem] * 3 + [vmem] * 2,
        out_specs=[vmem] * 4,
        scratch_shapes=[
            pltpu.VMEM((NB, 4, BUCKET), f32),
            pltpu.VMEM((chips, RQ, 4, BUCKET), f32),
            pltpu.VMEM((4, NB, BUCKET), f32),
            pltpu.VMEM((PACK, NB, 128), f32),
            pltpu.VMEM((NB, parent_total), f32),
            pltpu.VMEM((PACK, NB, chips * 8), f32),
            pltpu.VMEM((chips, cell_rows, 128), f32),
            pltpu.VMEM((chips, 8, 128), f32),
            pltpu.VMEM((chips, 8, 128), f32),
            pltpu.VMEM((subs, chips, cell_rows, 128), f32),
            pltpu.VMEM((subs, 8, 128), f32),
            pltpu.SemaphoreType.DMA((3,)),
            pltpu.SemaphoreType.DMA((3, chips)),
            pltpu.SemaphoreType.DMA((3,)),
            pltpu.SemaphoreType.DMA((6,)),
        ],
        compiler_params=pltpu.CompilerParams(
            collective_id=0, has_side_effects=True, vmem_limit_bytes=VMEM_BYTES
        ),
    )(positions, masses, parent_of, send_ids, cell_send_ids, parent_centers, jnp.asarray(expand, f32))


def local(
    positions,
    masses,
    old_accel,
    active,
    parent_of,
    parent_centers,
    local_list,
    near_list,
    far_list,
    send_ids,
    cell_send_ids,
):
    moment_count = len(exponent_rows())
    chip_rows, pool, table, parents = exchange(
        positions, masses[None], parent_of, send_ids[0].T, cell_send_ids[0].T, parent_centers, moment_count
    )
    accel, parents = fields(
        active,
        local_list,
        near_list,
        far_list,
        chip_rows,
        pool.reshape(-1, 4, BUCKET),
        table.reshape(-1, 128),
        parents,
        old_accel,
    )
    return (accel, parents.T)


def solution(mesh):
    return jax.shard_map(
        local,
        mesh=mesh,
        in_specs=(
            P(None, ("dom", "sub")),
            P(("dom", "sub")),
            P(None, ("dom", "sub")),
            P("dom"),
            P(("dom", "sub")),
            P(),
            P("dom", None),
            P("dom", None),
            P("dom", None),
            P(("dom", "sub"), None, None),
            P(("dom", "sub"), None, None),
        ),
        out_specs=(P(None, ("dom", "sub")), P(None, "dom")),
        check_vma=False,
    )
```

```python
import functools
import math

import jax
import jax.numpy as jnp
import numpy as np
from jax import lax
from jax.experimental import pallas as pl
from jax.experimental.pallas import tpu as pltpu
from jax.sharding import PartitionSpec as P

BUCKET = 256
NB = 32
RQ = 4
RQC = 8


soft_sq = 0.0025
far_sq = 0.25


def exponent_rows():
    listing = []
    for degree in range(5):
        for power_x in range(degree, -1, -1):
            for power_y in range(degree - power_x, -1, -1):
                listing.append((power_x, power_y, degree - power_x - power_y))
    return listing


def multinomial(triple):
    return math.factorial(sum(triple)) / (
        math.factorial(triple[0]) * math.factorial(triple[1]) * math.factorial(triple[2])
    )


def weight_layout():
    triples = exponent_rows()
    position = {triple: number for number, triple in enumerate(triples)}
    weight_table = np.zeros((46, 35))
    s_scale = [1.0, 1.0, 1.5, 2.5, 4.375]
    t_scale = [-0.5, -1.5, -3.75]
    mono_index = []
    radial_index = []
    for number, triple in enumerate(triples):
        weight_table[number, number] = multinomial(triple) * s_scale[sum(triple)]
        mono_index.append(number)
        radial_index.append(sum(triple))
    for number in range(10):
        triple = triples[number]
        for axis_at in range(3):
            raised = list(triple)
            raised[axis_at] += 2
            weight_table[35 + number, position[tuple(raised)]] += (
                multinomial(triple) * t_scale[sum(triple)]
            )
        mono_index.append(number)
        radial_index.append(sum(triple) + 1)
    for axis_one in range(3):
        for axis_two in range(3):
            raised = [0, 0, 0]
            raised[axis_one] += 2
            raised[axis_two] += 2
            weight_table[45, position[tuple(raised)]] += 0.375
    mono_index.append(0)
    radial_index.append(2)
    return (weight_table, mono_index, radial_index)


def monomial_list(comp_x, comp_y, comp_z):
    powers = []
    for component in (comp_x, comp_y, comp_z):
        series = [jnp.ones_like(component)]
        for degree in range(4):
            series.append(series[-1] * component)
        powers.append(series)
    return [
        powers[0][power_x] * powers[1][power_y] * powers[2][power_z]
        for power_x, power_y, power_z in exponent_rows()
    ]


def gradient_table():
    weight_table, _, _ = weight_layout()
    triples = exponent_rows()
    position = {triple: number for number, triple in enumerate(triples)}
    table = np.zeros((128, 38))

    def lowered(numbers, first, base, start, count):
        for offset, number in enumerate(numbers):
            triple = triples[first + offset]
            for axis_at in range(3):
                if triple[axis_at] > 0:
                    less = list(triple)
                    less[axis_at] -= 1
                    column = base + axis_at * count + position[tuple(less)] - start
                    table[column, :35] += triple[axis_at] * weight_table[number]

    lowered(range(20, 35), 20, 0, 10, 10)
    lowered(range(10, 20), 10, 30, 4, 6)
    lowered(range(39, 45), 4, 48, 1, 3)
    lowered(range(4, 10), 4, 57, 1, 3)
    lowered(range(36, 39), 1, 66, 0, 1)
    lowered(range(1, 4), 1, 69, 0, 1)
    table[72, :35] = weight_table[0]
    table[73, :35] = weight_table[35]
    table[74, :35] = weight_table[45]
    for axis_at in range(3):
        table[75 + axis_at, 35 + axis_at] = 1.0
    return table


def split_three(value):
    first = value.astype(jnp.bfloat16).astype(jnp.float32)
    rest = value - first
    second = rest.astype(jnp.bfloat16).astype(jnp.float32)
    return first, second, rest - second


def weighted(columns, base, monomials):
    total = columns[base] * monomials[0]
    for number in range(1, len(monomials)):
        total = total + columns[base + number] * monomials[number]
    return total


def far_group(cells, points):
    columns = [cells[:, number : number + 1] for number in range(78)]
    r = [points[axis_at : axis_at + 1, :] - columns[75 + axis_at] for axis_at in range(3)]
    x, y, z = r
    xx, xy, xz, yy, yz, zz = x * x, x * y, x * z, y * y, y * z, z * z
    rho_sq = xx + yy + zz + far_sq
    inv_rho = lax.rsqrt(rho_sq)
    inv_sq = inv_rho * inv_rho
    radial = [inv_rho]
    for degree in range(5):
        radial.append(radial[-1] * inv_sq)
    quad = [xx, xy, xz, yy, yz, zz]
    cubic = [
        xx * x, xx * y, xx * z, x * yy, x * yz, x * zz, yy * y, yy * z, y * zz, zz * z,
    ]

    def dot(grad):
        return x * grad[0] + y * grad[1] + z * grad[2]

    grad_four = [weighted(columns, 10 * axis_at, cubic) for axis_at in range(3)]
    scalar = (2.25 * radial[5]) * dot(grad_four)
    total = [radial[4] * grad for grad in grad_four]
    grad_three = [weighted(columns, 30 + 6 * axis_at, quad) for axis_at in range(3)]
    grad_two_t = [weighted(columns, 48 + 3 * axis_at, r) for axis_at in range(3)]
    value_three = dot(grad_three) * (1.0 / 3.0) + dot(grad_two_t) * 0.5
    scalar = scalar + (7.0 * radial[4]) * value_three
    total = [
        t + radial[3] * (a + b) for t, a, b in zip(total, grad_three, grad_two_t)
    ]
    grad_two = [weighted(columns, 57 + 3 * axis_at, r) for axis_at in range(3)]
    value_two = dot(grad_two) * 0.5 + dot(columns[66:69]) + columns[74]
    scalar = scalar + (5.0 * radial[3]) * value_two
    total = [
        t + radial[2] * (a + b) for t, a, b in zip(total, grad_two, columns[66:69])
    ]
    value_one = dot(columns[69:72]) + columns[73]
    scalar = scalar + (3.0 * radial[2]) * value_one + radial[1] * columns[72]
    return [t + radial[1] * a - c * scalar for t, a, c in zip(total, columns[69:72], r)]


def split_two(value):
    high = value.astype(jnp.bfloat16).astype(jnp.float32)
    return high, value - high


def near_sum(target, source_of, count):
    row_at = lax.broadcasted_iota(jnp.int32, (8, BUCKET), 0)
    twice = jnp.concatenate([target, target], axis=0)
    middle = jnp.where(row_at % 4 == 3, 0.0, jnp.mean(twice, axis=1, keepdims=True))
    at = twice - middle
    norm = jnp.sum(jnp.where(row_at < 3, at * at, 0.0), axis=0, keepdims=True) + soft_sq
    feature = jnp.where(
        row_at < 3, -2.0 * at, jnp.where(row_at == 3, norm, jnp.where(row_at < 7, 1.0, 0.0))
    )
    one, two, three = split_three(feature)
    lhs = jnp.concatenate([one, two, three, one, two, one], axis=0).astype(jnp.bfloat16)
    running = jnp.zeros((8, BUCKET), jnp.float32)
    for number in range(count):
        source = source_of(number)
        offset = jnp.concatenate([source, source], axis=0) - middle
        feature = jnp.where(row_at < 3, offset, jnp.where(row_at == 3, 1.0, offset * offset))
        one, two, three = split_three(feature)
        rhs = jnp.concatenate([one, one, one, two, two, three], axis=0).astype(jnp.bfloat16)
        carried = jnp.where(row_at % 4 == 3, 1.0, offset) * source[3:4, :]
        high, low = split_two(carried)
        values = jnp.where(row_at < 4, high, low).astype(jnp.bfloat16)
        dist_sq = lax.dot_general(
            rhs, lhs, (((0,), (0,)), ((), ())), preferred_element_type=jnp.float32
        )
        inv = lax.rsqrt(dist_sq)
        weight = inv * inv * inv
        coarse = weight.astype(jnp.bfloat16)
        fine = (weight - coarse.astype(jnp.float32)).astype(jnp.bfloat16)
        for part in (coarse, fine):
            running = running + jnp.dot(values, part, preferred_element_type=jnp.float32)
    summed = running[0:4] + running[4:8]
    return summed[0:3] - at[0:3] * summed[3:4]


def far_sum(target, table_ref, index_of, count, cells):
    for number in range(count):
        cells[pl.ds(number, 1), :] = table_ref[pl.ds(index_of(number), 1), :]
    parts = None
    for group in range(count // 8):
        piece = far_group(cells[8 * group : 8 * group + 8, :], target)
        parts = piece if parts is None else [a + b for a, b in zip(parts, piece)]
    return jnp.concatenate([jnp.sum(part, axis=0, keepdims=True) for part in parts], axis=0)


def field_kernel(
    active_ref, local_ref, near_ref, far_ref, chip_ref, pool_ref, table_ref, parent_ref, early_ref, old_ref,
    out_ref, parent_out_ref, cells,
):
    my_sub = lax.axis_index("sub")
    subs, chips = lax.axis_size("sub"), lax.axis_size("dom")
    local_count, near_count = local_ref.shape[0], near_ref.shape[0]
    lap_rows = table_ref.shape[0] // PACK
    out_ref[...] = old_ref[...]
    parent_out_ref[...] = parent_ref[...]
    buckets = out_ref.shape[1] // BUCKET

    def place(entry, slots):
        device = lax.div(entry, slots)
        return lax.rem(device, subs) * chips + lax.div(device, subs), lax.rem(entry, slots)

    def pool_at(entry):
        where, slot = place(entry, RQ)
        return where * RQ + slot

    def table_at(entry):
        where, slot = place(entry, RQC)
        row = lax.div(slot, PACK)
        return (slot - PACK * row) * lap_rows + where * CELL_ROWS + row

    def visit(bucket, item):
        row = my_sub * buckets + bucket

        def put(near):
            target = chip_ref[row]
            far = far_sum(
                target,
                table_ref,
                lambda number: table_at(far_ref[number, row]),
                far_ref.shape[0],
                cells,
            )
            out_ref[:, pl.ds(pl.multiple_of(bucket * BUCKET, BUCKET), BUCKET)] = near + far

        def near_source(number):
            return pool_ref[pool_at(near_ref[number, row])]

        def any_source(number):
            if number < near_count:
                return near_source(number)
            return chip_ref[local_ref[number - near_count, row]]

        is_active = active_ref[row] > 0
        started = item < early_ref.shape[0]

        @pl.when(is_active & started)
        def _():
            put(near_sum(chip_ref[row], near_source, near_count) + early_ref[item][0:3])

        @pl.when(is_active & jnp.logical_not(started))
        def _():
            put(near_sum(chip_ref[row], any_source, local_count + near_count))

        return item + jnp.where(is_active, 1, 0)

    lax.fori_loop(0, buckets, visit, 0)


def fields(active, local_list, near_list, far_list, chip_rows, pool_rows, table, parents, early, old_accel):
    smem = pl.BlockSpec(memory_space=pltpu.SMEM)
    vmem = pl.BlockSpec(memory_space=pltpu.VMEM)
    return pl.pallas_call(
        field_kernel,
        out_shape=[jax.ShapeDtypeStruct(array.shape, jnp.float32) for array in (old_accel, parents)],
        in_specs=[smem] * 4 + [vmem] * 6,
        out_specs=[vmem] * 2,
        scratch_shapes=[pltpu.VMEM((far_list.shape[1], 128), jnp.float32)],
        compiler_params=pltpu.CompilerParams(vmem_limit_bytes=VMEM_BYTES),
    )(
        active, local_list.T, near_list.T, far_list.T, chip_rows, pool_rows, table, parents, early, old_accel
    )


PACK = 3
WIDTH = 40
CELL_ROWS = 4
ITEMS = 8
IDLE = 3
VMEM_BYTES = 24 << 20


def packed_columns(columns, rows):
    lane_at = lax.broadcasted_iota(jnp.int32, (rows, 128), 1)
    result = jnp.zeros((rows, 128), jnp.float32)
    for number, column in enumerate(columns):
        result = jnp.where(lane_at == number, column, result)
    return result


def moment_columns(comp, centers):
    monomials = monomial_list(
        comp[0] - centers[0], comp[1] - centers[1], comp[2] - centers[2]
    )
    return [jnp.sum(comp[3] * monomial, axis=1, keepdims=True) for monomial in monomials]


def exchange_kernel(
    positions_hbm, masses_hbm, send_hbm, active_hbm, local_hbm, cell_send_hbm, parent_of_hbm,
    parent_centers_hbm, expand_hbm,
    chip_ref, pool_ref, table_ref, parent_ref, early_ref,
    positions_ref, masses_ref, send_ref, active_ref, local_ref, cell_send_ref, parent_of_ref,
    parent_centers_ref, expand_ref,
    rows, blocks, comp, spread, one_hot, pick, cell_out, term_out, term_in, cell_in, halves,
    load_sem, send_sem, recv_sem, near_sem, far_sem,
):
    subs = lax.axis_size("sub")
    my_dom = lax.axis_index("dom")
    my_sub = lax.axis_index("sub")
    chips = lax.axis_size("dom")
    count = rows.shape[0]
    items = early_ref.shape[0]
    parents = parent_ref.shape[0]
    deep = -(-parents // PACK)
    barrier = pltpu.get_barrier_semaphore()
    mesh_ids = pl.DeviceIdType.MESH
    sibling = (my_dom, lax.rem(my_sub + 1, subs))

    def chip_at(step):
        return lax.rem(my_dom + step, chips)

    def greet(step, carry):
        pl.semaphore_signal(
            barrier, inc=1, device_id=(chip_at(step), my_sub), device_id_type=mesh_ids
        )
        return carry

    loads = [
        pltpu.make_async_copy(source, sink, load_sem.at[number])
        for number, (source, sink) in enumerate(
            (
                (positions_hbm, positions_ref),
                (masses_hbm, masses_ref),
                (send_hbm, send_ref),
                (active_hbm, active_ref),
                (local_hbm, local_ref),
                (cell_send_hbm, cell_send_ref),
                (parent_of_hbm, parent_of_ref),
                (parent_centers_hbm, parent_centers_ref),
                (expand_hbm, expand_ref),
            )
        )
    ]
    for load in loads:
        load.start()
    pl.semaphore_signal(barrier, inc=1, device_id=sibling, device_id_type=mesh_ids)
    lax.fori_loop(1, chips, greet, 0)
    for load in loads[:3]:
        load.wait()

    for bucket in range(count):
        lanes = pl.ds(bucket * BUCKET, BUCKET)
        tile = jnp.concatenate([positions_ref[:, lanes], masses_ref[:, lanes]], axis=0)
        rows[bucket] = tile
        for axis_at in range(4):
            comp[axis_at, pl.ds(bucket, 1), :] = tile[axis_at : axis_at + 1, :]

    def gather(chip, carry):
        for slot in range(RQ):
            blocks[chip, slot] = rows[jnp.maximum(send_ref[slot, chip], 0)]
        return carry

    lax.fori_loop(0, chips, gather, 0)

    outgoing = ((term_out, term_in), (cell_out, cell_in.at[my_sub]), (blocks, pool_ref.at[my_sub]))

    def turn(place):
        return lax.rem(place + chips // 2 - 1, chips - 1) + 1

    def copy_to(number, step):
        source, sink = outgoing[number]
        to_dom = chip_at(step)
        return pltpu.make_async_remote_copy(
            src_ref=source.at[to_dom], dst_ref=sink.at[my_dom],
            send_sem=send_sem.at[number], recv_sem=recv_sem.at[number, step],
            device_id=(to_dom, my_sub), device_id_type=mesh_ids,
        )

    def send(number, first, last):
        def one(place, carry):
            copy_to(number, turn(place)).start()
            return carry

        lax.fori_loop(first, last, one, 0)

    def keep(number):
        source, sink = outgoing[number]
        pltpu.make_async_copy(source.at[my_dom], sink.at[my_dom], recv_sem.at[number, 0]).start()

    def arrived(number, step):
        sink = outgoing[number][1].at[lax.rem(my_dom + chips - step, chips)]
        pltpu.make_async_copy(sink, sink, recv_sem.at[number, step]).wait()

    def forward(number, step):
        piece = outgoing[number][1].at[lax.rem(my_dom + chips - step, chips)]
        return pltpu.make_async_remote_copy(
            src_ref=piece, dst_ref=piece,
            send_sem=far_sem.at[2 * number], recv_sem=far_sem.at[2 * number + 1],
            device_id=sibling, device_id_type=mesh_ids,
        )

    def relay(number, first, last):
        def one(place, carry):
            step = turn(place)
            arrived(number, step)
            forward(number, step).start()
            return carry

        lax.fori_loop(first, last, one, 0)

    def relay_own(number):
        arrived(number, 0)
        forward(number, 0).start()

    def settle(ref, sem):
        pltpu.make_async_copy(ref, ref, sem).wait()

    pl.semaphore_wait(barrier, chips + subs - 2)
    own_rows = chip_ref.at[pl.ds(my_sub * count, count)]
    twin = pltpu.make_async_remote_copy(
        src_ref=rows, dst_ref=own_rows, send_sem=near_sem.at[0], recv_sem=near_sem.at[1],
        device_id=sibling, device_id_type=mesh_ids,
    )
    twin.start()
    send(2, 0, chips // 2)
    mine = pltpu.make_async_copy(rows, own_rows, near_sem.at[2])
    mine.start()
    keep(2)
    for load in loads[3:]:
        load.wait()

    values = [comp[axis_at] for axis_at in range(4)]
    centers = [jnp.mean(values[axis_at], axis=1, keepdims=True) for axis_at in range(3)]
    cells = packed_columns(moment_columns(values, centers) + centers, count)
    for lap in range(PACK):
        spread[lap] = cells if lap == 0 else pltpu.roll(cells, WIDTH * lap, 1)

    def gather_cells(chip, carry):
        for row in range(cell_out.shape[1]):
            total = None
            for lap in range(PACK):
                slot = PACK * row + lap
                if slot < RQC:
                    piece = spread[lap, pl.ds(jnp.maximum(cell_send_ref[slot, chip], 0), 1), :]
                    total = piece if total is None else total + piece
            if total is None:
                total = jnp.zeros((1, 128), jnp.float32)
            cell_out[chip, pl.ds(row, 1), :] = total
        return carry

    lax.fori_loop(0, chips, gather_cells, 0)

    wide = lax.broadcasted_iota(jnp.int32, (1, one_hot.shape[1]), 1)
    lane = lax.broadcasted_iota(jnp.int32, (1, pick.shape[2]), 1)
    chip_of, deep_of = lane // 8, lane % 8
    for bucket in range(count):
        owner = parent_of_ref[bucket]
        one_hot[pl.ds(bucket, 1), :] = jnp.where(wide == owner, 1.0, 0.0)
        for lap in range(PACK):
            within = deep_of + deep * lap
            named = (deep_of < deep) & (within < parents) & (chip_of * parents + within == owner)
            pick[lap, pl.ds(bucket, 1), :] = jnp.where(named, 1.0, 0.0)
    centers_of = lax.dot_general(
        one_hot[...], parent_centers_ref[...], (((1,), (1,)), ((), ())),
        precision=lax.Precision.HIGHEST, preferred_element_type=jnp.float32,
    )
    terms = packed_columns(
        moment_columns(values, [centers_of[:, axis_at : axis_at + 1] for axis_at in range(3)]), count
    )
    sums = None
    for lap in range(PACK):
        piece = lax.dot_general(
            pick[lap], terms if lap == 0 else pltpu.roll(terms, WIDTH * lap, 1),
            (((0,), (0,)), ((), ())),
            precision=lax.Precision.HIGHEST, preferred_element_type=jnp.float32,
        )
        sums = piece if sums is None else sums + piece
    term_out[...] = sums.reshape(term_out.shape)
    for number in (1, 0):
        send(number, 0, chips - 1)
        keep(number)
    send(2, chips // 2, chips - 1)
    relay_own(2)
    twin.wait()
    mine.wait()

    def early(item, last):
        base = my_sub * count
        found = count
        for bucket in range(count - 1, -1, -1):
            fits = (active_ref[base + bucket] > 0) & (bucket > last)
            found = jnp.where(fits, bucket, found)
        row = base + jnp.minimum(found, count - 1)
        total = near_sum(
            chip_ref[row], lambda number: chip_ref[local_ref[number, row]], local_ref.shape[0]
        )
        early_ref[item] = jnp.concatenate([total, jnp.zeros((1, BUCKET), jnp.float32)], axis=0)
        share = -(-(chips - 1) // (items - IDLE))

        @pl.when(item >= IDLE)
        def _():
            first = (item - IDLE) * share
            relay(2, first, jnp.minimum(first + share, chips - 1))

        @pl.when(item == items - 2)
        def _():
            lax.fori_loop(0, chips, lambda step, carry: (arrived(0, step), carry)[1], 0)
            halves[my_sub] = jnp.sum(term_in[...], axis=0)
            relay_own(1)
            relay(1, 0, chips - 1)

        return found

    lax.fori_loop(0, items, early, -1)
    swap = pltpu.make_async_remote_copy(
        src_ref=halves.at[my_sub], dst_ref=halves.at[my_sub],
        send_sem=far_sem.at[0], recv_sem=far_sem.at[1],
        device_id=sibling, device_id_type=mesh_ids,
    )
    swap.start()
    settle(cell_in.at[0], far_sem.at[2])
    settle(cell_in.at[0], far_sem.at[3])
    packed = cell_in[...].reshape(-1, 128)
    for lap in range(PACK):
        table_ref[lap] = jnp.dot(
            packed, expand_ref[lap], precision=lax.Precision.HIGHEST, preferred_element_type=jnp.float32
        )
    settle(halves.at[0], far_sem.at[0])
    settle(halves.at[0], far_sem.at[1])
    total = halves[0]
    for sub in range(1, halves.shape[0]):
        total = total + halves[sub]
    for lap in range(PACK):
        size = min(deep, parents - lap * deep)
        turned = total if lap == 0 else pltpu.roll(total, 128 - WIDTH * lap, 1)
        parent_ref[lap * deep : lap * deep + size, :] = turned[:size, : parent_ref.shape[1]]
    settle(pool_ref.at[0], far_sem.at[4])
    settle(pool_ref.at[0], far_sem.at[5])
    for number, (source, sink) in enumerate(outgoing):
        settle(source.at[pl.ds(0, chips - 1)], send_sem.at[number])


def exchange(
    positions, masses, send_ids, active, local_list, cell_send_ids, parent_of, parent_centers, moment_count
):
    subs = lax.axis_size("sub")
    chips = lax.axis_size("dom")
    parent_total = parent_centers.shape[1]
    parents = parent_total // chips
    vmem = pl.BlockSpec(memory_space=pltpu.VMEM)
    table = gradient_table()
    expand = np.zeros((PACK, 128, 128))
    for lap in range(PACK):
        expand[lap, WIDTH * lap : WIDTH * lap + 38] = table[:, :38].T
    shapes = (
        (subs * NB, 4, BUCKET),
        (subs, chips, RQ, 4, BUCKET),
        (PACK, subs * chips * CELL_ROWS, 128),
        (parents, moment_count),
        (ITEMS, 4, BUCKET),
    )
    f32 = jnp.float32
    arrays = (
        positions, masses, send_ids, active, local_list, cell_send_ids, parent_of, parent_centers,
        jnp.asarray(expand, f32),
    )
    spaces = (pltpu.VMEM,) * 2 + (pltpu.SMEM,) * 5 + (pltpu.VMEM,) * 2
    return pl.pallas_call(
        exchange_kernel,
        out_shape=[pltpu.VMEM(shape, f32) for shape in shapes],
        in_specs=[pl.BlockSpec(memory_space=pltpu.HBM)] * len(arrays),
        out_specs=[vmem] * len(shapes),
        scratch_shapes=[space(array.shape, array.dtype) for space, array in zip(spaces, arrays)]
        + [
            pltpu.VMEM((NB, 4, BUCKET), f32),
            pltpu.VMEM((chips, RQ, 4, BUCKET), f32),
            pltpu.VMEM((4, NB, BUCKET), f32),
            pltpu.VMEM((PACK, NB, 128), f32),
            pltpu.VMEM((NB, parent_total), f32),
            pltpu.VMEM((PACK, NB, chips * 8), f32),
            pltpu.VMEM((chips, CELL_ROWS, 128), f32),
            pltpu.VMEM((chips, 8, 128), f32),
            pltpu.VMEM((chips, 8, 128), f32),
            pltpu.VMEM((subs, chips, CELL_ROWS, 128), f32),
            pltpu.VMEM((subs, 8, 128), f32),
            pltpu.SemaphoreType.DMA((len(arrays),)),
            pltpu.SemaphoreType.DMA((3,)),
            pltpu.SemaphoreType.DMA((3, chips)),
            pltpu.SemaphoreType.DMA((3,)),
            pltpu.SemaphoreType.DMA((6,)),
        ],
        compiler_params=pltpu.CompilerParams(
            collective_id=0,
            has_side_effects=True,
            vmem_limit_bytes=(61 << 20) - 5 * sum(math.prod(shape) for shape in shapes),
        ),
    )(*arrays)


def local(
    positions,
    masses,
    old_accel,
    active,
    parent_of,
    parent_centers,
    local_list,
    near_list,
    far_list,
    send_ids,
    cell_send_ids,
):
    moment_count = len(exponent_rows())
    chip_rows, pool, table, parents, early = exchange(
        positions,
        masses[None],
        send_ids[0].T,
        active,
        local_list.T,
        cell_send_ids[0].T,
        parent_of,
        parent_centers,
        moment_count,
    )
    accel, parents = fields(
        active,
        local_list,
        near_list,
        far_list,
        chip_rows,
        pool.reshape(-1, 4, BUCKET),
        table.reshape(-1, 128),
        parents,
        early,
        old_accel,
    )
    return (accel, parents.T)


def solution(mesh):
    return jax.shard_map(
        local,
        mesh=mesh,
        in_specs=(
            P(None, ("dom", "sub")),
            P(("dom", "sub")),
            P(None, ("dom", "sub")),
            P("dom"),
            P(("dom", "sub")),
            P(),
            P("dom", None),
            P("dom", None),
            P("dom", None),
            P(("dom", "sub"), None, None),
            P(("dom", "sub"), None, None),
        ),
        out_specs=(P(None, ("dom", "sub")), P(None, "dom")),
        check_vma=False,
    )
```

```python
import functools
import math

import jax
import jax.numpy as jnp
import numpy as np
from jax import lax
from jax.experimental import pallas as pl
from jax.experimental.pallas import tpu as pltpu
from jax.sharding import PartitionSpec as P

BUCKET = 256
NB = 32
RQ = 4
RQC = 8


soft_sq = 0.0025
far_sq = 0.25


def exponent_rows():
    listing = []
    for degree in range(5):
        for power_x in range(degree, -1, -1):
            for power_y in range(degree - power_x, -1, -1):
                listing.append((power_x, power_y, degree - power_x - power_y))
    return listing


def multinomial(triple):
    return math.factorial(sum(triple)) / (
        math.factorial(triple[0]) * math.factorial(triple[1]) * math.factorial(triple[2])
    )


def weight_layout():
    triples = exponent_rows()
    position = {triple: number for number, triple in enumerate(triples)}
    weight_table = np.zeros((46, 35))
    s_scale = [1.0, 1.0, 1.5, 2.5, 4.375]
    t_scale = [-0.5, -1.5, -3.75]
    mono_index = []
    radial_index = []
    for number, triple in enumerate(triples):
        weight_table[number, number] = multinomial(triple) * s_scale[sum(triple)]
        mono_index.append(number)
        radial_index.append(sum(triple))
    for number in range(10):
        triple = triples[number]
        for axis_at in range(3):
            raised = list(triple)
            raised[axis_at] += 2
            weight_table[35 + number, position[tuple(raised)]] += (
                multinomial(triple) * t_scale[sum(triple)]
            )
        mono_index.append(number)
        radial_index.append(sum(triple) + 1)
    for axis_one in range(3):
        for axis_two in range(3):
            raised = [0, 0, 0]
            raised[axis_one] += 2
            raised[axis_two] += 2
            weight_table[45, position[tuple(raised)]] += 0.375
    mono_index.append(0)
    radial_index.append(2)
    return (weight_table, mono_index, radial_index)


def monomial_list(comp_x, comp_y, comp_z):
    powers = []
    for component in (comp_x, comp_y, comp_z):
        series = [jnp.ones_like(component)]
        for degree in range(4):
            series.append(series[-1] * component)
        powers.append(series)
    return [
        powers[0][power_x] * powers[1][power_y] * powers[2][power_z]
        for power_x, power_y, power_z in exponent_rows()
    ]


def gradient_table():
    weight_table, _, _ = weight_layout()
    triples = exponent_rows()
    position = {triple: number for number, triple in enumerate(triples)}
    table = np.zeros((128, 38))

    def lowered(numbers, first, base, start, count):
        for offset, number in enumerate(numbers):
            triple = triples[first + offset]
            for axis_at in range(3):
                if triple[axis_at] > 0:
                    less = list(triple)
                    less[axis_at] -= 1
                    column = base + axis_at * count + position[tuple(less)] - start
                    table[column, :35] += triple[axis_at] * weight_table[number]

    lowered(range(20, 35), 20, 0, 10, 10)
    lowered(range(10, 20), 10, 30, 4, 6)
    lowered(range(39, 45), 4, 48, 1, 3)
    lowered(range(4, 10), 4, 57, 1, 3)
    lowered(range(36, 39), 1, 66, 0, 1)
    lowered(range(1, 4), 1, 69, 0, 1)
    table[72, :35] = weight_table[0]
    table[73, :35] = weight_table[35]
    table[74, :35] = weight_table[45]
    for axis_at in range(3):
        table[75 + axis_at, 35 + axis_at] = 1.0
    return table


def split_three(value):
    first = value.astype(jnp.bfloat16).astype(jnp.float32)
    rest = value - first
    second = rest.astype(jnp.bfloat16).astype(jnp.float32)
    return first, second, rest - second


def weighted(columns, base, monomials):
    total = columns[base] * monomials[0]
    for number in range(1, len(monomials)):
        total = total + columns[base + number] * monomials[number]
    return total


def far_group(cells, points):
    columns = [cells[:, number : number + 1] for number in range(78)]
    r = [points[axis_at : axis_at + 1, :] - columns[75 + axis_at] for axis_at in range(3)]
    x, y, z = r
    xx, xy, xz, yy, yz, zz = x * x, x * y, x * z, y * y, y * z, z * z
    rho_sq = xx + yy + zz + far_sq
    inv_rho = lax.rsqrt(rho_sq)
    inv_sq = inv_rho * inv_rho
    radial = [inv_rho]
    for degree in range(5):
        radial.append(radial[-1] * inv_sq)
    quad = [xx, xy, xz, yy, yz, zz]
    cubic = [
        xx * x, xx * y, xx * z, x * yy, x * yz, x * zz, yy * y, yy * z, y * zz, zz * z,
    ]

    def dot(grad):
        return x * grad[0] + y * grad[1] + z * grad[2]

    grad_four = [weighted(columns, 10 * axis_at, cubic) for axis_at in range(3)]
    scalar = (2.25 * radial[5]) * dot(grad_four)
    total = [radial[4] * grad for grad in grad_four]
    grad_three = [weighted(columns, 30 + 6 * axis_at, quad) for axis_at in range(3)]
    grad_two_t = [weighted(columns, 48 + 3 * axis_at, r) for axis_at in range(3)]
    value_three = dot(grad_three) * (1.0 / 3.0) + dot(grad_two_t) * 0.5
    scalar = scalar + (7.0 * radial[4]) * value_three
    total = [
        t + radial[3] * (a + b) for t, a, b in zip(total, grad_three, grad_two_t)
    ]
    grad_two = [weighted(columns, 57 + 3 * axis_at, r) for axis_at in range(3)]
    value_two = dot(grad_two) * 0.5 + dot(columns[66:69]) + columns[74]
    scalar = scalar + (5.0 * radial[3]) * value_two
    total = [
        t + radial[2] * (a + b) for t, a, b in zip(total, grad_two, columns[66:69])
    ]
    value_one = dot(columns[69:72]) + columns[73]
    scalar = scalar + (3.0 * radial[2]) * value_one + radial[1] * columns[72]
    return [t + radial[1] * a - c * scalar for t, a, c in zip(total, columns[69:72], r)]


def split_two(value):
    high = value.astype(jnp.bfloat16).astype(jnp.float32)
    return high, value - high


def near_sum(target, source_of, count):
    row_at = lax.broadcasted_iota(jnp.int32, (8, BUCKET), 0)
    twice = jnp.concatenate([target, target], axis=0)
    middle = jnp.where(row_at % 4 == 3, 0.0, jnp.mean(twice, axis=1, keepdims=True))
    at = twice - middle
    norm = jnp.sum(jnp.where(row_at < 3, at * at, 0.0), axis=0, keepdims=True) + soft_sq
    feature = jnp.where(
        row_at < 3, -2.0 * at, jnp.where(row_at == 3, norm, jnp.where(row_at < 7, 1.0, 0.0))
    )
    one, two, three = split_three(feature)
    lhs = jnp.concatenate([one, two, three, one, two, one], axis=0).astype(jnp.bfloat16)
    running = jnp.zeros((8, BUCKET), jnp.float32)
    for number in range(count):
        source = source_of(number)
        offset = jnp.concatenate([source, source], axis=0) - middle
        feature = jnp.where(row_at < 3, offset, jnp.where(row_at == 3, 1.0, offset * offset))
        one, two, three = split_three(feature)
        rhs = jnp.concatenate([one, one, one, two, two, three], axis=0).astype(jnp.bfloat16)
        carried = jnp.where(row_at % 4 == 3, 1.0, offset) * source[3:4, :]
        high, low = split_two(carried)
        values = jnp.where(row_at < 4, high, low).astype(jnp.bfloat16)
        dist_sq = lax.dot_general(
            rhs, lhs, (((0,), (0,)), ((), ())), preferred_element_type=jnp.float32
        )
        inv = lax.rsqrt(dist_sq)
        weight = inv * inv * inv
        coarse = weight.astype(jnp.bfloat16)
        fine = (weight - coarse.astype(jnp.float32)).astype(jnp.bfloat16)
        for part in (coarse, fine):
            running = running + jnp.dot(values, part, preferred_element_type=jnp.float32)
    summed = running[0:4] + running[4:8]
    return summed[0:3] - at[0:3] * summed[3:4]


def far_sum(target, table_ref, index_of, count, cells):
    for number in range(count):
        cells[pl.ds(number, 1), :] = table_ref[pl.ds(index_of(number), 1), :]
    parts = None
    for group in range(count // 8):
        piece = far_group(cells[8 * group : 8 * group + 8, :], target)
        parts = piece if parts is None else [a + b for a, b in zip(parts, piece)]
    return jnp.concatenate([jnp.sum(part, axis=0, keepdims=True) for part in parts], axis=0)


def field_kernel(
    active_ref, local_ref, near_ref, far_ref, chip_ref, pool_ref, table_ref, early_ref, old_ref,
    mid_ref, away_ref, cells, listed,
):
    my_sub = lax.axis_index("sub")
    subs, chips = lax.axis_size("sub"), lax.axis_size("dom")
    local_count, near_count = local_ref.shape[0], near_ref.shape[0]
    lap_rows = table_ref.shape[0] // PACK
    mid_ref[...] = old_ref[...]
    away_ref[...] = jnp.zeros_like(away_ref)
    buckets = mid_ref.shape[1] // BUCKET
    total_rows = active_ref.shape[0]

    def place(entry, slots):
        device = lax.div(entry, slots)
        return lax.rem(device, subs) * chips + lax.div(device, subs), lax.rem(entry, slots)

    def pool_at(entry):
        where, slot = place(entry, RQ)
        return where * RQ + slot

    def table_at(entry):
        where, slot = place(entry, RQC)
        row = lax.div(slot, PACK)
        return (slot - PACK * row) * lap_rows + where * CELL_ROWS + row

    filled = jnp.int32(0)
    owned = jnp.int32(0)
    for step in range(total_rows):
        row = shared_row(step, total_rows)
        listed[filled] = row
        filled = filled + jnp.where(active_ref[row] > 0, 1, 0)
        if step == buckets - 1:
            owned = filled
    mine = lax.div(filled + 1 - my_sub, 2)

    def visit(item, carry):
        row = listed[item]

        def put(near):
            far = far_sum(
                chip_ref[row],
                table_ref,
                lambda number: table_at(far_ref[number, row]),
                far_ref.shape[0],
                cells,
            )
            total = near + far

            @pl.when(item < owned)
            def _():
                bucket = row - my_sub * buckets
                mid_ref[:, pl.ds(pl.multiple_of(bucket * BUCKET, BUCKET), BUCKET)] = total

            @pl.when(item >= owned)
            def _():
                away_ref[item - owned, 0:3] = total

        def near_source(number):
            return pool_ref[pool_at(near_ref[number, row])]

        def any_source(number):
            if number < near_count:
                return near_source(number)
            return chip_ref[local_ref[number - near_count, row]]

        @pl.when(item < early_ref.shape[0])
        def _():
            put(near_sum(chip_ref[row], near_source, near_count) + early_ref[item][0:3])

        @pl.when(item >= early_ref.shape[0])
        def _():
            put(near_sum(chip_ref[row], any_source, local_count + near_count))

        return carry

    lax.fori_loop(0, mine, visit, 0)


def fields(active, local_list, near_list, far_list, chip_rows, pool_rows, table, early, old_accel):
    smem = pl.BlockSpec(memory_space=pltpu.SMEM)
    vmem = pl.BlockSpec(memory_space=pltpu.VMEM)
    f32 = jnp.float32
    return pl.pallas_call(
        field_kernel,
        out_shape=[
            pltpu.VMEM(old_accel.shape, f32),
            pltpu.VMEM((NB // 4, 4, BUCKET), f32),
        ],
        in_specs=[smem] * 4 + [vmem] * 5,
        out_specs=[vmem] * 2,
        scratch_shapes=[
            pltpu.VMEM((far_list.shape[0], 128), f32),
            pltpu.SMEM((active.shape[0] + 1,), jnp.int32),
        ],
        compiler_params=pltpu.CompilerParams(vmem_limit_bytes=VMEM_BYTES),
    )(active, local_list, near_list, far_list, chip_rows, pool_rows, table, early, old_accel)


def return_kernel(away_ref, home_ref, sems):
    mesh_ids = pl.DeviceIdType.MESH
    sibling = (lax.axis_index("dom"), lax.rem(lax.axis_index("sub") + 1, lax.axis_size("sub")))
    barrier = pltpu.get_barrier_semaphore()
    pl.semaphore_signal(barrier, inc=1, device_id=sibling, device_id_type=mesh_ids)
    pl.semaphore_wait(barrier, 1)
    copy = pltpu.make_async_remote_copy(
        src_ref=away_ref, dst_ref=home_ref, send_sem=sems.at[0], recv_sem=sems.at[1],
        device_id=sibling, device_id_type=mesh_ids,
    )
    copy.start()
    copy.wait()


def bring_back(away):
    vmem = pl.BlockSpec(memory_space=pltpu.VMEM)
    return pl.pallas_call(
        return_kernel,
        out_shape=pltpu.VMEM(away.shape, jnp.float32),
        in_specs=[vmem],
        out_specs=vmem,
        scratch_shapes=[pltpu.SemaphoreType.DMA((2,))],
        compiler_params=pltpu.CompilerParams(
            collective_id=1, has_side_effects=True, vmem_limit_bytes=VMEM_BYTES
        ),
    )(away)


def merge_kernel(active_ref, home_ref, mid_ref, parent_ref, out_ref, parent_out_ref):
    my_sub = lax.axis_index("sub")
    buckets = mid_ref.shape[1] // BUCKET
    parent_out_ref[...] = parent_ref[...]
    owned = jnp.int32(0)
    others = jnp.int32(0)
    ranks = []
    for bucket in range(buckets):
        mark = jnp.where(active_ref[my_sub * buckets + bucket] > 0, 1, 0)
        ranks.append((owned, mark))
        owned = owned + mark
        others = others + jnp.where(active_ref[(1 - my_sub) * buckets + bucket] > 0, 1, 0)
    helped = lax.div(owned + others + my_sub, 2) - others
    for bucket in range(buckets):
        rank, mark = ranks[bucket]
        slot = jnp.where(my_sub == 0, owned - 1 - rank, rank)
        theirs = (mark > 0) & (slot < helped)
        lanes = pl.ds(bucket * BUCKET, BUCKET)
        got = home_ref[jnp.clip(slot, 0, home_ref.shape[0] - 1)]
        out_ref[:, lanes] = jnp.where(theirs, got[0:3], mid_ref[:, lanes])


def merge(active, home, mid, parents):
    smem = pl.BlockSpec(memory_space=pltpu.SMEM)
    vmem = pl.BlockSpec(memory_space=pltpu.VMEM)
    return pl.pallas_call(
        merge_kernel,
        out_shape=[jax.ShapeDtypeStruct(array.shape, jnp.float32) for array in (mid, parents)],
        in_specs=[smem] + [vmem] * 3,
        out_specs=[vmem] * 2,
        compiler_params=pltpu.CompilerParams(vmem_limit_bytes=VMEM_BYTES),
    )(active, home, mid, parents)


PACK = 3
WIDTH = 40
CELL_ROWS = 4
ITEMS = 8
IDLE = 3
VMEM_BYTES = 24 << 20


def packed_columns(columns, rows):
    lane_at = lax.broadcasted_iota(jnp.int32, (rows, 128), 1)
    result = jnp.zeros((rows, 128), jnp.float32)
    for number, column in enumerate(columns):
        result = jnp.where(lane_at == number, column, result)
    return result


def moment_columns(comp, centers):
    monomials = monomial_list(
        comp[0] - centers[0], comp[1] - centers[1], comp[2] - centers[2]
    )
    return [jnp.sum(comp[3] * monomial, axis=1, keepdims=True) for monomial in monomials]


def shared_row(place, total):
    my_sub = lax.axis_index("sub")
    return place + my_sub * (total - 1 - 2 * place)


def exchange_kernel(
    positions_hbm, masses_hbm, send_hbm, active_hbm, local_hbm, cell_send_hbm, parent_of_hbm,
    parent_centers_hbm, expand_hbm, near_hbm, far_hbm, old_hbm,
    chip_ref, pool_ref, table_ref, parent_ref, early_ref,
    active_out, local_out, near_out, far_out, old_out,
    positions_ref, masses_ref, send_ref, active_ref, local_ref, cell_send_ref, parent_of_ref,
    parent_centers_ref, expand_ref,
    rows, blocks, comp, spread, one_hot, pick, cell_out, term_out, term_in, cell_in, halves,
    load_sem, send_sem, recv_sem, near_sem, far_sem,
):
    subs = lax.axis_size("sub")
    my_dom = lax.axis_index("dom")
    my_sub = lax.axis_index("sub")
    chips = lax.axis_size("dom")
    count = rows.shape[0]
    items = early_ref.shape[0]
    parents = parent_ref.shape[0]
    deep = -(-parents // PACK)
    barrier = pltpu.get_barrier_semaphore()
    mesh_ids = pl.DeviceIdType.MESH
    sibling = (my_dom, lax.rem(my_sub + 1, subs))

    def chip_at(step):
        return lax.rem(my_dom + step, chips)

    def greet(step, carry):
        pl.semaphore_signal(
            barrier, inc=1, device_id=(chip_at(step), my_sub), device_id_type=mesh_ids
        )
        return carry

    loads = [
        pltpu.make_async_copy(source, sink, load_sem.at[number])
        for number, (source, sink) in enumerate(
            (
                (positions_hbm, positions_ref),
                (masses_hbm, masses_ref),
                (send_hbm, send_ref),
                (active_hbm, active_ref),
                (local_hbm, local_ref),
                (cell_send_hbm, cell_send_ref),
                (parent_of_hbm, parent_of_ref),
                (parent_centers_hbm, parent_centers_ref),
                (expand_hbm, expand_ref),
                (active_hbm, active_out),
                (local_hbm, local_out),
                (near_hbm, near_out),
                (far_hbm, far_out),
                (old_hbm, old_out),
            )
        )
    ]
    for load in loads:
        load.start()
    pl.semaphore_signal(barrier, inc=1, device_id=sibling, device_id_type=mesh_ids)
    lax.fori_loop(1, chips, greet, 0)
    for load in loads[:3]:
        load.wait()

    for bucket in range(count):
        lanes = pl.ds(bucket * BUCKET, BUCKET)
        tile = jnp.concatenate([positions_ref[:, lanes], masses_ref[:, lanes]], axis=0)
        rows[bucket] = tile
        for axis_at in range(4):
            comp[axis_at, pl.ds(bucket, 1), :] = tile[axis_at : axis_at + 1, :]

    def gather(chip, carry):
        for slot in range(RQ):
            blocks[chip, slot] = rows[jnp.maximum(send_ref[slot, chip], 0)]
        return carry

    lax.fori_loop(0, chips, gather, 0)

    outgoing = ((term_out, term_in), (cell_out, cell_in.at[my_sub]), (blocks, pool_ref.at[my_sub]))

    sizes = (deep, -(-RQC // PACK), RQ)

    def turn(place):
        return lax.rem(place + chips // 2 - 1, chips - 1) + 1

    def part(ref, number):
        return ref.at[pl.ds(0, sizes[number])]

    def copy_to(number, step):
        source, sink = outgoing[number]
        to_dom = chip_at(step)
        return pltpu.make_async_remote_copy(
            src_ref=part(source.at[to_dom], number), dst_ref=part(sink.at[my_dom], number),
            send_sem=send_sem.at[number], recv_sem=recv_sem.at[number, step],
            device_id=(to_dom, my_sub), device_id_type=mesh_ids,
        )

    def send(number, first, last):
        def one(place, carry):
            copy_to(number, turn(place)).start()
            return carry

        lax.fori_loop(first, last, one, 0)

    def keep(number):
        source, sink = outgoing[number]
        pltpu.make_async_copy(
            part(source.at[my_dom], number), part(sink.at[my_dom], number), recv_sem.at[number, 0]
        ).start()

    def arrived(number, step):
        sink = part(outgoing[number][1].at[lax.rem(my_dom + chips - step, chips)], number)
        pltpu.make_async_copy(sink, sink, recv_sem.at[number, step]).wait()

    def forward(number, step):
        piece = part(outgoing[number][1].at[lax.rem(my_dom + chips - step, chips)], number)
        return pltpu.make_async_remote_copy(
            src_ref=piece, dst_ref=piece,
            send_sem=far_sem.at[2 * number], recv_sem=far_sem.at[2 * number + 1],
            device_id=sibling, device_id_type=mesh_ids,
        )

    def relay(number, first, last):
        def one(place, carry):
            step = turn(place)
            arrived(number, step)
            forward(number, step).start()
            return carry

        lax.fori_loop(first, last, one, 0)

    def relay_own(number):
        arrived(number, 0)
        forward(number, 0).start()

    def settle(ref, sem):
        pltpu.make_async_copy(ref, ref, sem).wait()

    pl.semaphore_wait(barrier, chips + subs - 2)
    own_rows = chip_ref.at[pl.ds(my_sub * count, count)]
    twin = pltpu.make_async_remote_copy(
        src_ref=rows, dst_ref=own_rows, send_sem=near_sem.at[0], recv_sem=near_sem.at[1],
        device_id=sibling, device_id_type=mesh_ids,
    )
    twin.start()
    send(2, 0, chips // 2)
    mine = pltpu.make_async_copy(rows, own_rows, near_sem.at[2])
    mine.start()
    keep(2)
    for load in loads[3:]:
        load.wait()

    values = [comp[axis_at] for axis_at in range(4)]
    centers = [jnp.mean(values[axis_at], axis=1, keepdims=True) for axis_at in range(3)]
    cells = packed_columns(moment_columns(values, centers) + centers, count)
    for lap in range(PACK):
        spread[lap] = cells if lap == 0 else pltpu.roll(cells, WIDTH * lap, 1)

    def gather_cells(chip, carry):
        for row in range(cell_out.shape[1]):
            total = None
            for lap in range(PACK):
                slot = PACK * row + lap
                if slot < RQC:
                    piece = spread[lap, pl.ds(jnp.maximum(cell_send_ref[slot, chip], 0), 1), :]
                    total = piece if total is None else total + piece
            if total is None:
                total = jnp.zeros((1, 128), jnp.float32)
            cell_out[chip, pl.ds(row, 1), :] = total
        return carry

    lax.fori_loop(0, chips, gather_cells, 0)

    wide = lax.broadcasted_iota(jnp.int32, (1, one_hot.shape[1]), 1)
    lane = lax.broadcasted_iota(jnp.int32, (1, pick.shape[2]), 1)
    chip_of, deep_of = lane // 8, lane % 8
    for bucket in range(count):
        owner = parent_of_ref[bucket]
        one_hot[pl.ds(bucket, 1), :] = jnp.where(wide == owner, 1.0, 0.0)
        for lap in range(PACK):
            within = deep_of + deep * lap
            named = (deep_of < deep) & (within < parents) & (chip_of * parents + within == owner)
            pick[lap, pl.ds(bucket, 1), :] = jnp.where(named, 1.0, 0.0)
    centers_of = lax.dot_general(
        one_hot[...], parent_centers_ref[...], (((1,), (1,)), ((), ())),
        precision=lax.Precision.HIGHEST, preferred_element_type=jnp.float32,
    )
    terms = packed_columns(
        moment_columns(values, [centers_of[:, axis_at : axis_at + 1] for axis_at in range(3)]), count
    )
    sums = None
    for lap in range(PACK):
        piece = lax.dot_general(
            pick[lap], terms if lap == 0 else pltpu.roll(terms, WIDTH * lap, 1),
            (((0,), (0,)), ((), ())),
            precision=lax.Precision.HIGHEST, preferred_element_type=jnp.float32,
        )
        sums = piece if sums is None else sums + piece
    term_out[...] = sums.reshape(term_out.shape)
    send(1, 0, chips - 1)
    keep(1)
    send(2, chips // 2, chips - 1)
    send(0, 0, chips - 1)
    keep(0)
    relay_own(2)
    twin.wait()
    mine.wait()

    total_rows = subs * count

    def early(item, last):
        found = total_rows
        for place in range(total_rows - 1, -1, -1):
            fits = (active_ref[shared_row(place, total_rows)] > 0) & (place > last)
            found = jnp.where(fits, place, found)
        row = shared_row(jnp.minimum(found, total_rows - 1), total_rows)
        total = near_sum(
            chip_ref[row], lambda number: chip_ref[local_ref[number, row]], local_ref.shape[0]
        )
        early_ref[item] = jnp.concatenate([total, jnp.zeros((1, BUCKET), jnp.float32)], axis=0)
        share = -(-(chips - 1) // (items - IDLE))

        @pl.when(item >= IDLE)
        def _():
            first = (item - IDLE) * share
            relay(2, first, jnp.minimum(first + share, chips - 1))

        @pl.when(item == items - 2)
        def _():
            lax.fori_loop(0, chips, lambda step, carry: (arrived(0, step), carry)[1], 0)
            halves[my_sub] = jnp.sum(term_in[:, 0:deep], axis=0)
            relay_own(1)
            relay(1, 0, chips - 1)

        return found

    lax.fori_loop(0, items, early, -1)
    swap = pltpu.make_async_remote_copy(
        src_ref=halves.at[my_sub], dst_ref=halves.at[my_sub],
        send_sem=far_sem.at[0], recv_sem=far_sem.at[1],
        device_id=sibling, device_id_type=mesh_ids,
    )
    swap.start()
    relayed = cell_in.at[0, :, pl.ds(0, sizes[1])]
    settle(relayed, far_sem.at[2])
    settle(relayed, far_sem.at[3])
    packed = cell_in[...].reshape(-1, 128)
    for lap in range(PACK):
        table_ref[lap] = jnp.dot(
            packed, expand_ref[lap], precision=lax.Precision.HIGHEST, preferred_element_type=jnp.float32
        )
    settle(halves.at[0], far_sem.at[0])
    settle(halves.at[0], far_sem.at[1])
    total = halves[0]
    for sub in range(1, halves.shape[0]):
        total = total + halves[sub]
    for lap in range(PACK):
        size = min(deep, parents - lap * deep)
        turned = total if lap == 0 else pltpu.roll(total, 128 - WIDTH * lap, 1)
        parent_ref[lap * deep : lap * deep + size, :] = turned[:size, : parent_ref.shape[1]]
    settle(pool_ref.at[0], far_sem.at[4])
    settle(pool_ref.at[0], far_sem.at[5])
    for number, (source, sink) in enumerate(outgoing):
        settle(source.at[pl.ds(0, chips - 1), pl.ds(0, sizes[number])], send_sem.at[number])


def exchange(
    positions, masses, send_ids, active, local_list, cell_send_ids, parent_of, parent_centers,
    near_list, far_list, old_accel, moment_count,
):
    subs = lax.axis_size("sub")
    chips = lax.axis_size("dom")
    parent_total = parent_centers.shape[1]
    parents = parent_total // chips
    table = gradient_table()
    expand = np.zeros((PACK, 128, 128))
    for lap in range(PACK):
        expand[lap, WIDTH * lap : WIDTH * lap + 38] = table[:, :38].T
    f32 = jnp.float32
    arrays = (
        positions, masses, send_ids, active, local_list, cell_send_ids, parent_of, parent_centers,
        jnp.asarray(expand, f32),
    )
    handed = (active, local_list, near_list, far_list, old_accel)
    results = [
        pltpu.VMEM(shape, f32)
        for shape in (
            (subs * NB, 4, BUCKET),
            (subs, chips, RQ, 4, BUCKET),
            (PACK, subs * chips * CELL_ROWS, 128),
            (parents, moment_count),
            (ITEMS, 4, BUCKET),
        )
    ] + [pltpu.VMEM(array.shape, array.dtype) for array in handed]
    spaces = (pltpu.VMEM,) * 2 + (pltpu.SMEM,) * 5 + (pltpu.VMEM,) * 2
    return pl.pallas_call(
        exchange_kernel,
        out_shape=results,
        in_specs=[pl.BlockSpec(memory_space=pltpu.HBM)] * (len(arrays) + 3),
        out_specs=[pl.BlockSpec(memory_space=pltpu.VMEM)] * len(results),
        scratch_shapes=[space(array.shape, array.dtype) for space, array in zip(spaces, arrays)]
        + [
            pltpu.VMEM((NB, 4, BUCKET), f32),
            pltpu.VMEM((chips, RQ, 4, BUCKET), f32),
            pltpu.VMEM((4, NB, BUCKET), f32),
            pltpu.VMEM((PACK, NB, 128), f32),
            pltpu.VMEM((NB, parent_total), f32),
            pltpu.VMEM((PACK, NB, chips * 8), f32),
            pltpu.VMEM((chips, CELL_ROWS, 128), f32),
            pltpu.VMEM((chips, 8, 128), f32),
            pltpu.VMEM((chips, 8, 128), f32),
            pltpu.VMEM((subs, chips, CELL_ROWS, 128), f32),
            pltpu.VMEM((subs, -(-parents // PACK), 128), f32),
            pltpu.SemaphoreType.DMA((len(arrays) + len(handed),)),
            pltpu.SemaphoreType.DMA((3,)),
            pltpu.SemaphoreType.DMA((3, chips)),
            pltpu.SemaphoreType.DMA((3,)),
            pltpu.SemaphoreType.DMA((6,)),
        ],
        compiler_params=pltpu.CompilerParams(
            collective_id=0,
            has_side_effects=True,
            vmem_limit_bytes=(60 << 20) - 5 * sum(math.prod(result.shape) for result in results),
        ),
    )(*arrays, *handed[2:])


def local(
    positions,
    masses,
    old_accel,
    active,
    parent_of,
    parent_centers,
    local_list,
    near_list,
    far_list,
    send_ids,
    cell_send_ids,
):
    moment_count = len(exponent_rows())
    chip_rows, pool, table, parents, early, *handed = exchange(
        positions,
        masses[None],
        send_ids[0].T,
        active,
        local_list.T,
        cell_send_ids[0].T,
        parent_of,
        parent_centers,
        near_list.T,
        far_list.T,
        old_accel,
        moment_count,
    )
    mid, away = fields(
        *handed[:4],
        chip_rows,
        pool.reshape(-1, 4, BUCKET),
        table.reshape(-1, 128),
        early,
        handed[4],
    )
    accel, parents = merge(handed[0], bring_back(away), mid, parents)
    return (accel, parents.T)


def solution(mesh):
    return jax.shard_map(
        local,
        mesh=mesh,
        in_specs=(
            P(None, ("dom", "sub")),
            P(("dom", "sub")),
            P(None, ("dom", "sub")),
            P("dom"),
            P(("dom", "sub")),
            P(),
            P("dom", None),
            P("dom", None),
            P("dom", None),
            P(("dom", "sub"), None, None),
            P(("dom", "sub"), None, None),
        ),
        out_specs=(P(None, ("dom", "sub")), P(None, "dom")),
        check_vma=False,
    )
```

```python
import functools
import math

import jax
import jax.numpy as jnp
import numpy as np
from jax import lax
from jax.experimental import pallas as pl
from jax.experimental.pallas import tpu as pltpu
from jax.sharding import PartitionSpec as P

BUCKET = 256
NB = 32
RQ = 4
RQC = 8


soft_sq = 0.0025
far_sq = 0.25


def exponent_rows():
    listing = []
    for degree in range(5):
        for power_x in range(degree, -1, -1):
            for power_y in range(degree - power_x, -1, -1):
                listing.append((power_x, power_y, degree - power_x - power_y))
    return listing


def multinomial(triple):
    return math.factorial(sum(triple)) / (
        math.factorial(triple[0]) * math.factorial(triple[1]) * math.factorial(triple[2])
    )


def weight_layout():
    triples = exponent_rows()
    position = {triple: number for number, triple in enumerate(triples)}
    weight_table = np.zeros((46, 35))
    s_scale = [1.0, 1.0, 1.5, 2.5, 4.375]
    t_scale = [-0.5, -1.5, -3.75]
    mono_index = []
    radial_index = []
    for number, triple in enumerate(triples):
        weight_table[number, number] = multinomial(triple) * s_scale[sum(triple)]
        mono_index.append(number)
        radial_index.append(sum(triple))
    for number in range(10):
        triple = triples[number]
        for axis_at in range(3):
            raised = list(triple)
            raised[axis_at] += 2
            weight_table[35 + number, position[tuple(raised)]] += (
                multinomial(triple) * t_scale[sum(triple)]
            )
        mono_index.append(number)
        radial_index.append(sum(triple) + 1)
    for axis_one in range(3):
        for axis_two in range(3):
            raised = [0, 0, 0]
            raised[axis_one] += 2
            raised[axis_two] += 2
            weight_table[45, position[tuple(raised)]] += 0.375
    mono_index.append(0)
    radial_index.append(2)
    return (weight_table, mono_index, radial_index)


def monomial_list(comp_x, comp_y, comp_z):
    powers = []
    for component in (comp_x, comp_y, comp_z):
        series = [jnp.ones_like(component)]
        for degree in range(4):
            series.append(series[-1] * component)
        powers.append(series)
    return [
        powers[0][power_x] * powers[1][power_y] * powers[2][power_z]
        for power_x, power_y, power_z in exponent_rows()
    ]


def gradient_table():
    weight_table, _, _ = weight_layout()
    triples = exponent_rows()
    position = {triple: number for number, triple in enumerate(triples)}
    table = np.zeros((128, 38))

    def lowered(numbers, first, base, start, count):
        for offset, number in enumerate(numbers):
            triple = triples[first + offset]
            for axis_at in range(3):
                if triple[axis_at] > 0:
                    less = list(triple)
                    less[axis_at] -= 1
                    column = base + axis_at * count + position[tuple(less)] - start
                    table[column, :35] += triple[axis_at] * weight_table[number]

    lowered(range(20, 35), 20, 0, 10, 10)
    lowered(range(10, 20), 10, 30, 4, 6)
    lowered(range(39, 45), 4, 48, 1, 3)
    lowered(range(4, 10), 4, 57, 1, 3)
    lowered(range(36, 39), 1, 66, 0, 1)
    lowered(range(1, 4), 1, 69, 0, 1)
    table[72, :35] = weight_table[0]
    table[73, :35] = weight_table[35]
    table[74, :35] = weight_table[45]
    for axis_at in range(3):
        table[75 + axis_at, 35 + axis_at] = 1.0
    return table


def split_three(value):
    first = value.astype(jnp.bfloat16).astype(jnp.float32)
    rest = value - first
    second = rest.astype(jnp.bfloat16).astype(jnp.float32)
    return first, second, rest - second


def weighted(columns, base, monomials):
    total = columns[base] * monomials[0]
    for number in range(1, len(monomials)):
        total = total + columns[base + number] * monomials[number]
    return total


def far_group(cells, points):
    columns = [cells[:, number : number + 1] for number in range(78)]
    r = [points[axis_at : axis_at + 1, :] - columns[75 + axis_at] for axis_at in range(3)]
    x, y, z = r
    xx, xy, xz, yy, yz, zz = x * x, x * y, x * z, y * y, y * z, z * z
    rho_sq = xx + yy + zz + far_sq
    inv_rho = lax.rsqrt(rho_sq)
    inv_sq = inv_rho * inv_rho
    radial = [inv_rho]
    for degree in range(5):
        radial.append(radial[-1] * inv_sq)
    quad = [xx, xy, xz, yy, yz, zz]
    cubic = [
        xx * x, xx * y, xx * z, x * yy, x * yz, x * zz, yy * y, yy * z, y * zz, zz * z,
    ]

    def dot(grad):
        return x * grad[0] + y * grad[1] + z * grad[2]

    grad_four = [weighted(columns, 10 * axis_at, cubic) for axis_at in range(3)]
    scalar = (2.25 * radial[5]) * dot(grad_four)
    total = [radial[4] * grad for grad in grad_four]
    grad_three = [weighted(columns, 30 + 6 * axis_at, quad) for axis_at in range(3)]
    grad_two_t = [weighted(columns, 48 + 3 * axis_at, r) for axis_at in range(3)]
    value_three = dot(grad_three) * (1.0 / 3.0) + dot(grad_two_t) * 0.5
    scalar = scalar + (7.0 * radial[4]) * value_three
    total = [
        t + radial[3] * (a + b) for t, a, b in zip(total, grad_three, grad_two_t)
    ]
    grad_two = [weighted(columns, 57 + 3 * axis_at, r) for axis_at in range(3)]
    value_two = dot(grad_two) * 0.5 + dot(columns[66:69]) + columns[74]
    scalar = scalar + (5.0 * radial[3]) * value_two
    total = [
        t + radial[2] * (a + b) for t, a, b in zip(total, grad_two, columns[66:69])
    ]
    value_one = dot(columns[69:72]) + columns[73]
    scalar = scalar + (3.0 * radial[2]) * value_one + radial[1] * columns[72]
    return [t + radial[1] * a - c * scalar for t, a, c in zip(total, columns[69:72], r)]


def split_two(value):
    high = value.astype(jnp.bfloat16).astype(jnp.float32)
    return high, value - high


def near_sum(target, source_of, count):
    row_at = lax.broadcasted_iota(jnp.int32, (8, BUCKET), 0)
    twice = jnp.concatenate([target, target], axis=0)
    middle = jnp.where(row_at % 4 == 3, 0.0, jnp.mean(twice, axis=1, keepdims=True))
    at = twice - middle
    norm = jnp.sum(jnp.where(row_at < 3, at * at, 0.0), axis=0, keepdims=True) + soft_sq
    feature = jnp.where(
        row_at < 3, -2.0 * at, jnp.where(row_at == 3, norm, jnp.where(row_at < 7, 1.0, 0.0))
    )
    one, two, three = split_three(feature)
    lhs = jnp.concatenate([one, two, three, one, two, one], axis=0).astype(jnp.bfloat16)
    running = jnp.zeros((8, BUCKET), jnp.float32)
    for number in range(count):
        source = source_of(number)
        offset = jnp.concatenate([source, source], axis=0) - middle
        feature = jnp.where(row_at < 3, offset, jnp.where(row_at == 3, 1.0, offset * offset))
        one, two, three = split_three(feature)
        rhs = jnp.concatenate([one, one, one, two, two, three], axis=0).astype(jnp.bfloat16)
        carried = jnp.where(row_at % 4 == 3, 1.0, offset) * source[3:4, :]
        high, low = split_two(carried)
        values = jnp.where(row_at < 4, high, low).astype(jnp.bfloat16)
        dist_sq = lax.dot_general(
            rhs, lhs, (((0,), (0,)), ((), ())), preferred_element_type=jnp.float32
        )
        inv = lax.rsqrt(dist_sq)
        weight = inv * inv * inv
        coarse = weight.astype(jnp.bfloat16)
        fine = (weight - coarse.astype(jnp.float32)).astype(jnp.bfloat16)
        for part in (coarse, fine):
            running = running + jnp.dot(values, part, preferred_element_type=jnp.float32)
    summed = running[0:4] + running[4:8]
    return summed[0:3] - at[0:3] * summed[3:4]


def far_sum(target, table_ref, index_of, count, cells):
    for number in range(count):
        cells[pl.ds(number, 1), :] = table_ref[pl.ds(index_of(number), 1), :]
    parts = None
    for group in range(count // 8):
        piece = far_group(cells[8 * group : 8 * group + 8, :], target)
        parts = piece if parts is None else [a + b for a, b in zip(parts, piece)]
    return jnp.concatenate([jnp.sum(part, axis=0, keepdims=True) for part in parts], axis=0)


def field_kernel(
    active_ref, local_ref, near_ref, far_ref, chip_ref, pool_ref, table_ref, early_ref,
    result_ref, cells, listed,
):
    my_sub = lax.axis_index("sub")
    subs, chips = lax.axis_size("sub"), lax.axis_size("dom")
    local_count, near_count = local_ref.shape[0], near_ref.shape[0]
    lap_rows = table_ref.shape[0] // PACK
    total_rows = active_ref.shape[0]
    buckets = total_rows // subs
    result_ref[buckets:] = jnp.zeros((result_ref.shape[0] - buckets, 4, BUCKET), jnp.float32)

    def place(entry, slots):
        device = lax.div(entry, slots)
        return lax.rem(device, subs) * chips + lax.div(device, subs), lax.rem(entry, slots)

    def pool_at(entry):
        where, slot = place(entry, RQ)
        return where * RQ + slot

    def table_at(entry):
        where, slot = place(entry, RQC)
        row = lax.div(slot, PACK)
        return (slot - PACK * row) * lap_rows + where * CELL_ROWS + row

    filled = jnp.int32(0)
    owned = jnp.int32(0)
    for step in range(total_rows):
        row = shared_row(step, total_rows)
        listed[filled] = row
        filled = filled + jnp.where(active_ref[row] > 0, 1, 0)
        if step == buckets - 1:
            owned = filled
    mine = lax.div(filled + 1 - my_sub, 2)

    def solve(item, started):
        row = listed[item]
        target = chip_ref[row]

        def source_of(number):
            if number < near_count:
                return pool_ref[pool_at(near_ref[number, row])]
            return chip_ref[local_ref[number - near_count, row]]

        near = near_sum(target, source_of, near_count if started else near_count + local_count)
        if started:
            near = near + early_ref[item][0:3]
        far = far_sum(
            target, table_ref, lambda number: table_at(far_ref[number, row]), far_ref.shape[0], cells
        )
        slot = jnp.where(item < owned, row - my_sub * buckets, buckets + item - owned)
        result_ref[slot, 0:3] = near + far

    def phase(begin, end, started):
        groups = lax.div(end - begin, GROUP)

        def group(number, carry):
            for lane in range(GROUP):
                solve(begin + GROUP * number + lane, started)
            return carry

        lax.fori_loop(0, groups, group, 0)
        done = begin + GROUP * groups
        size = GROUP // 2
        while size:
            fits = end - done >= size

            @pl.when(fits)
            def _():
                for lane in range(size):
                    solve(done + lane, started)

            done = done + jnp.where(fits, size, 0)
            size //= 2

    split = jnp.minimum(mine, early_ref.shape[0])
    phase(jnp.int32(0), split, True)
    phase(split, mine, False)


def fields(active, local_list, near_list, far_list, chip_rows, pool_rows, table, early):
    smem = pl.BlockSpec(memory_space=pltpu.SMEM)
    vmem = pl.BlockSpec(memory_space=pltpu.VMEM)
    f32 = jnp.float32
    return pl.pallas_call(
        field_kernel,
        out_shape=pltpu.VMEM((NB + NB // 4, 4, BUCKET), f32),
        in_specs=[smem] * 4 + [vmem] * 4,
        out_specs=vmem,
        scratch_shapes=[
            pltpu.VMEM((far_list.shape[0], 128), f32),
            pltpu.SMEM((active.shape[0] + 1,), jnp.int32),
        ],
        compiler_params=pltpu.CompilerParams(
            vmem_limit_bytes=VMEM_BYTES
        ),
    )(active, local_list, near_list, far_list, chip_rows, pool_rows, table, early)


def return_kernel(result_ref, home_ref, sems):
    mesh_ids = pl.DeviceIdType.MESH
    sibling = (lax.axis_index("dom"), lax.rem(lax.axis_index("sub") + 1, lax.axis_size("sub")))
    barrier = pltpu.get_barrier_semaphore()
    pl.semaphore_signal(barrier, inc=1, device_id=sibling, device_id_type=mesh_ids)
    pl.semaphore_wait(barrier, 1)
    copy = pltpu.make_async_remote_copy(
        src_ref=result_ref.at[pl.ds(NB, NB // 4)], dst_ref=home_ref, send_sem=sems.at[0], recv_sem=sems.at[1],
        device_id=sibling, device_id_type=mesh_ids,
    )
    copy.start()
    copy.wait()


def bring_back(result):
    vmem = pl.BlockSpec(memory_space=pltpu.VMEM)
    return pl.pallas_call(
        return_kernel,
        out_shape=pltpu.VMEM((NB // 4, 4, BUCKET), jnp.float32),
        in_specs=[vmem],
        out_specs=vmem,
        scratch_shapes=[pltpu.SemaphoreType.DMA((2,))],
        compiler_params=pltpu.CompilerParams(
            collective_id=1, has_side_effects=True, vmem_limit_bytes=VMEM_BYTES
        ),
    )(result)


def merge_kernel(
    active_ref, home_ref, result_ref, old_ref, parent_ref, out_ref, parent_out_ref
):
    my_sub = lax.axis_index("sub")
    buckets = old_ref.shape[1] // BUCKET
    parent_out_ref[...] = parent_ref[...]
    owned = jnp.int32(0)
    others = jnp.int32(0)
    ranks = []
    for bucket in range(buckets):
        mark = jnp.where(active_ref[my_sub * buckets + bucket] > 0, 1, 0)
        ranks.append((owned, mark))
        owned = owned + mark
        others = others + jnp.where(active_ref[(1 - my_sub) * buckets + bucket] > 0, 1, 0)
    helped = lax.div(owned + others + my_sub, 2) - others
    for bucket in range(buckets):
        rank, mark = ranks[bucket]
        slot = jnp.where(my_sub == 0, owned - 1 - rank, rank)
        lanes = pl.ds(bucket * BUCKET, BUCKET)
        got = home_ref[jnp.clip(slot, 0, home_ref.shape[0] - 1)]
        fresh = jnp.where(slot < helped, got[0:3], result_ref[bucket][0:3])
        out_ref[:, lanes] = jnp.where(mark > 0, fresh, old_ref[:, lanes])


def merge(active, home, result, old_accel, parents):
    smem = pl.BlockSpec(memory_space=pltpu.SMEM)
    vmem = pl.BlockSpec(memory_space=pltpu.VMEM)
    return pl.pallas_call(
        merge_kernel,
        out_shape=[jax.ShapeDtypeStruct(array.shape, jnp.float32) for array in (old_accel, parents)],
        in_specs=[smem] + [vmem] * 4,
        out_specs=[vmem] * 2,
        compiler_params=pltpu.CompilerParams(vmem_limit_bytes=VMEM_BYTES),
    )(active, home, result, old_accel, parents)


PACK = 3
GROUP = 4
WIDTH = 40
CELL_ROWS = 4
ITEMS = 12
IDLE = 3
VMEM_BYTES = 24 << 20


def packed_columns(columns, rows):
    lane_at = lax.broadcasted_iota(jnp.int32, (rows, 128), 1)
    result = jnp.zeros((rows, 128), jnp.float32)
    for number, column in enumerate(columns):
        result = jnp.where(lane_at == number, column, result)
    return result


def moment_columns(comp, centers):
    monomials = monomial_list(
        comp[0] - centers[0], comp[1] - centers[1], comp[2] - centers[2]
    )
    return [jnp.sum(comp[3] * monomial, axis=1, keepdims=True) for monomial in monomials]


def shared_row(place, total):
    my_sub = lax.axis_index("sub")
    return place + my_sub * (total - 1 - 2 * place)


def exchange_kernel(
    positions_hbm, masses_hbm, send_hbm, active_hbm, local_hbm, cell_send_hbm, parent_of_hbm,
    parent_centers_hbm, expand_hbm, near_hbm, far_hbm, old_hbm,
    chip_ref, pool_ref, table_ref, parent_ref, early_ref,
    active_out, local_out, near_out, far_out, old_out,
    positions_ref, masses_ref, send_ref, active_ref, local_ref, cell_send_ref, parent_of_ref,
    parent_centers_ref, expand_ref,
    rows, blocks, comp, spread, one_hot, pick, cell_out, term_out, term_in, cell_in, halves,
    load_sem, send_sem, recv_sem, near_sem, far_sem,
):
    subs = lax.axis_size("sub")
    my_dom = lax.axis_index("dom")
    my_sub = lax.axis_index("sub")
    chips = lax.axis_size("dom")
    count = rows.shape[0]
    items = early_ref.shape[0]
    parents = parent_ref.shape[0]
    deep = -(-parents // PACK)
    barrier = pltpu.get_barrier_semaphore()
    mesh_ids = pl.DeviceIdType.MESH
    sibling = (my_dom, lax.rem(my_sub + 1, subs))

    def chip_at(step):
        return lax.rem(my_dom + step, chips)

    def greet(step, carry):
        pl.semaphore_signal(
            barrier, inc=1, device_id=(chip_at(step), my_sub), device_id_type=mesh_ids
        )
        return carry

    loads = [
        pltpu.make_async_copy(source, sink, load_sem.at[number])
        for number, (source, sink) in enumerate(
            (
                (positions_hbm, positions_ref),
                (masses_hbm, masses_ref),
                (send_hbm, send_ref),
                (active_hbm, active_ref),
                (local_hbm, local_ref),
                (cell_send_hbm, cell_send_ref),
                (parent_of_hbm, parent_of_ref),
                (parent_centers_hbm, parent_centers_ref),
                (expand_hbm, expand_ref),
                (active_hbm, active_out),
                (local_hbm, local_out),
                (near_hbm, near_out),
                (far_hbm, far_out),
                (old_hbm, old_out),
            )
        )
    ]
    for load in loads:
        load.start()
    pl.semaphore_signal(barrier, inc=1, device_id=sibling, device_id_type=mesh_ids)
    lax.fori_loop(1, chips, greet, 0)
    for load in loads[:3]:
        load.wait()

    for bucket in range(count):
        lanes = pl.ds(bucket * BUCKET, BUCKET)
        tile = jnp.concatenate([positions_ref[:, lanes], masses_ref[:, lanes]], axis=0)
        rows[bucket] = tile
        for axis_at in range(4):
            comp[axis_at, pl.ds(bucket, 1), :] = tile[axis_at : axis_at + 1, :]

    def gather(chip, carry):
        for slot in range(RQ):
            blocks[chip, slot] = rows[jnp.maximum(send_ref[slot, chip], 0)]
        return carry

    lax.fori_loop(0, chips, gather, 0)

    outgoing = ((term_out, term_in), (cell_out, cell_in.at[my_sub]), (blocks, pool_ref.at[my_sub]))

    sizes = (deep, -(-RQC // PACK), RQ)

    def turn(place):
        return lax.rem(place + chips // 2 - 1, chips - 1) + 1

    def part(ref, number):
        return ref.at[pl.ds(0, sizes[number])]

    def copy_to(number, step):
        source, sink = outgoing[number]
        to_dom = chip_at(step)
        return pltpu.make_async_remote_copy(
            src_ref=part(source.at[to_dom], number), dst_ref=part(sink.at[my_dom], number),
            send_sem=send_sem.at[number], recv_sem=recv_sem.at[number, step],
            device_id=(to_dom, my_sub), device_id_type=mesh_ids,
        )

    def send(number, first, last):
        def one(place, carry):
            copy_to(number, turn(place)).start()
            return carry

        lax.fori_loop(first, last, one, 0)

    def keep(number):
        source, sink = outgoing[number]
        pltpu.make_async_copy(
            part(source.at[my_dom], number), part(sink.at[my_dom], number), recv_sem.at[number, 0]
        ).start()

    def arrived(number, step):
        sink = part(outgoing[number][1].at[lax.rem(my_dom + chips - step, chips)], number)
        pltpu.make_async_copy(sink, sink, recv_sem.at[number, step]).wait()

    def forward(number, step):
        piece = part(outgoing[number][1].at[lax.rem(my_dom + chips - step, chips)], number)
        return pltpu.make_async_remote_copy(
            src_ref=piece, dst_ref=piece,
            send_sem=far_sem.at[2 * number], recv_sem=far_sem.at[2 * number + 1],
            device_id=sibling, device_id_type=mesh_ids,
        )

    def relay(number, first, last):
        def one(place, carry):
            step = turn(place)
            arrived(number, step)
            forward(number, step).start()
            return carry

        lax.fori_loop(first, last, one, 0)

    def relay_own(number):
        arrived(number, 0)
        forward(number, 0).start()

    def settle(ref, sem):
        pltpu.make_async_copy(ref, ref, sem).wait()

    pl.semaphore_wait(barrier, chips + subs - 2)
    own_rows = chip_ref.at[pl.ds(my_sub * count, count)]
    twin = pltpu.make_async_remote_copy(
        src_ref=rows, dst_ref=own_rows, send_sem=near_sem.at[0], recv_sem=near_sem.at[1],
        device_id=sibling, device_id_type=mesh_ids,
    )
    twin.start()
    send(2, 0, chips // 2)
    mine = pltpu.make_async_copy(rows, own_rows, near_sem.at[2])
    mine.start()
    keep(2)
    for load in loads[3:]:
        load.wait()

    values = [comp[axis_at] for axis_at in range(4)]
    centers = [jnp.mean(values[axis_at], axis=1, keepdims=True) for axis_at in range(3)]
    cells = packed_columns(moment_columns(values, centers) + centers, count)
    for lap in range(PACK):
        spread[lap] = cells if lap == 0 else pltpu.roll(cells, WIDTH * lap, 1)

    def gather_cells(chip, carry):
        for row in range(cell_out.shape[1]):
            total = None
            for lap in range(PACK):
                slot = PACK * row + lap
                if slot < RQC:
                    piece = spread[lap, pl.ds(jnp.maximum(cell_send_ref[slot, chip], 0), 1), :]
                    total = piece if total is None else total + piece
            if total is None:
                total = jnp.zeros((1, 128), jnp.float32)
            cell_out[chip, pl.ds(row, 1), :] = total
        return carry

    lax.fori_loop(0, chips, gather_cells, 0)

    wide = lax.broadcasted_iota(jnp.int32, (1, one_hot.shape[1]), 1)
    lane = lax.broadcasted_iota(jnp.int32, (1, pick.shape[2]), 1)
    chip_of, deep_of = lane // 8, lane % 8
    for bucket in range(count):
        owner = parent_of_ref[bucket]
        one_hot[pl.ds(bucket, 1), :] = jnp.where(wide == owner, 1.0, 0.0)
        for lap in range(PACK):
            within = deep_of + deep * lap
            named = (deep_of < deep) & (within < parents) & (chip_of * parents + within == owner)
            pick[lap, pl.ds(bucket, 1), :] = jnp.where(named, 1.0, 0.0)
    centers_of = lax.dot_general(
        one_hot[...], parent_centers_ref[...], (((1,), (1,)), ((), ())),
        precision=lax.Precision.HIGHEST, preferred_element_type=jnp.float32,
    )
    terms = packed_columns(
        moment_columns(values, [centers_of[:, axis_at : axis_at + 1] for axis_at in range(3)]), count
    )
    sums = None
    for lap in range(PACK):
        piece = lax.dot_general(
            pick[lap], terms if lap == 0 else pltpu.roll(terms, WIDTH * lap, 1),
            (((0,), (0,)), ((), ())),
            precision=lax.Precision.HIGHEST, preferred_element_type=jnp.float32,
        )
        sums = piece if sums is None else sums + piece
    term_out[...] = sums.reshape(term_out.shape)
    send(1, 0, chips - 1)
    keep(1)
    send(2, chips // 2, chips - 1)
    send(0, 0, chips - 1)
    keep(0)
    relay_own(2)
    twin.wait()
    mine.wait()

    total_rows = subs * count

    def next_place(last):
        found = total_rows
        for place in range(total_rows - 1, -1, -1):
            fits = (active_ref[shared_row(place, total_rows)] > 0) & (place > last)
            found = jnp.where(fits, place, found)
        return found

    def start(item, place):
        row = shared_row(jnp.minimum(place, total_rows - 1), total_rows)
        total = near_sum(
            chip_ref[row], lambda number: chip_ref[local_ref[number, row]], local_ref.shape[0]
        )
        early_ref[item] = jnp.concatenate([total, jnp.zeros((1, BUCKET), jnp.float32)], axis=0)

    share = -(-(chips - 1) // (items // 2 - IDLE))

    def early(pair, last):
        first = next_place(last)
        second = next_place(first)
        start(2 * pair, first)
        start(2 * pair + 1, second)

        @pl.when(pair >= IDLE)
        def _():
            begin = (pair - IDLE) * share
            relay(2, begin, jnp.minimum(begin + share, chips - 1))

        @pl.when(pair == items // 2 - 2)
        def _():
            lax.fori_loop(0, chips, lambda step, carry: (arrived(0, step), carry)[1], 0)
            halves[my_sub] = jnp.sum(term_in[:, 0:deep], axis=0)
            relay_own(1)
            relay(1, 0, chips - 1)

        return second

    lax.fori_loop(0, items // 2, early, -1)
    swap = pltpu.make_async_remote_copy(
        src_ref=halves.at[my_sub], dst_ref=halves.at[my_sub],
        send_sem=far_sem.at[0], recv_sem=far_sem.at[1],
        device_id=sibling, device_id_type=mesh_ids,
    )
    swap.start()
    relayed = cell_in.at[0, :, pl.ds(0, sizes[1])]
    settle(relayed, far_sem.at[2])
    settle(relayed, far_sem.at[3])
    packed = cell_in[...].reshape(-1, 128)
    for lap in range(PACK):
        table_ref[lap] = jnp.dot(
            packed, expand_ref[lap], precision=lax.Precision.HIGHEST, preferred_element_type=jnp.float32
        )
    settle(halves.at[0], far_sem.at[0])
    settle(halves.at[0], far_sem.at[1])
    total = halves[0]
    for sub in range(1, halves.shape[0]):
        total = total + halves[sub]
    for lap in range(PACK):
        size = min(deep, parents - lap * deep)
        turned = total if lap == 0 else pltpu.roll(total, 128 - WIDTH * lap, 1)
        parent_ref[lap * deep : lap * deep + size, :] = turned[:size, : parent_ref.shape[1]]
    settle(pool_ref.at[0], far_sem.at[4])
    settle(pool_ref.at[0], far_sem.at[5])
    for number, (source, sink) in enumerate(outgoing):
        settle(source.at[pl.ds(0, chips - 1), pl.ds(0, sizes[number])], send_sem.at[number])


def exchange(
    positions, masses, send_ids, active, local_list, cell_send_ids, parent_of, parent_centers,
    near_list, far_list, old_accel, moment_count,
):
    subs = lax.axis_size("sub")
    chips = lax.axis_size("dom")
    parent_total = parent_centers.shape[1]
    parents = parent_total // chips
    table = gradient_table()
    expand = np.zeros((PACK, 128, 128))
    for lap in range(PACK):
        expand[lap, WIDTH * lap : WIDTH * lap + 38] = table[:, :38].T
    f32 = jnp.float32
    arrays = (
        positions, masses, send_ids, active, local_list, cell_send_ids, parent_of, parent_centers,
        jnp.asarray(expand, f32),
    )
    handed = (active, local_list, near_list, far_list, old_accel)
    results = [
        pltpu.VMEM(shape, f32)
        for shape in (
            (subs * NB, 4, BUCKET),
            (subs, chips, RQ, 4, BUCKET),
            (PACK, subs * chips * CELL_ROWS, 128),
            (parents, moment_count),
            (ITEMS, 4, BUCKET),
        )
    ] + [pltpu.VMEM(array.shape, array.dtype) for array in handed]
    spaces = (pltpu.VMEM,) * 2 + (pltpu.SMEM,) * 5 + (pltpu.VMEM,) * 2
    return pl.pallas_call(
        exchange_kernel,
        out_shape=results,
        in_specs=[pl.BlockSpec(memory_space=pltpu.HBM)] * (len(arrays) + 3),
        out_specs=[pl.BlockSpec(memory_space=pltpu.VMEM)] * len(results),
        scratch_shapes=[space(array.shape, array.dtype) for space, array in zip(spaces, arrays)]
        + [
            pltpu.VMEM((NB, 4, BUCKET), f32),
            pltpu.VMEM((chips, RQ, 4, BUCKET), f32),
            pltpu.VMEM((4, NB, BUCKET), f32),
            pltpu.VMEM((PACK, NB, 128), f32),
            pltpu.VMEM((NB, parent_total), f32),
            pltpu.VMEM((PACK, NB, chips * 8), f32),
            pltpu.VMEM((chips, CELL_ROWS, 128), f32),
            pltpu.VMEM((chips, 8, 128), f32),
            pltpu.VMEM((chips, 8, 128), f32),
            pltpu.VMEM((subs, chips, CELL_ROWS, 128), f32),
            pltpu.VMEM((subs, -(-parents // PACK), 128), f32),
            pltpu.SemaphoreType.DMA((len(arrays) + len(handed),)),
            pltpu.SemaphoreType.DMA((3,)),
            pltpu.SemaphoreType.DMA((3, chips)),
            pltpu.SemaphoreType.DMA((3,)),
            pltpu.SemaphoreType.DMA((6,)),
        ],
        compiler_params=pltpu.CompilerParams(
            collective_id=0,
            has_side_effects=True,
            vmem_limit_bytes=(60 << 20) - 5 * sum(math.prod(result.shape) for result in results),
        ),
    )(*arrays, *handed[2:])


def local(
    positions,
    masses,
    old_accel,
    active,
    parent_of,
    parent_centers,
    local_list,
    near_list,
    far_list,
    send_ids,
    cell_send_ids,
):
    moment_count = len(exponent_rows())
    chip_rows, pool, table, parents, early, *handed = exchange(
        positions,
        masses[None],
        send_ids[0].T,
        active,
        local_list.T,
        cell_send_ids[0].T,
        parent_of,
        parent_centers,
        near_list.T,
        far_list.T,
        old_accel,
        moment_count,
    )
    result = fields(
        *handed[:4],
        chip_rows,
        pool.reshape(-1, 4, BUCKET),
        table.reshape(-1, 128),
        early,
    )
    accel, parents = merge(handed[0], bring_back(result), result, handed[4], parents)
    return (accel, parents.T)


def solution(mesh):
    return jax.shard_map(
        local,
        mesh=mesh,
        in_specs=(
            P(None, ("dom", "sub")),
            P(("dom", "sub")),
            P(None, ("dom", "sub")),
            P("dom"),
            P(("dom", "sub")),
            P(),
            P("dom", None),
            P("dom", None),
            P("dom", None),
            P(("dom", "sub"), None, None),
            P(("dom", "sub"), None, None),
        ),
        out_specs=(P(None, ("dom", "sub")), P(None, "dom")),
        check_vma=False,
    )
```

```python
import functools
import math

import jax
import jax.numpy as jnp
import numpy as np
from jax import lax
from jax.experimental import pallas as pl
from jax.experimental.pallas import tpu as pltpu
from jax.sharding import PartitionSpec as P

BUCKET = 256
NB = 32
RQ = 4
RQC = 8


soft_sq = 0.0025
far_sq = 0.25


def exponent_rows():
    listing = []
    for degree in range(5):
        for power_x in range(degree, -1, -1):
            for power_y in range(degree - power_x, -1, -1):
                listing.append((power_x, power_y, degree - power_x - power_y))
    return listing


def multinomial(triple):
    return math.factorial(sum(triple)) / (
        math.factorial(triple[0]) * math.factorial(triple[1]) * math.factorial(triple[2])
    )


def weight_layout():
    triples = exponent_rows()
    position = {triple: number for number, triple in enumerate(triples)}
    weight_table = np.zeros((46, 35))
    s_scale = [1.0, 1.0, 1.5, 2.5, 4.375]
    t_scale = [-0.5, -1.5, -3.75]
    mono_index = []
    radial_index = []
    for number, triple in enumerate(triples):
        weight_table[number, number] = multinomial(triple) * s_scale[sum(triple)]
        mono_index.append(number)
        radial_index.append(sum(triple))
    for number in range(10):
        triple = triples[number]
        for axis_at in range(3):
            raised = list(triple)
            raised[axis_at] += 2
            weight_table[35 + number, position[tuple(raised)]] += (
                multinomial(triple) * t_scale[sum(triple)]
            )
        mono_index.append(number)
        radial_index.append(sum(triple) + 1)
    for axis_one in range(3):
        for axis_two in range(3):
            raised = [0, 0, 0]
            raised[axis_one] += 2
            raised[axis_two] += 2
            weight_table[45, position[tuple(raised)]] += 0.375
    mono_index.append(0)
    radial_index.append(2)
    return (weight_table, mono_index, radial_index)


def monomial_list(comp_x, comp_y, comp_z):
    powers = []
    for component in (comp_x, comp_y, comp_z):
        series = [jnp.ones_like(component)]
        for degree in range(4):
            series.append(series[-1] * component)
        powers.append(series)
    return [
        powers[0][power_x] * powers[1][power_y] * powers[2][power_z]
        for power_x, power_y, power_z in exponent_rows()
    ]


def gradient_table():
    weight_table, _, _ = weight_layout()
    triples = exponent_rows()
    position = {triple: number for number, triple in enumerate(triples)}
    table = np.zeros((128, 38))

    def lowered(numbers, first, base, start, count):
        for offset, number in enumerate(numbers):
            triple = triples[first + offset]
            for axis_at in range(3):
                if triple[axis_at] > 0:
                    less = list(triple)
                    less[axis_at] -= 1
                    column = base + axis_at * count + position[tuple(less)] - start
                    table[column, :35] += triple[axis_at] * weight_table[number]

    lowered(range(20, 35), 20, 0, 10, 10)
    lowered(range(10, 20), 10, 30, 4, 6)
    lowered(range(39, 45), 4, 48, 1, 3)
    lowered(range(4, 10), 4, 57, 1, 3)
    lowered(range(36, 39), 1, 66, 0, 1)
    lowered(range(1, 4), 1, 69, 0, 1)
    table[72, :35] = weight_table[0]
    table[73, :35] = weight_table[35]
    table[74, :35] = weight_table[45]
    for axis_at in range(3):
        table[75 + axis_at, 35 + axis_at] = 1.0
    return table


def split_three(value):
    first = value.astype(jnp.bfloat16).astype(jnp.float32)
    rest = value - first
    second = rest.astype(jnp.bfloat16).astype(jnp.float32)
    return first, second, rest - second


def weighted(columns, base, monomials):
    total = columns[base] * monomials[0]
    for number in range(1, len(monomials)):
        total = total + columns[base + number] * monomials[number]
    return total


def far_group(cells, points):
    columns = [cells[:, number : number + 1] for number in range(78)]
    r = [points[axis_at : axis_at + 1, :] - columns[75 + axis_at] for axis_at in range(3)]
    x, y, z = r
    xx, xy, xz, yy, yz, zz = x * x, x * y, x * z, y * y, y * z, z * z
    rho_sq = xx + yy + zz + far_sq
    inv_rho = lax.rsqrt(rho_sq)
    inv_sq = inv_rho * inv_rho
    radial = [inv_rho]
    for degree in range(5):
        radial.append(radial[-1] * inv_sq)
    quad = [xx, xy, xz, yy, yz, zz]
    cubic = [
        xx * x, xx * y, xx * z, x * yy, x * yz, x * zz, yy * y, yy * z, y * zz, zz * z,
    ]

    def dot(grad):
        return x * grad[0] + y * grad[1] + z * grad[2]

    grad_four = [weighted(columns, 10 * axis_at, cubic) for axis_at in range(3)]
    scalar = (2.25 * radial[5]) * dot(grad_four)
    total = [radial[4] * grad for grad in grad_four]
    grad_three = [weighted(columns, 30 + 6 * axis_at, quad) for axis_at in range(3)]
    grad_two_t = [weighted(columns, 48 + 3 * axis_at, r) for axis_at in range(3)]
    value_three = dot(grad_three) * (1.0 / 3.0) + dot(grad_two_t) * 0.5
    scalar = scalar + (7.0 * radial[4]) * value_three
    total = [
        t + radial[3] * (a + b) for t, a, b in zip(total, grad_three, grad_two_t)
    ]
    grad_two = [weighted(columns, 57 + 3 * axis_at, r) for axis_at in range(3)]
    value_two = dot(grad_two) * 0.5 + dot(columns[66:69]) + columns[74]
    scalar = scalar + (5.0 * radial[3]) * value_two
    total = [
        t + radial[2] * (a + b) for t, a, b in zip(total, grad_two, columns[66:69])
    ]
    value_one = dot(columns[69:72]) + columns[73]
    scalar = scalar + (3.0 * radial[2]) * value_one + radial[1] * columns[72]
    return [t + radial[1] * a - c * scalar for t, a, c in zip(total, columns[69:72], r)]


def split_two(value):
    high = value.astype(jnp.bfloat16).astype(jnp.float32)
    return high, value - high


def near_sum(target, source_of, count):
    row_at = lax.broadcasted_iota(jnp.int32, (8, BUCKET), 0)
    twice = jnp.concatenate([target, target], axis=0)
    middle = jnp.where(row_at % 4 == 3, 0.0, jnp.mean(twice, axis=1, keepdims=True))
    at = twice - middle
    norm = jnp.sum(jnp.where(row_at < 3, at * at, 0.0), axis=0, keepdims=True) + soft_sq
    feature = jnp.where(
        row_at < 3, -2.0 * at, jnp.where(row_at == 3, norm, jnp.where(row_at < 7, 1.0, 0.0))
    )
    one, two, three = split_three(feature)
    lhs = jnp.concatenate([one, two, three, one, two, one], axis=0).astype(jnp.bfloat16)
    running = jnp.zeros((8, BUCKET), jnp.float32)
    for number in range(count):
        source = source_of(number)
        offset = jnp.concatenate([source, source], axis=0) - middle
        feature = jnp.where(row_at < 3, offset, jnp.where(row_at == 3, 1.0, offset * offset))
        one, two, three = split_three(feature)
        rhs = jnp.concatenate([one, one, one, two, two, three], axis=0).astype(jnp.bfloat16)
        carried = jnp.where(row_at % 4 == 3, 1.0, offset) * source[3:4, :]
        high, low = split_two(carried)
        values = jnp.where(row_at < 4, high, low).astype(jnp.bfloat16)
        dist_sq = lax.dot_general(
            rhs, lhs, (((0,), (0,)), ((), ())), preferred_element_type=jnp.float32
        )
        inv = lax.rsqrt(dist_sq)
        weight = inv * inv * inv
        coarse = weight.astype(jnp.bfloat16)
        fine = (weight - coarse.astype(jnp.float32)).astype(jnp.bfloat16)
        for part in (coarse, fine):
            running = running + jnp.dot(values, part, preferred_element_type=jnp.float32)
    summed = running[0:4] + running[4:8]
    return summed[0:3] - at[0:3] * summed[3:4]


def far_sum(target, table_ref, index_of, count, cells):
    for number in range(count):
        cells[pl.ds(number, 1), :] = table_ref[pl.ds(index_of(number), 1), :]
    parts = None
    for group in range(count // 8):
        piece = far_group(cells[8 * group : 8 * group + 8, :], target)
        parts = piece if parts is None else [a + b for a, b in zip(parts, piece)]
    return jnp.concatenate([jnp.sum(part, axis=0, keepdims=True) for part in parts], axis=0)


def field_kernel(
    active_ref, local_ref, near_ref, far_ref, chip_ref, pool_ref, table_ref, early_ref,
    result_ref, cells, listed,
):
    my_sub = lax.axis_index("sub")
    subs, chips = lax.axis_size("sub"), lax.axis_size("dom")
    local_count, near_count = local_ref.shape[0], near_ref.shape[0]
    lap_rows = table_ref.shape[0] // PACK
    total_rows = active_ref.shape[0]
    buckets = total_rows // subs
    result_ref[buckets:] = jnp.zeros((result_ref.shape[0] - buckets, 4, BUCKET), jnp.float32)

    def place(entry, slots):
        device = lax.div(entry, slots)
        return lax.rem(device, subs) * chips + lax.div(device, subs), lax.rem(entry, slots)

    def pool_at(entry):
        where, slot = place(entry, RQ)
        return where * RQ + slot

    def table_at(entry):
        where, slot = place(entry, RQC)
        row = lax.div(slot, PACK)
        return (slot - PACK * row) * lap_rows + where * CELL_ROWS + row

    filled = jnp.int32(0)
    owned = jnp.int32(0)
    for step in range(total_rows):
        row = shared_row(step, total_rows)
        listed[filled] = row
        filled = filled + jnp.where(active_ref[row] > 0, 1, 0)
        if step == buckets - 1:
            owned = filled
    mine = lax.div(filled + 1 - my_sub, 2)

    def solve(item, started):
        row = listed[item]
        target = chip_ref[row]

        def source_of(number):
            if number < near_count:
                return pool_ref[pool_at(near_ref[number, row])]
            return chip_ref[local_ref[number - near_count, row]]

        near = near_sum(target, source_of, near_count if started else near_count + local_count)
        if started:
            near = near + early_ref[item][0:3]
        far = far_sum(
            target, table_ref, lambda number: table_at(far_ref[number, row]), far_ref.shape[0], cells
        )
        slot = jnp.where(item < owned, row - my_sub * buckets, buckets + item - owned)
        result_ref[slot, 0:3] = near + far

    def phase(begin, end, started):
        groups = lax.div(end - begin, GROUP)

        def group(number, carry):
            for lane in range(GROUP):
                solve(begin + GROUP * number + lane, started)
            return carry

        lax.fori_loop(0, groups, group, 0)
        done = begin + GROUP * groups
        size = GROUP // 2
        while size:
            fits = end - done >= size

            @pl.when(fits)
            def _():
                for lane in range(size):
                    solve(done + lane, started)

            done = done + jnp.where(fits, size, 0)
            size //= 2

    split = jnp.minimum(mine, early_ref.shape[0])
    phase(jnp.int32(0), split, True)
    phase(split, mine, False)


def fields(active, local_list, near_list, far_list, chip_rows, pool_rows, table, early):
    smem = pl.BlockSpec(memory_space=pltpu.SMEM)
    vmem = pl.BlockSpec(memory_space=pltpu.VMEM)
    f32 = jnp.float32
    return pl.pallas_call(
        field_kernel,
        out_shape=pltpu.VMEM((NB + NB // 4, 4, BUCKET), f32),
        in_specs=[smem] * 4 + [vmem] * 4,
        out_specs=vmem,
        scratch_shapes=[
            pltpu.VMEM((far_list.shape[0], 128), f32),
            pltpu.SMEM((active.shape[0] + 1,), jnp.int32),
        ],
        compiler_params=pltpu.CompilerParams(
            vmem_limit_bytes=VMEM_BYTES
        ),
    )(active, local_list, near_list, far_list, chip_rows, pool_rows, table, early)


def return_kernel(result_ref, home_ref, sems):
    mesh_ids = pl.DeviceIdType.MESH
    sibling = (lax.axis_index("dom"), lax.rem(lax.axis_index("sub") + 1, lax.axis_size("sub")))
    barrier = pltpu.get_barrier_semaphore()
    pl.semaphore_signal(barrier, inc=1, device_id=sibling, device_id_type=mesh_ids)
    pl.semaphore_wait(barrier, 1)
    copy = pltpu.make_async_remote_copy(
        src_ref=result_ref.at[pl.ds(NB, NB // 4)], dst_ref=home_ref, send_sem=sems.at[0], recv_sem=sems.at[1],
        device_id=sibling, device_id_type=mesh_ids,
    )
    copy.start()
    copy.wait()


def bring_back(result):
    vmem = pl.BlockSpec(memory_space=pltpu.VMEM)
    return pl.pallas_call(
        return_kernel,
        out_shape=pltpu.VMEM((NB // 4, 4, BUCKET), jnp.float32),
        in_specs=[vmem],
        out_specs=vmem,
        scratch_shapes=[pltpu.SemaphoreType.DMA((2,))],
        compiler_params=pltpu.CompilerParams(
            collective_id=1, has_side_effects=True, vmem_limit_bytes=VMEM_BYTES
        ),
    )(result)


def merge_kernel(
    active_ref, home_ref, result_ref, old_ref, parent_ref, out_ref, parent_out_ref
):
    my_sub = lax.axis_index("sub")
    buckets = old_ref.shape[1] // BUCKET
    parent_out_ref[...] = parent_ref[...]
    owned = jnp.int32(0)
    others = jnp.int32(0)
    ranks = []
    for bucket in range(buckets):
        mark = jnp.where(active_ref[my_sub * buckets + bucket] > 0, 1, 0)
        ranks.append((owned, mark))
        owned = owned + mark
        others = others + jnp.where(active_ref[(1 - my_sub) * buckets + bucket] > 0, 1, 0)
    helped = lax.div(owned + others + my_sub, 2) - others
    for bucket in range(buckets):
        rank, mark = ranks[bucket]
        slot = jnp.where(my_sub == 0, owned - 1 - rank, rank)
        lanes = pl.ds(bucket * BUCKET, BUCKET)
        got = home_ref[jnp.clip(slot, 0, home_ref.shape[0] - 1)]
        fresh = jnp.where(slot < helped, got[0:3], result_ref[bucket][0:3])
        out_ref[:, lanes] = jnp.where(mark > 0, fresh, old_ref[:, lanes])


def merge(active, home, result, old_accel, parents):
    smem = pl.BlockSpec(memory_space=pltpu.SMEM)
    vmem = pl.BlockSpec(memory_space=pltpu.VMEM)
    return pl.pallas_call(
        merge_kernel,
        out_shape=[jax.ShapeDtypeStruct(array.shape, jnp.float32) for array in (old_accel, parents)],
        in_specs=[smem] + [vmem] * 4,
        out_specs=[vmem] * 2,
        compiler_params=pltpu.CompilerParams(vmem_limit_bytes=VMEM_BYTES),
    )(active, home, result, old_accel, parents)


PACK = 3
GROUP = 4
WIDTH = 40
CELL_ROWS = 4
ITEMS = 12
IDLE = 3
AHEAD = 2
VMEM_BYTES = 24 << 20


def packed_columns(columns, rows):
    lane_at = lax.broadcasted_iota(jnp.int32, (rows, 128), 1)
    result = jnp.zeros((rows, 128), jnp.float32)
    for number, column in enumerate(columns):
        result = jnp.where(lane_at == number, column, result)
    return result


def moment_columns(comp, centers):
    monomials = monomial_list(
        comp[0] - centers[0], comp[1] - centers[1], comp[2] - centers[2]
    )
    return [jnp.sum(comp[3] * monomial, axis=1, keepdims=True) for monomial in monomials]


def shared_row(place, total):
    my_sub = lax.axis_index("sub")
    return place + my_sub * (total - 1 - 2 * place)


def exchange_kernel(
    positions_hbm, masses_hbm, send_hbm, active_hbm, local_hbm, cell_send_hbm, parent_of_hbm,
    parent_centers_hbm, expand_hbm, near_hbm, far_hbm, old_hbm,
    chip_ref, pool_ref, table_ref, parent_ref, early_ref,
    active_out, local_out, near_out, far_out, old_out,
    positions_ref, masses_ref, send_ref, active_ref, local_ref, cell_send_ref, parent_of_ref,
    parent_centers_ref, expand_ref,
    rows, blocks, comp, spread, one_hot, pick, cell_out, term_out, term_in, cell_in, halves,
    load_sem, send_sem, recv_sem, near_sem, far_sem,
):
    subs = lax.axis_size("sub")
    my_dom = lax.axis_index("dom")
    my_sub = lax.axis_index("sub")
    chips = lax.axis_size("dom")
    count = rows.shape[0]
    items = early_ref.shape[0]
    parents = parent_ref.shape[0]
    deep = -(-parents // PACK)
    barrier = pltpu.get_barrier_semaphore()
    mesh_ids = pl.DeviceIdType.MESH
    sibling = (my_dom, lax.rem(my_sub + 1, subs))

    def chip_at(step):
        return lax.rem(my_dom + step, chips)

    def greet(step, carry):
        pl.semaphore_signal(
            barrier, inc=1, device_id=(chip_at(step), my_sub), device_id_type=mesh_ids
        )
        return carry

    loads = [
        pltpu.make_async_copy(source, sink, load_sem.at[number])
        for number, (source, sink) in enumerate(
            (
                (positions_hbm, positions_ref),
                (masses_hbm, masses_ref),
                (send_hbm, send_ref),
                (active_hbm, active_ref),
                (local_hbm, local_ref),
                (cell_send_hbm, cell_send_ref),
                (parent_of_hbm, parent_of_ref),
                (parent_centers_hbm, parent_centers_ref),
                (expand_hbm, expand_ref),
                (active_hbm, active_out),
                (local_hbm, local_out),
                (near_hbm, near_out),
                (far_hbm, far_out),
                (old_hbm, old_out),
            )
        )
    ]
    for load in loads:
        load.start()
    pl.semaphore_signal(barrier, inc=1, device_id=sibling, device_id_type=mesh_ids)
    lax.fori_loop(1, chips, greet, 0)
    for load in loads[:3]:
        load.wait()

    for bucket in range(count):
        lanes = pl.ds(bucket * BUCKET, BUCKET)
        tile = jnp.concatenate([positions_ref[:, lanes], masses_ref[:, lanes]], axis=0)
        rows[bucket] = tile
        for axis_at in range(4):
            comp[axis_at, pl.ds(bucket, 1), :] = tile[axis_at : axis_at + 1, :]

    def gather(chip, carry):
        for slot in range(RQ):
            blocks[chip, slot] = rows[jnp.maximum(send_ref[slot, chip], 0)]
        return carry

    lax.fori_loop(0, chips, gather, 0)

    outgoing = ((term_out, term_in), (cell_out, cell_in.at[my_sub]), (blocks, pool_ref.at[my_sub]))

    sizes = (deep, -(-RQC // PACK), RQ)

    def turn(place):
        return lax.rem(place + chips // 2 - 1, chips - 1) + 1

    def part(ref, number):
        return ref.at[pl.ds(0, sizes[number])]

    def copy_to(number, step):
        source, sink = outgoing[number]
        to_dom = chip_at(step)
        return pltpu.make_async_remote_copy(
            src_ref=part(source.at[to_dom], number), dst_ref=part(sink.at[my_dom], number),
            send_sem=send_sem.at[number], recv_sem=recv_sem.at[number, step],
            device_id=(to_dom, my_sub), device_id_type=mesh_ids,
        )

    def send(number, first, last):
        def one(place, carry):
            copy_to(number, turn(place)).start()
            return carry

        lax.fori_loop(first, last, one, 0)

    def keep(number):
        source, sink = outgoing[number]
        pltpu.make_async_copy(
            part(source.at[my_dom], number), part(sink.at[my_dom], number), recv_sem.at[number, 0]
        ).start()

    def arrived(number, step):
        sink = part(outgoing[number][1].at[lax.rem(my_dom + chips - step, chips)], number)
        pltpu.make_async_copy(sink, sink, recv_sem.at[number, step]).wait()

    def forward(number, step):
        piece = part(outgoing[number][1].at[lax.rem(my_dom + chips - step, chips)], number)
        return pltpu.make_async_remote_copy(
            src_ref=piece, dst_ref=piece,
            send_sem=far_sem.at[2 * number], recv_sem=far_sem.at[2 * number + 1],
            device_id=sibling, device_id_type=mesh_ids,
        )

    def relay(number, first, last):
        def one(place, carry):
            step = turn(place)
            arrived(number, step)
            forward(number, step).start()
            return carry

        lax.fori_loop(first, last, one, 0)

    def relay_own(number):
        arrived(number, 0)
        forward(number, 0).start()

    def settle(ref, sem):
        pltpu.make_async_copy(ref, ref, sem).wait()

    for load in loads[3:]:
        load.wait()
    values = [comp[axis_at] for axis_at in range(4)]
    centers = [jnp.mean(values[axis_at], axis=1, keepdims=True) for axis_at in range(3)]
    cells = packed_columns(moment_columns(values, centers) + centers, count)
    for lap in range(PACK):
        spread[lap] = cells if lap == 0 else pltpu.roll(cells, WIDTH * lap, 1)

    def gather_cells(chip, carry):
        for row in range(cell_out.shape[1]):
            total = None
            for lap in range(PACK):
                slot = PACK * row + lap
                if slot < RQC:
                    piece = spread[lap, pl.ds(jnp.maximum(cell_send_ref[slot, chip], 0), 1), :]
                    total = piece if total is None else total + piece
            if total is None:
                total = jnp.zeros((1, 128), jnp.float32)
            cell_out[chip, pl.ds(row, 1), :] = total
        return carry

    lax.fori_loop(0, chips, gather_cells, 0)

    wide = lax.broadcasted_iota(jnp.int32, (1, one_hot.shape[1]), 1)
    lane = lax.broadcasted_iota(jnp.int32, (1, pick.shape[2]), 1)
    chip_of, deep_of = lane // 8, lane % 8
    for bucket in range(count):
        owner = parent_of_ref[bucket]
        one_hot[pl.ds(bucket, 1), :] = jnp.where(wide == owner, 1.0, 0.0)
        for lap in range(PACK):
            within = deep_of + deep * lap
            named = (deep_of < deep) & (within < parents) & (chip_of * parents + within == owner)
            pick[lap, pl.ds(bucket, 1), :] = jnp.where(named, 1.0, 0.0)
    centers_of = lax.dot_general(
        one_hot[...], parent_centers_ref[...], (((1,), (1,)), ((), ())),
        precision=lax.Precision.HIGHEST, preferred_element_type=jnp.float32,
    )
    terms = packed_columns(
        moment_columns(values, [centers_of[:, axis_at : axis_at + 1] for axis_at in range(3)]), count
    )
    sums = None
    for lap in range(PACK):
        piece = lax.dot_general(
            pick[lap], terms if lap == 0 else pltpu.roll(terms, WIDTH * lap, 1),
            (((0,), (0,)), ((), ())),
            precision=lax.Precision.HIGHEST, preferred_element_type=jnp.float32,
        )
        sums = piece if sums is None else sums + piece
    term_out[...] = sums.reshape(term_out.shape)
    pl.semaphore_wait(barrier, chips + subs - 2)
    own_rows = chip_ref.at[pl.ds(my_sub * count, count)]
    twin = pltpu.make_async_remote_copy(
        src_ref=rows, dst_ref=own_rows, send_sem=near_sem.at[0], recv_sem=near_sem.at[1],
        device_id=sibling, device_id_type=mesh_ids,
    )
    twin.start()
    send(2, 0, chips // 2)
    mine = pltpu.make_async_copy(rows, own_rows, near_sem.at[2])
    mine.start()
    keep(2)
    send(1, 0, chips - 1)
    keep(1)
    send(2, chips // 2, chips - 1)
    send(0, 0, chips - 1)
    keep(0)
    relay_own(2)
    twin.wait()
    mine.wait()

    total_rows = subs * count

    def next_place(last):
        found = total_rows
        for place in range(total_rows - 1, -1, -1):
            fits = (active_ref[shared_row(place, total_rows)] > 0) & (place > last)
            found = jnp.where(fits, place, found)
        return found

    def start(item, place):
        row = shared_row(jnp.minimum(place, total_rows - 1), total_rows)
        total = near_sum(
            chip_ref[row], lambda number: chip_ref[local_ref[number, row]], local_ref.shape[0]
        )
        early_ref[item] = jnp.concatenate([total, jnp.zeros((1, BUCKET), jnp.float32)], axis=0)

    laps = items // AHEAD
    share = -(-(chips - 1) // (laps - IDLE))

    def next_places(last):
        places = []
        for _ in range(AHEAD):
            last = next_place(last)
            places.append(last)
        return tuple(places)

    def early(lap, places):
        for lane, place in enumerate(places):
            start(AHEAD * lap + lane, place)
        following = next_places(places[-1])

        @pl.when(lap >= IDLE)
        def _():
            begin = (lap - IDLE) * share
            relay(2, begin, jnp.minimum(begin + share, chips - 1))

        @pl.when(lap == laps - 2)
        def _():
            lax.fori_loop(0, chips, lambda step, carry: (arrived(0, step), carry)[1], 0)
            halves[my_sub] = jnp.sum(term_in[:, 0:deep], axis=0)
            relay_own(1)
            relay(1, 0, chips - 1)

        return following

    lax.fori_loop(0, laps, early, next_places(-1))
    swap = pltpu.make_async_remote_copy(
        src_ref=halves.at[my_sub], dst_ref=halves.at[my_sub],
        send_sem=far_sem.at[0], recv_sem=far_sem.at[1],
        device_id=sibling, device_id_type=mesh_ids,
    )
    swap.start()
    relayed = cell_in.at[0, :, pl.ds(0, sizes[1])]
    settle(relayed, far_sem.at[2])
    settle(relayed, far_sem.at[3])
    packed = cell_in[...].reshape(-1, 128)
    for lap in range(PACK):
        table_ref[lap] = jnp.dot(
            packed, expand_ref[lap], precision=lax.Precision.HIGHEST, preferred_element_type=jnp.float32
        )
    settle(halves.at[0], far_sem.at[0])
    settle(halves.at[0], far_sem.at[1])
    total = halves[0]
    for sub in range(1, halves.shape[0]):
        total = total + halves[sub]
    for lap in range(PACK):
        size = min(deep, parents - lap * deep)
        turned = total if lap == 0 else pltpu.roll(total, 128 - WIDTH * lap, 1)
        parent_ref[lap * deep : lap * deep + size, :] = turned[:size, : parent_ref.shape[1]]
    settle(pool_ref.at[0], far_sem.at[4])
    settle(pool_ref.at[0], far_sem.at[5])
    for number, (source, sink) in enumerate(outgoing):
        settle(source.at[pl.ds(0, chips - 1), pl.ds(0, sizes[number])], send_sem.at[number])


def exchange(
    positions, masses, send_ids, active, local_list, cell_send_ids, parent_of, parent_centers,
    near_list, far_list, old_accel, moment_count,
):
    subs = lax.axis_size("sub")
    chips = lax.axis_size("dom")
    parent_total = parent_centers.shape[1]
    parents = parent_total // chips
    table = gradient_table()
    expand = np.zeros((PACK, 128, 128))
    for lap in range(PACK):
        expand[lap, WIDTH * lap : WIDTH * lap + 38] = table[:, :38].T
    f32 = jnp.float32
    arrays = (
        positions, masses, send_ids, active, local_list, cell_send_ids, parent_of, parent_centers,
        jnp.asarray(expand, f32),
    )
    handed = (active, local_list, near_list, far_list, old_accel)
    results = [
        pltpu.VMEM(shape, f32)
        for shape in (
            (subs * NB, 4, BUCKET),
            (subs, chips, RQ, 4, BUCKET),
            (PACK, subs * chips * CELL_ROWS, 128),
            (parents, moment_count),
            (ITEMS, 4, BUCKET),
        )
    ] + [pltpu.VMEM(array.shape, array.dtype) for array in handed]
    spaces = (pltpu.VMEM,) * 2 + (pltpu.SMEM,) * 5 + (pltpu.VMEM,) * 2
    return pl.pallas_call(
        exchange_kernel,
        out_shape=results,
        in_specs=[pl.BlockSpec(memory_space=pltpu.HBM)] * (len(arrays) + 3),
        out_specs=[pl.BlockSpec(memory_space=pltpu.VMEM)] * len(results),
        scratch_shapes=[space(array.shape, array.dtype) for space, array in zip(spaces, arrays)]
        + [
            pltpu.VMEM((NB, 4, BUCKET), f32),
            pltpu.VMEM((chips, RQ, 4, BUCKET), f32),
            pltpu.VMEM((4, NB, BUCKET), f32),
            pltpu.VMEM((PACK, NB, 128), f32),
            pltpu.VMEM((NB, parent_total), f32),
            pltpu.VMEM((PACK, NB, chips * 8), f32),
            pltpu.VMEM((chips, CELL_ROWS, 128), f32),
            pltpu.VMEM((chips, 8, 128), f32),
            pltpu.VMEM((chips, 8, 128), f32),
            pltpu.VMEM((subs, chips, CELL_ROWS, 128), f32),
            pltpu.VMEM((subs, -(-parents // PACK), 128), f32),
            pltpu.SemaphoreType.DMA((len(arrays) + len(handed),)),
            pltpu.SemaphoreType.DMA((3,)),
            pltpu.SemaphoreType.DMA((3, chips)),
            pltpu.SemaphoreType.DMA((3,)),
            pltpu.SemaphoreType.DMA((6,)),
        ],
        compiler_params=pltpu.CompilerParams(
            collective_id=0,
            has_side_effects=True,
            vmem_limit_bytes=(60 << 20) - 5 * sum(math.prod(result.shape) for result in results),
        ),
    )(*arrays, *handed[2:])


def local(
    positions,
    masses,
    old_accel,
    active,
    parent_of,
    parent_centers,
    local_list,
    near_list,
    far_list,
    send_ids,
    cell_send_ids,
):
    moment_count = len(exponent_rows())
    chip_rows, pool, table, parents, early, *handed = exchange(
        positions,
        masses[None],
        send_ids[0].T,
        active,
        local_list.T,
        cell_send_ids[0].T,
        parent_of,
        parent_centers,
        near_list.T,
        far_list.T,
        old_accel,
        moment_count,
    )
    result = fields(
        *handed[:4],
        chip_rows,
        pool.reshape(-1, 4, BUCKET),
        table.reshape(-1, 128),
        early,
    )
    accel, parents = merge(handed[0], bring_back(result), result, handed[4], parents)
    return (accel, parents.T)


def solution(mesh):
    return jax.shard_map(
        local,
        mesh=mesh,
        in_specs=(
            P(None, ("dom", "sub")),
            P(("dom", "sub")),
            P(None, ("dom", "sub")),
            P("dom"),
            P(("dom", "sub")),
            P(),
            P("dom", None),
            P("dom", None),
            P("dom", None),
            P(("dom", "sub"), None, None),
            P(("dom", "sub"), None, None),
        ),
        out_specs=(P(None, ("dom", "sub")), P(None, "dom")),
        check_vma=False,
    )
```

```python
import functools
import math

import jax
import jax.numpy as jnp
import numpy as np
from jax import lax
from jax.experimental import pallas as pl
from jax.experimental.pallas import tpu as pltpu
from jax.sharding import PartitionSpec as P

BUCKET = 256
NB = 32
RQ = 4
RQC = 8


soft_sq = 0.0025
far_sq = 0.25


def exponent_rows():
    listing = []
    for degree in range(5):
        for power_x in range(degree, -1, -1):
            for power_y in range(degree - power_x, -1, -1):
                listing.append((power_x, power_y, degree - power_x - power_y))
    return listing


def multinomial(triple):
    return math.factorial(sum(triple)) / (
        math.factorial(triple[0]) * math.factorial(triple[1]) * math.factorial(triple[2])
    )


def weight_layout():
    triples = exponent_rows()
    position = {triple: number for number, triple in enumerate(triples)}
    weight_table = np.zeros((46, 35))
    s_scale = [1.0, 1.0, 1.5, 2.5, 4.375]
    t_scale = [-0.5, -1.5, -3.75]
    mono_index = []
    radial_index = []
    for number, triple in enumerate(triples):
        weight_table[number, number] = multinomial(triple) * s_scale[sum(triple)]
        mono_index.append(number)
        radial_index.append(sum(triple))
    for number in range(10):
        triple = triples[number]
        for axis_at in range(3):
            raised = list(triple)
            raised[axis_at] += 2
            weight_table[35 + number, position[tuple(raised)]] += (
                multinomial(triple) * t_scale[sum(triple)]
            )
        mono_index.append(number)
        radial_index.append(sum(triple) + 1)
    for axis_one in range(3):
        for axis_two in range(3):
            raised = [0, 0, 0]
            raised[axis_one] += 2
            raised[axis_two] += 2
            weight_table[45, position[tuple(raised)]] += 0.375
    mono_index.append(0)
    radial_index.append(2)
    return (weight_table, mono_index, radial_index)


def monomial_list(comp_x, comp_y, comp_z):
    powers = []
    for component in (comp_x, comp_y, comp_z):
        series = [jnp.ones_like(component)]
        for degree in range(4):
            series.append(series[-1] * component)
        powers.append(series)
    return [
        powers[0][power_x] * powers[1][power_y] * powers[2][power_z]
        for power_x, power_y, power_z in exponent_rows()
    ]


def gradient_table():
    weight_table, _, _ = weight_layout()
    triples = exponent_rows()
    position = {triple: number for number, triple in enumerate(triples)}
    table = np.zeros((128, 38))

    def lowered(numbers, first, base, start, count):
        for offset, number in enumerate(numbers):
            triple = triples[first + offset]
            for axis_at in range(3):
                if triple[axis_at] > 0:
                    less = list(triple)
                    less[axis_at] -= 1
                    column = base + axis_at * count + position[tuple(less)] - start
                    table[column, :35] += triple[axis_at] * weight_table[number]

    lowered(range(20, 35), 20, 0, 10, 10)
    lowered(range(10, 20), 10, 30, 4, 6)
    lowered(range(39, 45), 4, 48, 1, 3)
    lowered(range(4, 10), 4, 57, 1, 3)
    lowered(range(36, 39), 1, 66, 0, 1)
    lowered(range(1, 4), 1, 69, 0, 1)
    table[72, :35] = weight_table[0]
    table[73, :35] = weight_table[35]
    table[74, :35] = weight_table[45]
    for axis_at in range(3):
        table[75 + axis_at, 35 + axis_at] = 1.0
    return table


def split_three(value):
    first = value.astype(jnp.bfloat16).astype(jnp.float32)
    rest = value - first
    second = rest.astype(jnp.bfloat16).astype(jnp.float32)
    return first, second, rest - second


def weighted(columns, base, monomials):
    total = columns[base] * monomials[0]
    for number in range(1, len(monomials)):
        total = total + columns[base + number] * monomials[number]
    return total


def far_group(cells, points):
    columns = [cells[:, number : number + 1] for number in range(78)]
    r = [points[axis_at : axis_at + 1, :] - columns[75 + axis_at] for axis_at in range(3)]
    x, y, z = r
    xx, xy, xz, yy, yz, zz = x * x, x * y, x * z, y * y, y * z, z * z
    rho_sq = xx + yy + zz + far_sq
    inv_rho = lax.rsqrt(rho_sq)
    inv_sq = inv_rho * inv_rho
    radial = [inv_rho]
    for degree in range(5):
        radial.append(radial[-1] * inv_sq)
    quad = [xx, xy, xz, yy, yz, zz]
    cubic = [
        xx * x, xx * y, xx * z, x * yy, x * yz, x * zz, yy * y, yy * z, y * zz, zz * z,
    ]

    def dot(grad):
        return x * grad[0] + y * grad[1] + z * grad[2]

    grad_four = [weighted(columns, 10 * axis_at, cubic) for axis_at in range(3)]
    scalar = (2.25 * radial[5]) * dot(grad_four)
    total = [radial[4] * grad for grad in grad_four]
    grad_three = [weighted(columns, 30 + 6 * axis_at, quad) for axis_at in range(3)]
    grad_two_t = [weighted(columns, 48 + 3 * axis_at, r) for axis_at in range(3)]
    value_three = dot(grad_three) * (1.0 / 3.0) + dot(grad_two_t) * 0.5
    scalar = scalar + (7.0 * radial[4]) * value_three
    total = [
        t + radial[3] * (a + b) for t, a, b in zip(total, grad_three, grad_two_t)
    ]
    grad_two = [weighted(columns, 57 + 3 * axis_at, r) for axis_at in range(3)]
    value_two = dot(grad_two) * 0.5 + dot(columns[66:69]) + columns[74]
    scalar = scalar + (5.0 * radial[3]) * value_two
    total = [
        t + radial[2] * (a + b) for t, a, b in zip(total, grad_two, columns[66:69])
    ]
    value_one = dot(columns[69:72]) + columns[73]
    scalar = scalar + (3.0 * radial[2]) * value_one + radial[1] * columns[72]
    return [t + radial[1] * a - c * scalar for t, a, c in zip(total, columns[69:72], r)]


def split_two(value):
    high = value.astype(jnp.bfloat16).astype(jnp.float32)
    return high, value - high


def near_sum(target, source_of, count):
    row_at = lax.broadcasted_iota(jnp.int32, (8, BUCKET), 0)
    twice = jnp.concatenate([target, target], axis=0)
    middle = jnp.where(row_at % 4 == 3, 0.0, jnp.mean(twice, axis=1, keepdims=True))
    at = twice - middle
    norm = jnp.sum(jnp.where(row_at < 3, at * at, 0.0), axis=0, keepdims=True) + soft_sq
    feature = jnp.where(
        row_at < 3, -2.0 * at, jnp.where(row_at == 3, norm, jnp.where(row_at < 7, 1.0, 0.0))
    )
    one, two, three = split_three(feature)
    lhs = jnp.concatenate([one, two, three, one, two, one], axis=0).astype(jnp.bfloat16)
    running = jnp.zeros((8, BUCKET), jnp.float32)
    for number in range(count):
        source = source_of(number)
        offset = jnp.concatenate([source, source], axis=0) - middle
        feature = jnp.where(row_at < 3, offset, jnp.where(row_at == 3, 1.0, offset * offset))
        one, two, three = split_three(feature)
        rhs = jnp.concatenate([one, one, one, two, two, three], axis=0).astype(jnp.bfloat16)
        carried = jnp.where(row_at % 4 == 3, 1.0, offset) * source[3:4, :]
        high, low = split_two(carried)
        values = jnp.where(row_at < 4, high, low).astype(jnp.bfloat16)
        dist_sq = lax.dot_general(
            rhs, lhs, (((0,), (0,)), ((), ())), preferred_element_type=jnp.float32
        )
        inv = lax.rsqrt(dist_sq)
        weight = inv * inv * inv
        coarse = weight.astype(jnp.bfloat16)
        fine = (weight - coarse.astype(jnp.float32)).astype(jnp.bfloat16)
        for part in (coarse, fine):
            running = running + jnp.dot(values, part, preferred_element_type=jnp.float32)
    summed = running[0:4] + running[4:8]
    return summed[0:3] - at[0:3] * summed[3:4]


def far_sum(target, table_ref, index_of, count, cells):
    for number in range(count):
        cells[pl.ds(number, 1), :] = table_ref[pl.ds(index_of(number), 1), :]
    parts = None
    for group in range(count // 8):
        piece = far_group(cells[8 * group : 8 * group + 8, :], target)
        parts = piece if parts is None else [a + b for a, b in zip(parts, piece)]
    return jnp.concatenate([jnp.sum(part, axis=0, keepdims=True) for part in parts], axis=0)


def field_kernel(
    active_ref, local_ref, near_ref, far_ref, chip_ref, pool_ref, table_ref, early_ref,
    result_ref, cells, listed,
):
    my_sub = lax.axis_index("sub")
    subs, chips = lax.axis_size("sub"), lax.axis_size("dom")
    local_count, near_count = local_ref.shape[0], near_ref.shape[0]
    lap_rows = table_ref.shape[0] // PACK
    total_rows = active_ref.shape[0]
    buckets = total_rows // subs
    result_ref[buckets:] = jnp.zeros((result_ref.shape[0] - buckets, 4, BUCKET), jnp.float32)

    def place(entry, slots):
        device = lax.div(entry, slots)
        return lax.rem(device, subs) * chips + lax.div(device, subs), lax.rem(entry, slots)

    def pool_at(entry):
        where, slot = place(entry, RQ)
        return where * RQ + slot

    def table_at(entry):
        where, slot = place(entry, RQC)
        row = lax.div(slot, PACK)
        return (slot - PACK * row) * lap_rows + where * CELL_ROWS + row

    filled = jnp.int32(0)
    owned = jnp.int32(0)
    for step in range(total_rows):
        row = shared_row(step, total_rows)
        listed[filled] = row
        filled = filled + jnp.where(active_ref[row] > 0, 1, 0)
        if step == buckets - 1:
            owned = filled
    mine = lax.div(filled + 1 - my_sub, 2)

    def solve(item, started):
        row = listed[item]
        target = chip_ref[row]

        def source_of(number):
            if number < near_count:
                return pool_ref[pool_at(near_ref[number, row])]
            return chip_ref[local_ref[number - near_count, row]]

        near = near_sum(target, source_of, near_count if started else near_count + local_count)
        if started:
            near = near + early_ref[item][0:3]
        far = far_sum(
            target, table_ref, lambda number: table_at(far_ref[number, row]), far_ref.shape[0], cells
        )
        slot = jnp.where(item < owned, row - my_sub * buckets, buckets + item - owned)
        result_ref[slot, 0:3] = near + far

    def phase(begin, end, started):
        groups = lax.div(end - begin, GROUP)

        def group(number, carry):
            for lane in range(GROUP):
                solve(begin + GROUP * number + lane, started)
            return carry

        lax.fori_loop(0, groups, group, 0)
        done = begin + GROUP * groups
        size = GROUP // 2
        while size:
            fits = end - done >= size

            @pl.when(fits)
            def _():
                for lane in range(size):
                    solve(done + lane, started)

            done = done + jnp.where(fits, size, 0)
            size //= 2

    split = jnp.minimum(mine, early_ref.shape[0])
    phase(jnp.int32(0), split, True)
    phase(split, mine, False)


def fields(active, local_list, near_list, far_list, chip_rows, pool_rows, table, early):
    smem = pl.BlockSpec(memory_space=pltpu.SMEM)
    vmem = pl.BlockSpec(memory_space=pltpu.VMEM)
    f32 = jnp.float32
    return pl.pallas_call(
        field_kernel,
        out_shape=pltpu.VMEM((NB + NB // 4, 4, BUCKET), f32),
        in_specs=[smem] * 4 + [vmem] * 4,
        out_specs=vmem,
        scratch_shapes=[
            pltpu.VMEM((far_list.shape[0], 128), f32),
            pltpu.SMEM((active.shape[0] + 1,), jnp.int32),
        ],
        compiler_params=pltpu.CompilerParams(
            vmem_limit_bytes=VMEM_BYTES
        ),
    )(active, local_list, near_list, far_list, chip_rows, pool_rows, table, early)


def return_kernel(active_ref, result_ref, old_ref, out_ref, home, marks, sems):
    my_sub = lax.axis_index("sub")
    mesh_ids = pl.DeviceIdType.MESH
    sibling = (lax.axis_index("dom"), lax.rem(my_sub + 1, lax.axis_size("sub")))
    barrier = pltpu.get_barrier_semaphore()
    pl.semaphore_signal(barrier, inc=1, device_id=sibling, device_id_type=mesh_ids)
    load = pltpu.make_async_copy(active_ref, marks, sems.at[2])
    load.start()
    pl.semaphore_wait(barrier, 1)
    copy = pltpu.make_async_remote_copy(
        src_ref=result_ref.at[pl.ds(NB, NB // 4)], dst_ref=home,
        send_sem=sems.at[0], recv_sem=sems.at[1],
        device_id=sibling, device_id_type=mesh_ids,
    )
    copy.start()
    load.wait()
    buckets = old_ref.shape[1] // BUCKET
    owned = jnp.int32(0)
    others = jnp.int32(0)
    ranks = []
    for bucket in range(buckets):
        lanes = pl.ds(bucket * BUCKET, BUCKET)
        mark = jnp.where(marks[my_sub * buckets + bucket] > 0, 1, 0)
        out_ref[:, lanes] = jnp.where(mark > 0, result_ref[bucket][0:3], old_ref[:, lanes])
        ranks.append((owned, mark))
        owned = owned + mark
        others = others + jnp.where(marks[(1 - my_sub) * buckets + bucket] > 0, 1, 0)
    helped = lax.div(owned + others + my_sub, 2) - others
    copy.wait()
    for bucket in range(buckets):
        rank, mark = ranks[bucket]
        slot = jnp.where(my_sub == 0, owned - 1 - rank, rank)
        lanes = pl.ds(bucket * BUCKET, BUCKET)
        got = home[jnp.clip(slot, 0, home.shape[0] - 1)]
        out_ref[:, lanes] = jnp.where((mark > 0) & (slot < helped), got[0:3], out_ref[:, lanes])


def bring_back(active, result, old_accel):
    vmem = pl.BlockSpec(memory_space=pltpu.VMEM)
    return pl.pallas_call(
        return_kernel,
        out_shape=pltpu.VMEM(old_accel.shape, jnp.float32),
        in_specs=[vmem] * 3,
        out_specs=vmem,
        scratch_shapes=[
            pltpu.VMEM((NB // 4, 4, BUCKET), jnp.float32),
            pltpu.SMEM(active.shape, jnp.int32),
            pltpu.SemaphoreType.DMA((3,)),
        ],
        compiler_params=pltpu.CompilerParams(
            collective_id=1, has_side_effects=True, vmem_limit_bytes=VMEM_BYTES
        ),
    )(active, result, old_accel)


def deliver_kernel(accel_ref, parent_ref, out_ref, parent_out_ref, sems):
    copies = [
        pltpu.make_async_copy(source, sink, sems.at[number])
        for number, (source, sink) in enumerate(
            ((accel_ref, out_ref), (parent_ref, parent_out_ref))
        )
    ]
    for copy in copies:
        copy.start()
    for copy in copies:
        copy.wait()


def deliver(accel, parents):
    vmem = pl.BlockSpec(memory_space=pltpu.VMEM)
    hbm = pl.BlockSpec(memory_space=pltpu.HBM)
    return pl.pallas_call(
        deliver_kernel,
        out_shape=[jax.ShapeDtypeStruct(array.shape, jnp.float32) for array in (accel, parents)],
        in_specs=[vmem] * 2,
        out_specs=[hbm] * 2,
        scratch_shapes=[pltpu.SemaphoreType.DMA((2,))],
        compiler_params=pltpu.CompilerParams(vmem_limit_bytes=VMEM_BYTES),
    )(accel, parents)


PACK = 3
GROUP = 4
WIDTH = 40
CELL_ROWS = 4
ITEMS = 12
IDLE = 3
AHEAD = 2
VMEM_BYTES = 24 << 20


def packed_columns(columns, rows):
    lane_at = lax.broadcasted_iota(jnp.int32, (rows, 128), 1)
    result = jnp.zeros((rows, 128), jnp.float32)
    for number, column in enumerate(columns):
        result = jnp.where(lane_at == number, column, result)
    return result


def moment_columns(comp, centers):
    monomials = monomial_list(
        comp[0] - centers[0], comp[1] - centers[1], comp[2] - centers[2]
    )
    return [jnp.sum(comp[3] * monomial, axis=1, keepdims=True) for monomial in monomials]


def shared_row(place, total):
    my_sub = lax.axis_index("sub")
    return place + my_sub * (total - 1 - 2 * place)


def exchange_kernel(
    positions_hbm, masses_hbm, send_hbm, active_hbm, local_hbm, cell_send_hbm, parent_of_hbm,
    parent_centers_hbm, expand_hbm, near_hbm, far_hbm, old_hbm,
    chip_ref, pool_ref, table_ref, parent_ref, early_ref,
    active_out, local_out, near_out, far_out, old_out,
    positions_ref, masses_ref, send_ref, active_ref, local_ref, cell_send_ref, parent_of_ref,
    parent_centers_ref, expand_ref,
    rows, blocks, comp, spread, one_hot, pick, cell_out, term_out, term_in, cell_in, halves,
    load_sem, send_sem, recv_sem, near_sem, far_sem,
):
    subs = lax.axis_size("sub")
    my_dom = lax.axis_index("dom")
    my_sub = lax.axis_index("sub")
    chips = lax.axis_size("dom")
    count = rows.shape[0]
    items = early_ref.shape[0]
    parents = parent_ref.shape[0]
    deep = -(-parents // PACK)
    barrier = pltpu.get_barrier_semaphore()
    mesh_ids = pl.DeviceIdType.MESH
    sibling = (my_dom, lax.rem(my_sub + 1, subs))

    def chip_at(step):
        return lax.rem(my_dom + step, chips)

    def greet(step, carry):
        pl.semaphore_signal(
            barrier, inc=1, device_id=(chip_at(step), my_sub), device_id_type=mesh_ids
        )
        return carry

    loads = [
        pltpu.make_async_copy(source, sink, load_sem.at[number])
        for number, (source, sink) in enumerate(
            (
                (positions_hbm, positions_ref),
                (masses_hbm, masses_ref),
                (send_hbm, send_ref),
                (active_hbm, active_ref),
                (local_hbm, local_ref),
                (cell_send_hbm, cell_send_ref),
                (parent_of_hbm, parent_of_ref),
                (parent_centers_hbm, parent_centers_ref),
                (expand_hbm, expand_ref),
                (active_hbm, active_out),
                (local_hbm, local_out),
                (near_hbm, near_out),
                (far_hbm, far_out),
                (old_hbm, old_out),
            )
        )
    ]
    for load in loads:
        load.start()
    pl.semaphore_signal(barrier, inc=1, device_id=sibling, device_id_type=mesh_ids)
    lax.fori_loop(1, chips, greet, 0)
    for load in loads[:3]:
        load.wait()

    for bucket in range(count):
        lanes = pl.ds(bucket * BUCKET, BUCKET)
        tile = jnp.concatenate([positions_ref[:, lanes], masses_ref[:, lanes]], axis=0)
        rows[bucket] = tile
        for axis_at in range(4):
            comp[axis_at, pl.ds(bucket, 1), :] = tile[axis_at : axis_at + 1, :]

    def gather(chip, carry):
        for slot in range(RQ):
            blocks[chip, slot] = rows[jnp.maximum(send_ref[slot, chip], 0)]
        return carry

    lax.fori_loop(0, chips, gather, 0)

    outgoing = ((term_out, term_in), (cell_out, cell_in.at[my_sub]), (blocks, pool_ref.at[my_sub]))

    sizes = (deep, -(-RQC // PACK), RQ)

    def turn(place):
        return lax.rem(place + chips // 2 - 1, chips - 1) + 1

    def part(ref, number):
        return ref.at[pl.ds(0, sizes[number])]

    def copy_to(number, step):
        source, sink = outgoing[number]
        to_dom = chip_at(step)
        return pltpu.make_async_remote_copy(
            src_ref=part(source.at[to_dom], number), dst_ref=part(sink.at[my_dom], number),
            send_sem=send_sem.at[number], recv_sem=recv_sem.at[number, step],
            device_id=(to_dom, my_sub), device_id_type=mesh_ids,
        )

    def send(number, first, last):
        def one(place, carry):
            copy_to(number, turn(place)).start()
            return carry

        lax.fori_loop(first, last, one, 0)

    def keep(number):
        source, sink = outgoing[number]
        pltpu.make_async_copy(
            part(source.at[my_dom], number), part(sink.at[my_dom], number), recv_sem.at[number, 0]
        ).start()

    def arrived(number, step):
        sink = part(outgoing[number][1].at[lax.rem(my_dom + chips - step, chips)], number)
        pltpu.make_async_copy(sink, sink, recv_sem.at[number, step]).wait()

    def forward(number, step):
        piece = part(outgoing[number][1].at[lax.rem(my_dom + chips - step, chips)], number)
        return pltpu.make_async_remote_copy(
            src_ref=piece, dst_ref=piece,
            send_sem=far_sem.at[2 * number], recv_sem=far_sem.at[2 * number + 1],
            device_id=sibling, device_id_type=mesh_ids,
        )

    def relay(number, first, last):
        def one(place, carry):
            step = turn(place)
            arrived(number, step)
            forward(number, step).start()
            return carry

        lax.fori_loop(first, last, one, 0)

    def relay_own(number):
        arrived(number, 0)
        forward(number, 0).start()

    def settle(ref, sem):
        pltpu.make_async_copy(ref, ref, sem).wait()

    for load in loads[3:]:
        load.wait()
    values = [comp[axis_at] for axis_at in range(4)]
    centers = [jnp.mean(values[axis_at], axis=1, keepdims=True) for axis_at in range(3)]
    cells = packed_columns(moment_columns(values, centers) + centers, count)
    for lap in range(PACK):
        spread[lap] = cells if lap == 0 else pltpu.roll(cells, WIDTH * lap, 1)

    def gather_cells(chip, carry):
        for row in range(cell_out.shape[1]):
            total = None
            for lap in range(PACK):
                slot = PACK * row + lap
                if slot < RQC:
                    piece = spread[lap, pl.ds(jnp.maximum(cell_send_ref[slot, chip], 0), 1), :]
                    total = piece if total is None else total + piece
            if total is None:
                total = jnp.zeros((1, 128), jnp.float32)
            cell_out[chip, pl.ds(row, 1), :] = total
        return carry

    lax.fori_loop(0, chips, gather_cells, 0)

    wide = lax.broadcasted_iota(jnp.int32, (1, one_hot.shape[1]), 1)
    lane = lax.broadcasted_iota(jnp.int32, (1, pick.shape[2]), 1)
    chip_of, deep_of = lane // 8, lane % 8
    for bucket in range(count):
        owner = parent_of_ref[bucket]
        one_hot[pl.ds(bucket, 1), :] = jnp.where(wide == owner, 1.0, 0.0)
        for lap in range(PACK):
            within = deep_of + deep * lap
            named = (deep_of < deep) & (within < parents) & (chip_of * parents + within == owner)
            pick[lap, pl.ds(bucket, 1), :] = jnp.where(named, 1.0, 0.0)
    centers_of = lax.dot_general(
        one_hot[...], parent_centers_ref[...], (((1,), (1,)), ((), ())),
        precision=lax.Precision.HIGHEST, preferred_element_type=jnp.float32,
    )
    terms = packed_columns(
        moment_columns(values, [centers_of[:, axis_at : axis_at + 1] for axis_at in range(3)]), count
    )
    sums = None
    for lap in range(PACK):
        piece = lax.dot_general(
            pick[lap], terms if lap == 0 else pltpu.roll(terms, WIDTH * lap, 1),
            (((0,), (0,)), ((), ())),
            precision=lax.Precision.HIGHEST, preferred_element_type=jnp.float32,
        )
        sums = piece if sums is None else sums + piece
    term_out[...] = sums.reshape(term_out.shape)
    pl.semaphore_wait(barrier, chips + subs - 2)
    own_rows = chip_ref.at[pl.ds(my_sub * count, count)]
    twin = pltpu.make_async_remote_copy(
        src_ref=rows, dst_ref=own_rows, send_sem=near_sem.at[0], recv_sem=near_sem.at[1],
        device_id=sibling, device_id_type=mesh_ids,
    )
    twin.start()
    send(2, 0, chips // 2)
    mine = pltpu.make_async_copy(rows, own_rows, near_sem.at[2])
    mine.start()
    keep(2)
    send(1, 0, chips - 1)
    keep(1)
    send(2, chips // 2, chips - 1)
    send(0, 0, chips - 1)
    keep(0)
    relay_own(2)
    twin.wait()
    mine.wait()

    total_rows = subs * count

    def next_place(last):
        found = total_rows
        for place in range(total_rows - 1, -1, -1):
            fits = (active_ref[shared_row(place, total_rows)] > 0) & (place > last)
            found = jnp.where(fits, place, found)
        return found

    def start(item, place):
        row = shared_row(jnp.minimum(place, total_rows - 1), total_rows)
        total = near_sum(
            chip_ref[row], lambda number: chip_ref[local_ref[number, row]], local_ref.shape[0]
        )
        early_ref[item] = jnp.concatenate([total, jnp.zeros((1, BUCKET), jnp.float32)], axis=0)

    laps = items // AHEAD
    share = -(-(chips - 1) // (laps - IDLE))

    def next_places(last):
        places = []
        for _ in range(AHEAD):
            last = next_place(last)
            places.append(last)
        return tuple(places)

    def early(lap, places):
        for lane, place in enumerate(places):
            start(AHEAD * lap + lane, place)
        following = next_places(places[-1])

        @pl.when(lap >= IDLE)
        def _():
            begin = (lap - IDLE) * share
            relay(2, begin, jnp.minimum(begin + share, chips - 1))

        @pl.when(lap == laps - 2)
        def _():
            lax.fori_loop(0, chips, lambda step, carry: (arrived(0, step), carry)[1], 0)
            halves[my_sub] = jnp.sum(term_in[:, 0:deep], axis=0)
            relay_own(1)
            relay(1, 0, chips - 1)

        return following

    lax.fori_loop(0, laps, early, next_places(-1))
    swap = pltpu.make_async_remote_copy(
        src_ref=halves.at[my_sub], dst_ref=halves.at[my_sub],
        send_sem=far_sem.at[0], recv_sem=far_sem.at[1],
        device_id=sibling, device_id_type=mesh_ids,
    )
    swap.start()
    relayed = cell_in.at[0, :, pl.ds(0, sizes[1])]
    settle(relayed, far_sem.at[2])
    settle(relayed, far_sem.at[3])
    packed = cell_in[...].reshape(-1, 128)
    for lap in range(PACK):
        table_ref[lap] = jnp.dot(
            packed, expand_ref[lap], precision=lax.Precision.HIGHEST, preferred_element_type=jnp.float32
        )
    settle(halves.at[0], far_sem.at[0])
    settle(halves.at[0], far_sem.at[1])
    total = halves[0]
    for sub in range(1, halves.shape[0]):
        total = total + halves[sub]
    for lap in range(PACK):
        size = min(deep, parents - lap * deep)
        turned = total if lap == 0 else pltpu.roll(total, 128 - WIDTH * lap, 1)
        parent_ref[lap * deep : lap * deep + size, :] = turned[:size, : parent_ref.shape[1]]
    settle(pool_ref.at[0], far_sem.at[4])
    settle(pool_ref.at[0], far_sem.at[5])
    for number, (source, sink) in enumerate(outgoing):
        settle(source.at[pl.ds(0, chips - 1), pl.ds(0, sizes[number])], send_sem.at[number])


def exchange(
    positions, masses, send_ids, active, local_list, cell_send_ids, parent_of, parent_centers,
    near_list, far_list, old_accel, moment_count,
):
    subs = lax.axis_size("sub")
    chips = lax.axis_size("dom")
    parent_total = parent_centers.shape[1]
    parents = parent_total // chips
    table = gradient_table()
    expand = np.zeros((PACK, 128, 128))
    for lap in range(PACK):
        expand[lap, WIDTH * lap : WIDTH * lap + 38] = table[:, :38].T
    f32 = jnp.float32
    arrays = (
        positions, masses, send_ids, active, local_list, cell_send_ids, parent_of, parent_centers,
        jnp.asarray(expand, f32),
    )
    handed = (active, local_list, near_list, far_list, old_accel)
    results = [
        pltpu.VMEM(shape, f32)
        for shape in (
            (subs * NB, 4, BUCKET),
            (subs, chips, RQ, 4, BUCKET),
            (PACK, subs * chips * CELL_ROWS, 128),
            (parents, moment_count),
            (ITEMS, 4, BUCKET),
        )
    ] + [pltpu.VMEM(array.shape, array.dtype) for array in handed]
    spaces = (pltpu.VMEM,) * 2 + (pltpu.SMEM,) * 5 + (pltpu.VMEM,) * 2
    return pl.pallas_call(
        exchange_kernel,
        out_shape=results,
        in_specs=[pl.BlockSpec(memory_space=pltpu.HBM)] * (len(arrays) + 3),
        out_specs=[pl.BlockSpec(memory_space=pltpu.VMEM)] * len(results),
        scratch_shapes=[space(array.shape, array.dtype) for space, array in zip(spaces, arrays)]
        + [
            pltpu.VMEM((NB, 4, BUCKET), f32),
            pltpu.VMEM((chips, RQ, 4, BUCKET), f32),
            pltpu.VMEM((4, NB, BUCKET), f32),
            pltpu.VMEM((PACK, NB, 128), f32),
            pltpu.VMEM((NB, parent_total), f32),
            pltpu.VMEM((PACK, NB, chips * 8), f32),
            pltpu.VMEM((chips, CELL_ROWS, 128), f32),
            pltpu.VMEM((chips, 8, 128), f32),
            pltpu.VMEM((chips, 8, 128), f32),
            pltpu.VMEM((subs, chips, CELL_ROWS, 128), f32),
            pltpu.VMEM((subs, -(-parents // PACK), 128), f32),
            pltpu.SemaphoreType.DMA((len(arrays) + len(handed),)),
            pltpu.SemaphoreType.DMA((3,)),
            pltpu.SemaphoreType.DMA((3, chips)),
            pltpu.SemaphoreType.DMA((3,)),
            pltpu.SemaphoreType.DMA((6,)),
        ],
        compiler_params=pltpu.CompilerParams(
            collective_id=0,
            has_side_effects=True,
            vmem_limit_bytes=(60 << 20) - 5 * sum(math.prod(result.shape) for result in results),
        ),
    )(*arrays, *handed[2:])


def local(
    positions,
    masses,
    old_accel,
    active,
    parent_of,
    parent_centers,
    local_list,
    near_list,
    far_list,
    send_ids,
    cell_send_ids,
):
    moment_count = len(exponent_rows())
    chip_rows, pool, table, parents, early, *handed = exchange(
        positions,
        masses[None],
        send_ids[0].T,
        active,
        local_list.T,
        cell_send_ids[0].T,
        parent_of,
        parent_centers,
        near_list.T,
        far_list.T,
        old_accel,
        moment_count,
    )
    result = fields(
        *handed[:4],
        chip_rows,
        pool.reshape(-1, 4, BUCKET),
        table.reshape(-1, 128),
        early,
    )
    accel, parents = deliver(bring_back(handed[0], result, handed[4]), parents)
    return (accel, parents.T)


def solution(mesh):
    return jax.shard_map(
        local,
        mesh=mesh,
        in_specs=(
            P(None, ("dom", "sub")),
            P(("dom", "sub")),
            P(None, ("dom", "sub")),
            P("dom"),
            P(("dom", "sub")),
            P(),
            P("dom", None),
            P("dom", None),
            P("dom", None),
            P(("dom", "sub"), None, None),
            P(("dom", "sub"), None, None),
        ),
        out_specs=(P(None, ("dom", "sub")), P(None, "dom")),
        check_vma=False,
    )
```
